32 devices in a mesh: event: 8 (over z, core), mesh: 4 (over y, x).
Axes of the slice: x: 2, y: 2, z: 4, core: 2. Of those that a mesh axis runs over, the one named last changes fastest.
Arguments:
- forward_start: float32 [8, 3, 125, 512], P('event', None, None, 'mesh'), may hold values from -6 to 6
- adjoint_start: float32 [8, 3, 125, 512], P('event', None, None, 'mesh'), may hold values from -6 to 6
- stiffness: float32 [125, 125], replicated
- projection: float32 [125, 64], replicated, may hold values from -0.5 to 0.5
- material: float32 [8, 512], P('event', 'mesh'), may hold values from 0.5 to 2
- neighbours: int32 [8, 6, 512], P('event', None, 'mesh'), may hold values from 0 to 511, as said below
- destinations: int32 [8, 512], P('event', 'mesh'), may hold values from 0 to 127
- counts: int32 [8, 4], P('event', 'mesh'), may hold values from 32 to 128, as said below
- smoothing: float32 [4, 128], P(None, ('event', 'mesh')), may hold values from 0.02 to 0.12
Outputs:
- forward_final: float32 [8, 3, 125, 512], P('event', None, None, 'mesh')
- tiles: float32 [64, 128], P(None, ('event', 'mesh'))
The draws below stay inside these ranges and needn't reach their ends.
Inputs may be any that keep to these rules, and one draw needn't show every extreme that they name: `counts`: in every event one partition holds exactly 128 live elements and another exactly 32; live elements fill a partition's first slots. `neighbours`: A neighbour slot lies in the element's own partition, or in the previous or next partition of the same event (wrapping around), and then among that partition's first 32 slots.
All inputs are finite; a program needn't handle non-finite values.
Results may differ from the reference program's by a relative error of at most 0.0003.
Values sent between devices are 32-bit elements; how exact they have to be, the bound alone decides.
A program may use at most 64 MiB of HBM per device.

```python
import math
import jax
import jax.numpy as jnp
from jax import lax

NODES = 125
KNODES = 64
COMP = 3
ECAP = 128
TILE_DEV = 4
STEPS = 2
BND = 32
EVENTS = 8
PARTITIONS = 4
ELEM = 512
NTILE = 128


def draw_stiffness(key, part):
    sample_key = jax.random.fold_in(key, 37)
    factor = jax.random.normal(sample_key, (NODES, NODES), jnp.float32)
    gram_matrix = jnp.dot(factor, factor.T, precision=lax.Precision.HIGHEST) / NODES
    return 0.25 * gram_matrix + 0.1 * jnp.eye(NODES, dtype=jnp.float32)


def draw_counts(key, part):
    first_key, second_key = jax.random.split(jax.random.fold_in(key, 11))
    drawn = jax.random.randint(first_key, (EVENTS, PARTITIONS), ECAP // 4, ECAP + 1)
    fullest = jax.random.randint(second_key, (EVENTS, 1), 0, PARTITIONS)
    columns = jnp.arange(PARTITIONS)[None, :]
    drawn = jnp.where(columns == fullest, ECAP, drawn)
    drawn = jnp.where(columns == (fullest + 1) % PARTITIONS, ECAP // 4, drawn)
    return drawn.astype(jnp.int32)


def draw_neighbours(key, part):
    side_key, near_key, far_key = jax.random.split(jax.random.fold_in(key, 23), 3)
    grid_shape = (EVENTS, 6, ELEM)
    which_side = jax.random.randint(side_key, grid_shape, 0, 4)
    near_slot = jax.random.randint(near_key, grid_shape, 0, ECAP)
    far_slot = jax.random.randint(far_key, grid_shape, 0, BND)
    partition = jnp.arange(ELEM)[None, None, :] // ECAP
    offset = jnp.where(which_side == 2, -1, jnp.where(which_side == 3, 1, 0))
    target = (partition + offset + PARTITIONS) % PARTITIONS
    local_slot = jnp.where(which_side >= 2, far_slot, near_slot)
    result = target * ECAP + local_slot
    result = result.at[:, 0, ELEM - 1].set(ELEM - 1)
    result = result.at[:, 1, 1].set(0)
    return result.astype(jnp.int32)


def with_ends(values, key, least, high):
    shape = values.shape
    place = [jax.random.randint(jax.random.fold_in(key, axis), (), 0, shape[axis]) for axis in range(len(shape))]
    values = values.at[tuple(place)].set(least)
    longest = shape.index(max(shape))
    place[longest] = (place[longest] + 1) % shape[longest]
    return values.at[tuple(place)].set(high)


def block_levels(own_key, dims, pieces, least, high):
    level, own = 1.0, jax.random.fold_in(own_key, 6)
    for axis_at, shards_of in pieces:
        steps = jnp.exp(jax.random.uniform(jax.random.fold_in(own, axis_at), (shards_of,), jnp.float32, least / len(pieces), high / len(pieces)))
        level = level * jnp.repeat(steps, dims[axis_at] // shards_of).reshape([-1 if axis == axis_at else 1 for axis in range(len(dims))])
    return level


def normal_values(stream_key, dims, spread, reach, pieces=(), held_as=jnp.bfloat16):
    level = block_levels(stream_key, dims, pieces, -0.22, 0.18) if pieces else 1.0
    values = jax.random.normal(stream_key, dims, jnp.float32) * spread * level
    return jnp.minimum(jnp.maximum(values, -reach), reach).astype(held_as)


def setup_inputs(seed: int = 0) -> dict:
    key_of = jax.random.split(jax.random.key(seed), 10)
    return {
        "forward_start": normal_values(key_of[0], (EVENTS, COMP, NODES, ELEM), 1.0, 6.0, ((0, 8), (3, 4)), jnp.float32),
        "adjoint_start": normal_values(key_of[1], (EVENTS, COMP, NODES, ELEM), 1.0, 6.0, ((0, 8), (3, 4)), jnp.float32),
        "stiffness": draw_stiffness(jax.random.fold_in(key_of[9], 71), 0),
        "projection": normal_values(key_of[3], (NODES, KNODES), NODES ** -0.5, 0.5, (), jnp.float32),
        "material": jnp.clip(jnp.exp(math.log(2.0) - 1.3862944 * jax.random.uniform(key_of[4], (EVENTS, ELEM), jnp.float32) ** block_levels(key_of[4], (EVENTS, ELEM), ((0, 8), (1, 4)), -0.2, 0.2)), 0.5, 2.0),
        "neighbours": draw_neighbours(jax.random.fold_in(key_of[9], 71), 0),
        "destinations": with_ends(jax.random.randint(key_of[6], (EVENTS, ELEM), 0, NTILE), jax.random.fold_in(key_of[6], 1), 0, NTILE - 1).astype(jnp.int32),
        "counts": draw_counts(jax.random.fold_in(key_of[9], 71), 0),
        "smoothing": jnp.clip(jnp.exp(math.log(0.12) - 1.7917595 * jax.random.uniform(key_of[8], (4, NTILE), jnp.float32) ** block_levels(key_of[8], (4, NTILE), ((1, 32),), -0.2, 0.2)), 0.02, 0.12),
    }


time_square = 0.4
penalty = 0.5
partner_face = (1, 0, 3, 2, 5, 4)

def element_faces(field):
    elements = field.shape[-1]
    cube = field.reshape(3, 5, 5, 5, elements)
    sheets = [cube[:, 0], cube[:, 4], cube[:, :, 0], cube[:, :, 4], cube[:, :, :, 0], cube[:, :, :, 4]]
    return jnp.stack(sheets).reshape(6, 3, 25, elements)

def lift_faces(jumps):
    elements = jumps.shape[-1]
    sheets = jumps.reshape(6, 3, 5, 5, elements)
    keep = (0, 0)
    lifted = jnp.pad(sheets[0][:, None], (keep, (0, 4), keep, keep, keep))
    lifted = lifted + jnp.pad(sheets[1][:, None], (keep, (4, 0), keep, keep, keep))
    lifted = lifted + jnp.pad(sheets[2][:, :, None], (keep, keep, (0, 4), keep, keep))
    lifted = lifted + jnp.pad(sheets[3][:, :, None], (keep, keep, (4, 0), keep, keep))
    lifted = lifted + jnp.pad(sheets[4][:, :, :, None], (keep, keep, keep, (0, 4), keep))
    lifted = lifted + jnp.pad(sheets[5][:, :, :, None], (keep, keep, keep, (4, 0), keep))
    return lifted.reshape(3, 125, elements)

def apply_stiffness(stiffness, field):
    return jnp.einsum('nm,cme->cne', stiffness, field, precision=lax.Precision.HIGHEST)

def pick_faces(faces, neighbour_rows):
    return jnp.stack([jnp.take(faces[partner_face[face]], neighbour_rows[face], axis=2) for face in range(6)])

def advance(field, previous, strain, across, own_faces, material_row, live):
    force = -material_row[None, None, :] * strain + penalty * lift_faces(across - own_faces)
    return live[None, None, :] * (2.0 * field - previous + time_square * force)

def node_laplace(values, coefs):
    width = values.shape[-1]
    cube = values.reshape(4, 4, 4, width)
    padded = jnp.pad(cube, ((1, 1), (1, 1), (1, 1), (0, 0)))
    first_dir = padded[2:, 1:-1, 1:-1] + padded[:-2, 1:-1, 1:-1] - 2.0 * cube
    second_dir = padded[1:-1, 2:, 1:-1] + padded[1:-1, :-2, 1:-1] - 2.0 * cube
    third_dir = padded[1:-1, 1:-1, 2:] + padded[1:-1, 1:-1, :-2] - 2.0 * cube
    summed = coefs[0] * first_dir + coefs[1] * second_dir + coefs[2] * third_dir
    return summed.reshape(64, width)

def smooth_columns(values, coefs):
    middle = values[:, 1:-1]
    chain = values[:, :-2] + values[:, 2:] - 2.0 * middle
    return middle + coefs[0] * chain + node_laplace(middle, coefs[1:])

def reference(forward_start, adjoint_start, stiffness, projection, material, neighbours, destinations, counts, smoothing):
    scale = math.sqrt(TILE_DEV / ECAP) / STEPS

    def one_event(summed, inputs):
        forward_row, adjoint_row, material_row, neighbour_rows, destination_row, count_row = inputs
        slots = jnp.arange(ECAP, dtype=jnp.int32)
        live = (slots[None, :] < count_row[:, None]).reshape(ELEM).astype(jnp.float32)
        forward = forward_row * live[None, None, :]
        adjoint = adjoint_row * live[None, None, :]
        forward_prev, adjoint_prev = (forward, adjoint)
        kernel = jnp.zeros((NODES, ELEM), jnp.float32)
        for step_index in range(STEPS):
            strain_forward = apply_stiffness(stiffness, forward)
            strain_adjoint = apply_stiffness(stiffness, adjoint)
            kernel = kernel + lax.optimization_barrier(jnp.sum(forward * strain_adjoint, axis=0))
            faces_forward = element_faces(forward)
            faces_adjoint = element_faces(adjoint)
            across_forward = pick_faces(faces_forward, neighbour_rows)
            across_adjoint = pick_faces(faces_adjoint, neighbour_rows)
            next_forward = advance(forward, forward_prev, strain_forward, across_forward, faces_forward, material_row, live)
            next_adjoint = advance(adjoint, adjoint_prev, strain_adjoint, across_adjoint, faces_adjoint, material_row, live)
            forward_prev, forward = (forward, next_forward)
            adjoint_prev, adjoint = (adjoint, next_adjoint)
        blocks = jnp.dot(projection.T, kernel, precision=lax.Precision.HIGHEST) * scale
        summed = summed.at[:, destination_row].add(blocks)
        return (summed, forward)
    summed, finals = lax.scan(one_event, jnp.zeros((KNODES, NTILE), jnp.float32), (forward_start, adjoint_start, material, neighbours, destinations, counts))
    tiles = summed
    for pass_index in range(2):
        padded = jnp.pad(tiles, ((0, 0), (1, 1)))
        tiles = smooth_columns(padded, smoothing)
    return (finals, tiles)
```

```python
import functools
import math

import jax
import jax.numpy as jnp
from jax import lax
from jax.experimental import pallas as pl
from jax.experimental.pallas import tpu as pltpu
from jax.sharding import PartitionSpec as P

STEPS = 2
time_square = 0.4
penalty = 0.5

PAD = 8
ROWS = 128
NODES = 125
SHIFT = (100, -100, 20, -20, 4, -4)
STRAIGHT_FROM = {1: 2, 0: 1, 2: 2}
MESH = pl.DeviceIdType.MESH
f32 = jnp.float32
bf16 = jnp.bfloat16


def on_face(face, node):
    i, j, k = node // 25, (node // 5) % 5, node % 5
    return (i == 0, i == 4, j == 0, j == 4, k == 0, k == 4)[face]


TILE_FACES = [
    [f for f in range(6) if any(on_face(f, n) for n in range(8 * t, min(8 * t + 8, NODES)))]
    for t in range(ROWS // 8)
]


def split(x):
    high = x.astype(bf16)
    return high, (x - high.astype(f32)).astype(bf16)


def mm(a, b, dims=((1,), (0,))):
    return lax.dot_general(a, b, (dims, ((), ())), preferred_element_type=f32)


def pick(x, index):
    return jnp.take_along_axis(x, index, axis=1, mode="promise_in_bounds")


def is_direct(m_size, e_size):
    return m_size * e_size <= 64


def round_count(m_size, e_size):
    return max(e_size // 2 - 1, 1) if is_direct(m_size, e_size) else max(e_size // 2 - 2, 0)


def kernel(
    m_size, e_size,
    fwd_in, adj_in, stiff_hbm, proj_hbm, mat_hbm, nb_hbm, dest_hbm, count_hbm, smooth_hbm,
    fwd_out, tiles_out,
    stiff_in, proj_in, mat_in, nb_in, dest_in, count_in, smooth_in,
    F, N, K, A, S, W, IDX, RIM, LIVE, send, rim, coef, coef_in, msg, mine, part, got, got2,
    in_s, small_s, rim_s, rim_r, coef_s, coef_r, a_s, a_r, b_s, b_r, rounds,
):
    me = lax.axis_index("mesh")
    ev = lax.axis_index("event")
    total = m_size * e_size
    direct = is_direct(m_size, e_size)
    lin = ev * m_size + me
    after = lax.rem(me + 1, m_size)
    before = lax.rem(me + m_size - 1, m_size)

    barrier = pltpu.get_barrier_semaphore()
    core = lax.rem(ev, 2)
    chip = lax.div(ev, 2)
    chips = e_size // 2
    near = [((2 * chip + 1 - core, me), None)]
    for step in (1, -1):
        inside = (chip + step >= 0) & (chip + step < chips)
        near += [((2 * (chip + step) + c, me), inside) for c in range(2)]
    near_count = 1 + 2 * ((chip > 0).astype(jnp.int32) + (chip < chips - 1).astype(jnp.int32))

    def greet(sem):
        for device, inside in near:
            if inside is None:
                pl.semaphore_signal(sem, inc=1, device_id=device, device_id_type=MESH)
            else:

                @pl.when(inside)
                def _():
                    pl.semaphore_signal(sem, inc=1, device_id=device, device_id_type=MESH)

    for o in range(1, m_size):
        pl.semaphore_signal(
            barrier, inc=1, device_id=(ev, lax.rem(me + o, m_size)), device_id_type=MESH
        )
    greet(barrier)

    loads = {}
    for fc in (3, 4, 5, 0, 1, 2):
        source = fwd_in if fc < 3 else adj_in
        load = pltpu.make_async_copy(
            source.at[pl.ds(NODES * (fc % 3), NODES), 0], F.at[fc, pl.ds(PAD, NODES)], in_s.at[fc]
        )
        load.start()
        loads[fc] = load

    small = []
    for n, (src, dst) in enumerate((
        (smooth_hbm, smooth_in), (stiff_hbm, stiff_in), (nb_hbm, nb_in), (count_hbm, count_in),
        (mat_hbm, mat_in), (proj_hbm, proj_in), (dest_hbm, dest_in),
    )):
        load = pltpu.make_async_copy(src, dst, small_s.at[n])
        load.start()
        small.append(load)

    lane = lax.broadcasted_iota(jnp.int32, (1, 128), 1)
    zero8 = jnp.zeros((PAD, 128), f32)
    for fc in range(6):
        F[fc, 0:PAD, :] = zero8
        F[fc, PAD + NODES : 144, :] = jnp.zeros((144 - PAD - NODES, 128), f32)

    def pack(fc):
        wide = [F[fc, PAD + 32 * g : PAD + 32 * g + 32, :] for g in range(4)]
        turned = [wide[0]] + [pltpu.roll(wide[g], 32 * g, 1) for g in range(1, 4)]
        return jnp.where(
            lane < 64, jnp.where(lane < 32, turned[0], turned[1]),
            jnp.where(lane < 96, turned[2], turned[3]),
        )

    def load_field(f):
        for c in range(3):
            loads[3 * f + c].wait()
            send[f, c] = pack(3 * f + c)

    load_field(1)

    pl.semaphore_wait(barrier, near_count + (m_size - 1))

    def remote(src, dst, s, r, device):
        copy = pltpu.make_async_remote_copy(
            src_ref=src, dst_ref=dst, send_sem=s, recv_sem=r, device_id=device, device_id_type=MESH
        )
        copy.start()
        return copy

    paired = m_size == 4
    first = 1 - lax.rem(me, 2) if paired else 0
    second = 1 - first
    sides = (first, second)
    low32 = pl.ds(0, 32)

    def rim_copy(f, k, c):
        slot = sides[1 - k] if paired else sides[k]
        return pltpu.make_async_remote_copy(
            src_ref=send.at[f, c], dst_ref=rim.at[f, slot, c, low32],
            send_sem=rim_s.at[f, k, c], recv_sem=rim_r.at[f, k, c],
            device_id=(ev, jnp.where(slot == 0, after, before)), device_id_type=MESH,
        )

    def relay_copy(f, c):
        return pltpu.make_async_remote_copy(
            src_ref=rim.at[f, first, c, low32], dst_ref=rim.at[f, second, c, low32],
            send_sem=rim_s.at[f, 1, c], recv_sem=rim_r.at[f, 1, c],
            device_id=(ev, lax.rem(me + 2, m_size)), device_id_type=MESH,
        )

    def straight(f):
        return STRAIGHT_FROM[f] if paired else 0

    def send_near(f):
        for c in range(3):
            rim_copy(f, 0, c).start()

    def send_far(f):
        for c in range(straight(f), 3):
            rim_copy(f, 1, c).start()

    send_near(1)
    load_field(0)
    coef[...] = jnp.zeros((8, 128), f32)
    small[0].wait()
    coef[0:4, 0:4] = smooth_in[...]
    send_far(1)
    coef_copies = [
        remote(coef, coef_in.at[0], coef_s.at[0], coef_r.at[0], (ev, after)),
        remote(coef, coef_in.at[1], coef_s.at[1], coef_r.at[1], (ev, before)),
    ]
    n_rounds = round_count(m_size, e_size)
    if n_rounds:
        greet(rounds.at[0])

    def next_round(n):
        if n < n_rounds:
            pl.semaphore_wait(rounds.at[n], near_count)
            if n + 1 < n_rounds:
                greet(rounds.at[n + 1])

    for load in small[1:]:
        load.wait()
    live = jnp.where(lane < count_in[0:1, 0:1], 1.0, 0.0).astype(f32)
    LIVE[...] = jnp.broadcast_to(live, (8, 128))
    for fc in range(6):
        F[fc, PAD : PAD + NODES, :] = F[fc, PAD : PAD + NODES, :] * live

    node = lax.broadcasted_iota(jnp.int32, (ROWS, 128), 0).astype(f32)
    i = jnp.floor((node + 0.5) / 25.0)
    rest = node - 25.0 * i
    j = jnp.floor((rest + 0.5) / 5.0)
    k = rest - 5.0 * j
    count = jnp.zeros((ROWS, 128), f32)
    for f, test in enumerate((i == 0.0, i == 4.0, j == 0.0, j == 4.0, k == 0.0, k == 4.0)):
        mask = jnp.where(test & (node < NODES - 0.5), 1.0, 0.0).astype(f32)
        W[f] = mask
        count = count + mask
    W[6] = count
    nb = nb_in[:, 0, :]
    target = lax.shift_right_logical(nb, 7)
    slot = nb & 127
    relative = lax.rem(target - me + m_size, m_size)
    for f in range(6):
        IDX[f] = jnp.broadcast_to(slot[f : f + 1], (8, 128))
        IDX[6 + f] = jnp.broadcast_to(relative[f : f + 1], (8, 128))
        for g in range(4):
            RIM[f, g] = jnp.broadcast_to((slot[f : f + 1] & 31) + 32 * g, (8, 128))
    S[...] = jnp.zeros((ROWS, ROWS), f32)
    S[0:NODES, 0:NODES] = stiff_in[...]
    s_hi, s_lo = split(S[...])
    material = mat_in[...]

    def strain(base):
        wide = jnp.concatenate([F[base + c, PAD : PAD + ROWS, :] for c in range(3)], axis=1)
        hi, lo = split(wide)
        both = mm(s_hi, hi) + (mm(s_hi, lo) + mm(s_lo, hi))
        return [both[:, 128 * c : 128 * (c + 1)] for c in range(3)]

    def face_sums(read, relative_to):
        sums = [None] * (ROWS // 8)
        for f in range(6):
            here = IDX[6 + f] == relative_to
            for t in range(ROWS // 8):
                if f in TILE_FACES[t]:
                    g = jnp.where(here, read(f, 8 * t + SHIFT[f]), 0.0)
                    g = g * W[f, 8 * t : 8 * t + 8, :]
                    sums[t] = g if sums[t] is None else sums[t] + g
        return sums

    def own_pass(base):
        def body(c, carry):
            sums = face_sums(lambda f, low: pick(F[base + c, low + PAD : low + 2 * PAD, :], IDX[f]), 0)
            for t in range(ROWS // 8):
                at = pl.ds(8 * t, 8)
                v = F[base + c, 8 * t + PAD : 8 * t + 2 * PAD, :]
                acc = sums[t] - W[6, at, :] * v
                N[base + c, at, :] = N[base + c, at, :] + (time_square * penalty) * acc
            return carry

        lax.fori_loop(0, 3, body, 0)

    def rim_pass(base, f, k, store, after_each=None):
        side = sides[k]
        relative_to = jnp.where(side == 1, 1, m_size - 1)

        def body(c, carry):
            rim_copy(f, k, c).wait_recv()
            if k == 0 and paired and straight(f) > 0:
                if straight(f) == 3:
                    relay_copy(f, c).start()
                else:

                    @pl.when(c < straight(f))
                    def _():
                        relay_copy(f, c).start()

            rim[f, side, c, 32:40, :] = pltpu.roll(rim[f, side, c, 0:8, :], 96, 1)

            def read(face, low):
                at = low % 32
                return pick(rim[f, side, c, at : at + 8, :], RIM[face, (low // 32) % 4])

            sums = face_sums(read, relative_to)
            for t in range(ROWS // 8):
                old = N[base + c, 8 * t : 8 * t + 8, :]
                store(c, t, old + (time_square * penalty) * sums[t])
            if after_each is not None:
                after_each(c)
            return carry

        lax.fori_loop(0, 3, body, 0)

    def send_next(c):
        send[2, c] = pack(c)
        rim_copy(2, 0, c).start()

    def add(base):
        def store(c, t, value):
            N[base + c, 8 * t : 8 * t + 8, :] = value

        return store

    st_f = strain(0)
    st_a = strain(3)
    energy = jnp.zeros((ROWS, 128), f32)
    for c in range(3):
        vf = F[c, PAD : PAD + ROWS, :]
        energy = energy + vf * st_a[c]
        N[c] = vf - time_square * material * st_f[c]
        N[3 + c] = F[3 + c, PAD : PAD + ROWS, :] - time_square * material * st_a[c]
    K[...] = energy
    send_near(0)
    own_pass(3)
    send_far(0)
    own_pass(0)
    next_round(0)

    def keep_adjoint(c, t, value):
        F[3 + c, 8 * t + PAD : 8 * t + 2 * PAD, :] = LIVE[...] * value

    def keep_forward(c, t, value):
        value = LIVE[...] * value
        at = pl.ds(8 * t + PAD, 8)
        line = pl.ds(8 * t, 8)
        N[c, line, :] = 2.0 * value - F[c, at, :]
        F[c, at, :] = value
        K[line, :] = K[line, :] + value * A[c, line, :]

    rim_pass(3, 1, 0, add(3))
    next_round(1)
    rim_pass(0, 0, 0, add(0))
    rim_pass(3, 1, 1, keep_adjoint)
    for n in range(2, n_rounds):
        next_round(n)
    for c, value in enumerate(strain(3)):
        A[c] = value
    rim_pass(0, 0, 1, keep_forward, send_next)

    elements = F.shape[-1]
    width = smooth_in.shape[1]
    scale = math.sqrt(width / elements) / STEPS
    twin = jnp.concatenate([proj_in[...], proj_in[...]], axis=0)
    t_hi, t_lo = split(twin)
    k_hi, k_lo = split(K[0:NODES, :])
    blocks = (mm(t_hi, k_hi) + (mm(t_hi, k_lo) + mm(t_lo, k_hi))) * scale
    b_hi, b_lo = split(blocks)
    row = lax.broadcasted_iota(jnp.int32, (total * width, 128), 0)
    owner = lax.div(row, width)
    tile = width * (lax.rem(owner, e_size) * m_size + lax.div(owner, e_size)) + lax.rem(row, width)
    dest = dest_in[...]
    nt = ((1,), (1,))

    def spread(offset):
        hot = jnp.where(tile + offset == dest, 1.0, 0.0).astype(f32).astype(bf16)
        return mm(hot, b_hi, nt) + mm(hot, b_lo, nt)

    packed = jnp.where(lane < 64, spread(-2), spread(2))
    msg[...] = packed.reshape(m_size, e_size, width, 128)

    def peer(oe, om):
        return lax.rem(ev + oe, e_size), lax.rem(me + om, m_size)

    if direct:
        offsets = [(oe, om) for oe in list(range(1, e_size)) + [0] for om in range(m_size) if oe or om]
        for oe, om in offsets:
            e, m = peer(oe, om)
            remote(msg.at[m, e], got.at[oe * m_size + om - 1], a_s.at[0], a_r.at[0], (e, m))
    else:
        a_copies = [
            remote(msg.at[lax.rem(me + o, m_size)], got.at[pl.ds(e_size * (o - 1), e_size)],
                   a_s.at[o - 1], a_r.at[o - 1], (ev, lax.rem(me + o, m_size)))
            for o in range(1, m_size)
        ]

    send_far(2)

    st_f = strain(0)
    for c in range(3):
        N[c] = N[c] - time_square * material * st_f[c]
    own_pass(0)

    for copy in coef_copies:
        copy.wait_recv()
    coef_copies += [
        remote(coef_in.at[0], coef_in.at[2], coef_s.at[2], coef_r.at[2],
               (lax.rem(ev + 1, e_size), me)),
        remote(coef_in.at[1], coef_in.at[3], coef_s.at[3], coef_r.at[3],
               (lax.rem(ev + e_size - 1, e_size), me)),
    ]
    if not direct:
        for copy in a_copies:
            copy.wait_recv()
        mine_sum = msg[me]
        for o in range(m_size - 1):
            mine_sum = mine_sum + got[e_size * o : e_size * (o + 1)]
        part[...] = mine_sum
        b_copies = [
            remote(part.at[lax.rem(ev + o, e_size)], got2.at[o - 1], b_s.at[o - 1], b_r.at[o - 1],
                   (lax.rem(ev + o, e_size), me))
            for o in range(1, e_size)
        ]

    def final(c, t, value):
        fwd_out[c, 8 * t : 8 * t + 8, :] = LIVE[...] * value

    rim_pass(0, 2, 0, add(0))
    rim_pass(0, 2, 1, final)

    for copy in coef_copies[2:]:
        copy.wait_recv()
    own_coef = pltpu.roll(coef[...], 2, 1)
    left = jnp.where(lin > 0, jnp.where(me > 0, coef_in[0], coef_in[2]), 0.0)
    right = jnp.where(
        lin < total - 1, jnp.where(me < m_size - 1, coef_in[1], coef_in[3]), 0.0
    )
    left = jnp.where(lane < 2, pltpu.roll(left, 126, 1), 0.0)
    right = pltpu.roll(right, 6, 1)
    mine[...] = jnp.zeros((128, 128), f32)
    mine[0:8, :] = own_coef + left + right
    coefs = mine[...].T[0:8]

    def smooth(x):
        chain = pltpu.roll(x, 1, 0) + pltpu.roll(x, 7, 0) - 2.0 * x
        new = x + coefs[:, 0:1] * chain
        for d, shift in ((1, 4), (2, 2), (3, 0)):
            digit = lax.shift_right_logical(lane, shift) & 3
            up = jnp.where(digit == 0, 0.0, pltpu.roll(x, 1 << shift, 1))
            down = jnp.where(digit == 3, 0.0, pltpu.roll(x, 128 - (1 << shift), 1))
            new = new + coefs[:, d : d + 1] * (up + down - 2.0 * x)
        return jnp.where(lane < 64, new, 0.0)

    if direct:
        gathered = pltpu.make_async_remote_copy(
            src_ref=got, dst_ref=got, send_sem=a_s.at[0], recv_sem=a_r.at[0],
            device_id=peer(1, 0), device_id_type=MESH,
        )
        gathered.wait_recv()
        parts = [msg[me, ev]] + [got[n] for n in range(total - 1)]
    else:
        for copy in b_copies:
            copy.wait_recv()
        parts = [part[ev]] + [got2[o] for o in range(e_size - 1)]
    while len(parts) > 1:
        parts = [sum(parts[n : n + 2][1:], parts[n]) for n in range(0, len(parts), 2)]
    summed = parts[0]
    x = jnp.concatenate([summed, pltpu.roll(summed, 64, 1)], axis=0)
    x = smooth(smooth(jnp.where(lane < 64, x, 0.0)))
    tiles_out[...] = x[2 : 2 + width, 0:64]

    for f in range(3):
        for k in range(2):
            for c in range(3):
                rim_copy(f, k, c).wait_send()
    if direct:
        gathered.wait_send()
    else:
        for copy in a_copies + b_copies:
            copy.wait_send()
    for copy in coef_copies:
        copy.wait_send()


def write_out(final_vmem, tiles_vmem, final_hbm, tiles_hbm, sems):
    copies = [
        pltpu.make_async_copy(
            final_vmem.at[c, pl.ds(0, NODES)], final_hbm.at[pl.ds(NODES * c, NODES), 0], sems.at[c]
        )
        for c in range(3)
    ]
    copies.append(pltpu.make_async_copy(tiles_vmem, tiles_hbm, sems.at[3]))
    for copy in copies:
        copy.start()
    for copy in copies:
        copy.wait()


def solution(mesh):
    m_size, e_size = mesh.shape["mesh"], mesh.shape["event"]
    in_specs = (
        P("event", None, None, "mesh"),
        P("event", None, None, "mesh"),
        P(),
        P(),
        P("event", "mesh"),
        P("event", None, "mesh"),
        P("event", "mesh"),
        P("event", "mesh"),
        P(None, ("event", "mesh")),
    )
    out_specs = (P("event", None, None, "mesh"), P(None, ("event", "mesh")))

    def per_device(*args):
        fwd, smoothing = args[0], args[-1]
        width = smoothing.shape[1]
        dma = pltpu.SemaphoreType.DMA
        vmem = pl.BlockSpec(memory_space=pltpu.VMEM)
        hbm = pl.BlockSpec(memory_space=pltpu.HBM)
        line = (3 * NODES, 1, fwd.shape[-1])
        args = (args[0].reshape(line), args[1].reshape(line), args[2], args[3].T, args[4],
                args[5].reshape(6, 1, fwd.shape[-1]), *args[6:])
        if is_direct(m_size, e_size):
            a_count, b_count = 1, 1
            part, got, got2 = (1, width, 128), (m_size * e_size - 1, width, 128), (1, width, 128)
        else:
            a_count, b_count = m_size - 1, e_size - 1
            part, got, got2 = (e_size, width, 128), ((m_size - 1) * e_size, width, 128), (e_size - 1, width, 128)
        final, tiles = pl.pallas_call(
            functools.partial(kernel, m_size, e_size),
            out_shape=(
                pltpu.VMEM((3, ROWS, 128), f32),
                pltpu.VMEM((width, 64), f32),
            ),
            in_specs=[hbm] * len(args),
            out_specs=(vmem, vmem),
            scratch_shapes=[pltpu.VMEM(x.shape, x.dtype) for x in args[2:]]
            + [
                pltpu.VMEM((6, 144, 128), f32),
                pltpu.VMEM((6, ROWS, 128), f32),
                pltpu.VMEM((ROWS, 128), f32),
                pltpu.VMEM((3, ROWS, 128), f32),
                pltpu.VMEM((ROWS, ROWS), f32),
                pltpu.VMEM((7, ROWS, 128), f32),
                pltpu.VMEM((12, 8, 128), jnp.int32),
                pltpu.VMEM((6, 4, 8, 128), jnp.int32),
                pltpu.VMEM((8, 128), f32),
                pltpu.VMEM((3, 3, 32, 128), f32),
                pltpu.VMEM((3, 2, 3, 40, 128), f32),
                pltpu.VMEM((8, 128), f32),
                pltpu.VMEM((4, 8, 128), f32),
                pltpu.VMEM((m_size, e_size, width, 128), f32),
                pltpu.VMEM((128, 128), f32),
                pltpu.VMEM(part, f32),
                pltpu.VMEM(got, f32),
                pltpu.VMEM(got2, f32),
                dma((6,)), dma((7,)), dma((3, 2, 3)), dma((3, 2, 3)), dma((4,)), dma((4,)),
                dma((a_count,)), dma((a_count,)), dma((b_count,)), dma((b_count,)),
                pltpu.SemaphoreType.REGULAR((max(round_count(m_size, e_size), 1),)),
            ],
            compiler_params=pltpu.CompilerParams(collective_id=0, has_side_effects=True),
        )(*args)
        final, tiles = pl.pallas_call(
            write_out,
            out_shape=(pltpu.HBM(line, f32), pltpu.HBM((width, 64), f32)),
            in_specs=[vmem, vmem],
            out_specs=(hbm, hbm),
            scratch_shapes=[dma((4,))],
        )(
            pltpu.with_memory_space_constraint(final, pltpu.VMEM),
            pltpu.with_memory_space_constraint(tiles, pltpu.VMEM),
        )
        return final.reshape(fwd.shape), tiles.T

    return jax.shard_map(
        per_device, mesh=mesh, in_specs=in_specs, out_specs=out_specs, check_vma=False
    )
```

```python
import functools
import math

import jax
import jax.numpy as jnp
from jax import lax
from jax.experimental import pallas as pl
from jax.experimental.pallas import tpu as pltpu
from jax.sharding import PartitionSpec as P

STEPS = 2
time_square = 0.4
penalty = 0.5

PAD = 8
ROWS = 128
NODES = 125
SHIFT = (100, -100, 20, -20, 4, -4)
MESH = pl.DeviceIdType.MESH
f32 = jnp.float32
bf16 = jnp.bfloat16


def on_face(face, node):
    i, j, k = node // 25, (node // 5) % 5, node % 5
    return (i == 0, i == 4, j == 0, j == 4, k == 0, k == 4)[face]


FACE_TILES = [
    (f, t)
    for t in range(ROWS // 8)
    for f in range(6)
    if any(on_face(f, n) for n in range(8 * t, min(8 * t + 8, NODES)))
]


def split(x):
    high = x.astype(bf16)
    return high, (x - high.astype(f32)).astype(bf16)


def mm(a, b, dims=((1,), (0,))):
    return lax.dot_general(a, b, (dims, ((), ())), preferred_element_type=f32)


def pick(x, index):
    return jnp.take_along_axis(x, index, axis=1, mode="promise_in_bounds")


def is_direct(m_size, e_size):
    return m_size * e_size <= 64


def round_count(m_size, e_size):
    return max(e_size // 2 - 1, 1) if is_direct(m_size, e_size) else max(e_size // 2 - 2, 0)


def kernel(
    m_size, e_size,
    fwd_in, adj_in, stiff_hbm, proj_hbm, mat_hbm, nb_hbm, dest_hbm, count_hbm, smooth_hbm,
    fwd_out, tiles_out,
    stiff_in, proj_in, mat_in, nb_in, dest_in, count_in, smooth_in,
    F, N, K, A, S, W, M, IDX, RIM, LIVE, send, rim, coef, coef_in, msg, mine, part, got, got2,
    in_s, small_s, rim_s, rim_r, coef_s, coef_r, a_s, a_r, b_s, b_r, rounds,
):
    me = lax.axis_index("mesh")
    ev = lax.axis_index("event")
    total = m_size * e_size
    direct = is_direct(m_size, e_size)
    lin = ev * m_size + me
    after = lax.rem(me + 1, m_size)
    before = lax.rem(me + m_size - 1, m_size)

    barrier = pltpu.get_barrier_semaphore()
    core = lax.rem(ev, 2)
    chip = lax.div(ev, 2)
    chips = e_size // 2
    near = [((2 * chip + 1 - core, me), None)]
    for step in (1, -1):
        inside = (chip + step >= 0) & (chip + step < chips)
        near += [((2 * (chip + step) + c, me), inside) for c in range(2)]
    near_count = 1 + 2 * ((chip > 0).astype(jnp.int32) + (chip < chips - 1).astype(jnp.int32))

    def greet(sem):
        for device, inside in near:
            if inside is None:
                pl.semaphore_signal(sem, inc=1, device_id=device, device_id_type=MESH)
            else:

                @pl.when(inside)
                def _():
                    pl.semaphore_signal(sem, inc=1, device_id=device, device_id_type=MESH)

    for o in range(1, m_size):
        pl.semaphore_signal(
            barrier, inc=1, device_id=(ev, lax.rem(me + o, m_size)), device_id_type=MESH
        )
    greet(barrier)

    loads = {}
    for fc in (3, 4, 5, 0, 1, 2):
        source = fwd_in if fc < 3 else adj_in
        load = pltpu.make_async_copy(
            source.at[pl.ds(NODES * (fc % 3), NODES), 0], F.at[fc, pl.ds(PAD, NODES)], in_s.at[fc]
        )
        load.start()
        loads[fc] = load

    small = []
    for n, (src, dst) in enumerate((
        (smooth_hbm, smooth_in), (stiff_hbm, stiff_in), (nb_hbm, nb_in), (count_hbm, count_in),
        (mat_hbm, mat_in), (proj_hbm, proj_in), (dest_hbm, dest_in),
    )):
        load = pltpu.make_async_copy(src, dst, small_s.at[n])
        load.start()
        small.append(load)

    lane = lax.broadcasted_iota(jnp.int32, (1, 128), 1)
    zero8 = jnp.zeros((PAD, 128), f32)
    for fc in range(6):
        F[fc, 0:PAD, :] = zero8
        F[fc, PAD + NODES : 144, :] = jnp.zeros((144 - PAD - NODES, 128), f32)

    def pack(fc):
        wide = [F[fc, PAD + 32 * g : PAD + 32 * g + 32, :] for g in range(4)]
        turned = [wide[0]] + [pltpu.roll(wide[g], 32 * g, 1) for g in range(1, 4)]
        return jnp.where(
            lane < 64, jnp.where(lane < 32, turned[0], turned[1]),
            jnp.where(lane < 96, turned[2], turned[3]),
        )

    def load_field(f):
        for c in range(3):
            loads[3 * f + c].wait()
            send[f, c] = pack(3 * f + c)

    load_field(1)

    pl.semaphore_wait(barrier, near_count + (m_size - 1))

    def remote(src, dst, s, r, device):
        copy = pltpu.make_async_remote_copy(
            src_ref=src, dst_ref=dst, send_sem=s, recv_sem=r, device_id=device, device_id_type=MESH
        )
        copy.start()
        return copy

    paired = m_size == 4
    first = 1 - lax.rem(me, 2) if paired else 0
    second = 1 - first
    sides = (first, second)
    low32 = pl.ds(0, 32)

    def rim_copy(f, k, c):
        slot = sides[1 - k] if paired else sides[k]
        return pltpu.make_async_remote_copy(
            src_ref=send.at[f, c], dst_ref=rim.at[f, slot, c, low32],
            send_sem=rim_s.at[f, k, c], recv_sem=rim_r.at[f, k, c],
            device_id=(ev, jnp.where(slot == 0, after, before)), device_id_type=MESH,
        )

    def relay_copy(f, c):
        return pltpu.make_async_remote_copy(
            src_ref=rim.at[f, first, c, low32], dst_ref=rim.at[f, second, c, low32],
            send_sem=rim_s.at[f, 1, c], recv_sem=rim_r.at[f, 1, c],
            device_id=(ev, lax.rem(me + 2, m_size)), device_id_type=MESH,
        )

    def send_near(f):
        for c in range(3):
            rim_copy(f, 0, c).start()

    def send_far(f):
        for c in range(3):
            rim_copy(f, 1, c).start()

    def at_core(which, job):
        @pl.when(core == which)
        def _():
            job()

    send_near(1)
    load_field(0)
    coef[...] = jnp.zeros((8, 128), f32)
    small[0].wait()
    coef[0:4, 0:4] = smooth_in[...]
    at_core(0, lambda: (send_far(1), send_near(0), send_far(0)))
    coef_copies = [
        remote(coef, coef_in.at[0], coef_s.at[0], coef_r.at[0], (ev, after)),
        remote(coef, coef_in.at[1], coef_s.at[1], coef_r.at[1], (ev, before)),
    ]
    n_rounds = round_count(m_size, e_size)
    if n_rounds:
        greet(rounds.at[0])

    def next_round(n):
        if n < n_rounds:
            pl.semaphore_wait(rounds.at[n], near_count)
            if n + 1 < n_rounds:
                greet(rounds.at[n + 1])

    for load in small[1:]:
        load.wait()
    live = jnp.where(lane < count_in[0:1, 0:1], 1.0, 0.0).astype(f32)
    LIVE[...] = jnp.broadcast_to(live, (8, 128))
    for fc in range(6):
        F[fc, PAD : PAD + NODES, :] = F[fc, PAD : PAD + NODES, :] * live

    node = lax.broadcasted_iota(jnp.int32, (ROWS, 128), 0).astype(f32)
    i = jnp.floor((node + 0.5) / 25.0)
    rest = node - 25.0 * i
    j = jnp.floor((rest + 0.5) / 5.0)
    k = rest - 5.0 * j
    count = jnp.zeros((ROWS, 128), f32)
    for f, test in enumerate((i == 0.0, i == 4.0, j == 0.0, j == 4.0, k == 0.0, k == 4.0)):
        mask = jnp.where(test & (node < NODES - 0.5), 1.0, 0.0).astype(f32)
        W[f] = mask
        count = count + mask
    W[6] = count
    nb = nb_in[:, 0, :]
    target = lax.shift_right_logical(nb, 7)
    slot = nb & 127
    relative = lax.rem(target - me + m_size, m_size)
    for f in range(6):
        IDX[f] = jnp.broadcast_to(slot[f : f + 1], (8, 128))
        IDX[6 + f] = jnp.broadcast_to(relative[f : f + 1], (8, 128))
        for g in range(4):
            RIM[f, g] = jnp.broadcast_to((slot[f : f + 1] & 31) + 32 * g, (8, 128))
    S[...] = jnp.zeros((ROWS, ROWS), f32)
    S[0:NODES, 0:NODES] = stiff_in[...]
    s_hi, s_lo = split(S[...])
    material = mat_in[...]

    def strain(base):
        wide = jnp.concatenate([F[base + c, PAD : PAD + ROWS, :] for c in range(3)], axis=1)
        hi, lo = split(wide)
        both = mm(s_hi, hi) + (mm(s_hi, lo) + mm(s_lo, hi))
        return [both[:, 128 * c : 128 * (c + 1)] for c in range(3)]

    def build_masks(which, relative_to):
        here = [jnp.where(IDX[6 + f] == relative_to, 1.0, 0.0).astype(f32) for f in range(6)]
        for n, (f, t) in enumerate(FACE_TILES):
            M[which, n] = here[f] * W[f, 8 * t : 8 * t + 8, :]

    def face_sums(read, which):
        sums = [None] * (ROWS // 8)
        for n, (f, t) in enumerate(FACE_TILES):
            g = read(f, 8 * t + SHIFT[f]) * M[which, n]
            sums[t] = g if sums[t] is None else sums[t] + g
        return sums

    def own_pass(base):
        for c in range(3):
            sums = face_sums(lambda f, low: pick(F[base + c, low + PAD : low + 2 * PAD, :], IDX[f]), 0)
            for t in range(ROWS // 8):
                at = pl.ds(8 * t, 8)
                v = F[base + c, 8 * t + PAD : 8 * t + 2 * PAD, :]
                acc = sums[t] - W[6, at, :] * v
                N[base + c, at, :] = N[base + c, at, :] + (time_square * penalty) * acc

    def arrive(f, k):
        for c in range(3):
            rim_copy(f, k, c).wait_recv()
            if k == 0 and paired:

                @pl.when(core == 1)
                def _():
                    relay_copy(f, c).start()

    def rim_pass(base, f, k, store, after_each=None):
        side = sides[k]
        for c in range(3):
            rim[f, side, c, 32:40, :] = pltpu.roll(rim[f, side, c, 0:8, :], 96, 1)
        for c in range(3):

            def read(face, low):
                at = low % 32
                return pick(rim[f, side, c, at : at + 8, :], RIM[face, (low // 32) % 4])

            sums = face_sums(read, 1 + k)
            for t in range(ROWS // 8):
                old = N[base + c, 8 * t : 8 * t + 8, :]
                store(c, t, old + (time_square * penalty) * sums[t])
            if after_each is not None:
                after_each(c)

    def send_next(c):
        send[2, c] = pack(c)
        rim_copy(2, 0, c).start()

    def add(base):
        def store(c, t, value):
            N[base + c, 8 * t : 8 * t + 8, :] = value

        return store

    build_masks(0, 0)
    st_f = strain(0)
    st_a = strain(3)
    energy = jnp.zeros((ROWS, 128), f32)
    for c in range(3):
        vf = F[c, PAD : PAD + ROWS, :]
        energy = energy + vf * st_a[c]
        N[c] = vf - time_square * material * st_f[c]
        N[3 + c] = F[3 + c, PAD : PAD + ROWS, :] - time_square * material * st_a[c]
    K[...] = energy
    if not paired:
        at_core(1, lambda: (send_far(1), send_near(0), send_far(0)))
    else:
        at_core(1, lambda: send_near(0))
    own_pass(3)
    own_pass(0)
    next_round(0)
    for k in range(2):
        build_masks(1 + k, jnp.where(sides[k] == 1, 1, m_size - 1))

    def keep_adjoint(c, t, value):
        F[3 + c, 8 * t + PAD : 8 * t + 2 * PAD, :] = LIVE[...] * value

    def keep_forward(c, t, value):
        value = LIVE[...] * value
        at = pl.ds(8 * t + PAD, 8)
        line = pl.ds(8 * t, 8)
        N[c, line, :] = 2.0 * value - F[c, at, :]
        F[c, at, :] = value
        K[line, :] = K[line, :] + value * A[c, line, :]

    arrive(1, 0)
    rim_pass(3, 1, 0, add(3))
    next_round(1)
    if paired:
        at_core(1, lambda: arrive(0, 0))
    arrive(1, 1)
    rim_pass(3, 1, 1, keep_adjoint)
    for n in range(2, n_rounds):
        next_round(n)
    for c, value in enumerate(strain(3)):
        A[c] = value
    if paired:
        at_core(0, lambda: arrive(0, 0))
    else:
        arrive(0, 0)
    rim_pass(0, 0, 0, add(0))
    arrive(0, 1)
    rim_pass(0, 0, 1, keep_forward, send_next)

    elements = F.shape[-1]
    width = smooth_in.shape[1]
    scale = math.sqrt(width / elements) / STEPS
    twin = jnp.concatenate([proj_in[...], proj_in[...]], axis=0)
    t_hi, t_lo = split(twin)
    k_hi, k_lo = split(K[0:NODES, :])
    blocks = (mm(t_hi, k_hi) + (mm(t_hi, k_lo) + mm(t_lo, k_hi))) * scale
    b_hi, b_lo = split(blocks)
    row = lax.broadcasted_iota(jnp.int32, (total * width, 128), 0)
    owner = lax.div(row, width)
    tile = width * (lax.rem(owner, e_size) * m_size + lax.div(owner, e_size)) + lax.rem(row, width)
    dest = dest_in[...]
    nt = ((1,), (1,))

    def spread(offset):
        hot = jnp.where(tile + offset == dest, 1.0, 0.0).astype(f32).astype(bf16)
        return mm(hot, b_hi, nt) + mm(hot, b_lo, nt)

    packed = jnp.where(lane < 64, spread(-2), spread(2))
    msg[...] = packed.reshape(m_size, e_size, width, 128)

    def peer(oe, om):
        return lax.rem(ev + oe, e_size), lax.rem(me + om, m_size)

    if direct:
        offsets = [(oe, om) for oe in list(range(1, e_size)) + [0] for om in range(m_size) if oe or om]
        for oe, om in offsets:
            e, m = peer(oe, om)
            remote(msg.at[m, e], got.at[oe * m_size + om - 1], a_s.at[0], a_r.at[0], (e, m))
    else:
        a_copies = [
            remote(msg.at[lax.rem(me + o, m_size)], got.at[pl.ds(e_size * (o - 1), e_size)],
                   a_s.at[o - 1], a_r.at[o - 1], (ev, lax.rem(me + o, m_size)))
            for o in range(1, m_size)
        ]

    if paired:
        at_core(0, lambda: send_far(2))
    else:
        send_far(2)

    st_f = strain(0)
    for c in range(3):
        N[c] = N[c] - time_square * material * st_f[c]
    own_pass(0)

    for copy in coef_copies:
        copy.wait_recv()
    coef_copies += [
        remote(coef_in.at[0], coef_in.at[2], coef_s.at[2], coef_r.at[2],
               (lax.rem(ev + 1, e_size), me)),
        remote(coef_in.at[1], coef_in.at[3], coef_s.at[3], coef_r.at[3],
               (lax.rem(ev + e_size - 1, e_size), me)),
    ]
    if not direct:
        for copy in a_copies:
            copy.wait_recv()
        mine_sum = msg[me]
        for o in range(m_size - 1):
            mine_sum = mine_sum + got[e_size * o : e_size * (o + 1)]
        part[...] = mine_sum
        b_copies = [
            remote(part.at[lax.rem(ev + o, e_size)], got2.at[o - 1], b_s.at[o - 1], b_r.at[o - 1],
                   (lax.rem(ev + o, e_size), me))
            for o in range(1, e_size)
        ]

    def final(c, t, value):
        fwd_out[c, 8 * t : 8 * t + 8, :] = LIVE[...] * value

    arrive(2, 0)
    rim_pass(0, 2, 0, add(0))
    arrive(2, 1)
    rim_pass(0, 2, 1, final)

    for copy in coef_copies[2:]:
        copy.wait_recv()
    own_coef = pltpu.roll(coef[...], 2, 1)
    left = jnp.where(lin > 0, jnp.where(me > 0, coef_in[0], coef_in[2]), 0.0)
    right = jnp.where(
        lin < total - 1, jnp.where(me < m_size - 1, coef_in[1], coef_in[3]), 0.0
    )
    left = jnp.where(lane < 2, pltpu.roll(left, 126, 1), 0.0)
    right = pltpu.roll(right, 6, 1)
    mine[...] = jnp.zeros((128, 128), f32)
    mine[0:8, :] = own_coef + left + right
    coefs = mine[...].T[0:8]

    def smooth(x):
        chain = pltpu.roll(x, 1, 0) + pltpu.roll(x, 7, 0) - 2.0 * x
        new = x + coefs[:, 0:1] * chain
        for d, shift in ((1, 4), (2, 2), (3, 0)):
            digit = lax.shift_right_logical(lane, shift) & 3
            up = jnp.where(digit == 0, 0.0, pltpu.roll(x, 1 << shift, 1))
            down = jnp.where(digit == 3, 0.0, pltpu.roll(x, 128 - (1 << shift), 1))
            new = new + coefs[:, d : d + 1] * (up + down - 2.0 * x)
        return jnp.where(lane < 64, new, 0.0)

    if direct:
        gathered = pltpu.make_async_remote_copy(
            src_ref=got, dst_ref=got, send_sem=a_s.at[0], recv_sem=a_r.at[0],
            device_id=peer(1, 0), device_id_type=MESH,
        )
        gathered.wait_recv()
        parts = [msg[me, ev]] + [got[n] for n in range(total - 1)]
    else:
        for copy in b_copies:
            copy.wait_recv()
        parts = [part[ev]] + [got2[o] for o in range(e_size - 1)]
    while len(parts) > 1:
        parts = [sum(parts[n : n + 2][1:], parts[n]) for n in range(0, len(parts), 2)]
    summed = parts[0]
    x = jnp.concatenate([summed, pltpu.roll(summed, 64, 1)], axis=0)
    x = smooth(smooth(jnp.where(lane < 64, x, 0.0)))
    tiles_out[...] = x[2 : 2 + width, 0:64]

    for f in range(3):
        for k in range(2):
            for c in range(3):
                rim_copy(f, k, c).wait_send()
    if direct:
        gathered.wait_send()
    else:
        for copy in a_copies + b_copies:
            copy.wait_send()
    for copy in coef_copies:
        copy.wait_send()


def write_out(final_vmem, tiles_vmem, final_hbm, tiles_hbm, sems):
    copies = [
        pltpu.make_async_copy(
            final_vmem.at[c, pl.ds(0, NODES)], final_hbm.at[pl.ds(NODES * c, NODES), 0], sems.at[c]
        )
        for c in range(3)
    ]
    copies.append(pltpu.make_async_copy(tiles_vmem, tiles_hbm, sems.at[3]))
    for copy in copies:
        copy.start()
    for copy in copies:
        copy.wait()


def solution(mesh):
    m_size, e_size = mesh.shape["mesh"], mesh.shape["event"]
    in_specs = (
        P("event", None, None, "mesh"),
        P("event", None, None, "mesh"),
        P(),
        P(),
        P("event", "mesh"),
        P("event", None, "mesh"),
        P("event", "mesh"),
        P("event", "mesh"),
        P(None, ("event", "mesh")),
    )
    out_specs = (P("event", None, None, "mesh"), P(None, ("event", "mesh")))

    def per_device(*args):
        fwd, smoothing = args[0], args[-1]
        width = smoothing.shape[1]
        dma = pltpu.SemaphoreType.DMA
        vmem = pl.BlockSpec(memory_space=pltpu.VMEM)
        hbm = pl.BlockSpec(memory_space=pltpu.HBM)
        line = (3 * NODES, 1, fwd.shape[-1])
        args = (args[0].reshape(line), args[1].reshape(line), args[2], args[3].T, args[4],
                args[5].reshape(6, 1, fwd.shape[-1]), *args[6:])
        if is_direct(m_size, e_size):
            a_count, b_count = 1, 1
            part, got, got2 = (1, width, 128), (m_size * e_size - 1, width, 128), (1, width, 128)
        else:
            a_count, b_count = m_size - 1, e_size - 1
            part, got, got2 = (e_size, width, 128), ((m_size - 1) * e_size, width, 128), (e_size - 1, width, 128)
        final, tiles = pl.pallas_call(
            functools.partial(kernel, m_size, e_size),
            out_shape=(
                pltpu.VMEM((3, ROWS, 128), f32),
                pltpu.VMEM((width, 64), f32),
            ),
            in_specs=[hbm] * len(args),
            out_specs=(vmem, vmem),
            scratch_shapes=[pltpu.VMEM(x.shape, x.dtype) for x in args[2:]]
            + [
                pltpu.VMEM((6, 144, 128), f32),
                pltpu.VMEM((6, ROWS, 128), f32),
                pltpu.VMEM((ROWS, 128), f32),
                pltpu.VMEM((3, ROWS, 128), f32),
                pltpu.VMEM((ROWS, ROWS), f32),
                pltpu.VMEM((7, ROWS, 128), f32),
                pltpu.VMEM((3, len(FACE_TILES), 8, 128), f32),
                pltpu.VMEM((12, 8, 128), jnp.int32),
                pltpu.VMEM((6, 4, 8, 128), jnp.int32),
                pltpu.VMEM((8, 128), f32),
                pltpu.VMEM((3, 3, 32, 128), f32),
                pltpu.VMEM((3, 2, 3, 40, 128), f32),
                pltpu.VMEM((8, 128), f32),
                pltpu.VMEM((4, 8, 128), f32),
                pltpu.VMEM((m_size, e_size, width, 128), f32),
                pltpu.VMEM((128, 128), f32),
                pltpu.VMEM(part, f32),
                pltpu.VMEM(got, f32),
                pltpu.VMEM(got2, f32),
                dma((6,)), dma((7,)), dma((3, 2, 3)), dma((3, 2, 3)), dma((4,)), dma((4,)),
                dma((a_count,)), dma((a_count,)), dma((b_count,)), dma((b_count,)),
                pltpu.SemaphoreType.REGULAR((max(round_count(m_size, e_size), 1),)),
            ],
            compiler_params=pltpu.CompilerParams(collective_id=0, has_side_effects=True),
        )(*args)
        final, tiles = pl.pallas_call(
            write_out,
            out_shape=(pltpu.HBM(line, f32), pltpu.HBM((width, 64), f32)),
            in_specs=[vmem, vmem],
            out_specs=(hbm, hbm),
            scratch_shapes=[dma((4,))],
        )(
            pltpu.with_memory_space_constraint(final, pltpu.VMEM),
            pltpu.with_memory_space_constraint(tiles, pltpu.VMEM),
        )
        return final.reshape(fwd.shape), tiles.T

    return jax.shard_map(
        per_device, mesh=mesh, in_specs=in_specs, out_specs=out_specs, check_vma=False
    )
```

```python
import functools
import math

import jax
import jax.numpy as jnp
from jax import lax
from jax.experimental import pallas as pl
from jax.experimental.pallas import tpu as pltpu
from jax.sharding import PartitionSpec as P

STEPS = 2
time_square = 0.4
penalty = 0.5

PAD = 8
ROWS = 128
NODES = 125
SHIFT = (100, -100, 20, -20, 4, -4)
MESH = pl.DeviceIdType.MESH
f32 = jnp.float32
bf16 = jnp.bfloat16


def on_face(face, node):
    i, j, k = node // 25, (node // 5) % 5, node % 5
    return (i == 0, i == 4, j == 0, j == 4, k == 0, k == 4)[face]


FACE_TILES = [
    (f, t)
    for f in range(6)
    for t in range(ROWS // 8)
    if any(on_face(f, n) for n in range(8 * t, min(8 * t + 8, NODES)))
]


def split(x):
    high = x.astype(bf16)
    return high, (x - high.astype(f32)).astype(bf16)


def mm(a, b, dims=((1,), (0,))):
    return lax.dot_general(a, b, (dims, ((), ())), preferred_element_type=f32)


def pick(x, index):
    dims = lax.GatherDimensionNumbers(
        offset_dims=(), collapsed_slice_dims=(1,), start_index_map=(1,),
        operand_batching_dims=(0,), start_indices_batching_dims=(0,),
    )
    return lax.gather(x, index[:, :, None], dims, (1, 1), mode=lax.GatherScatterMode.PROMISE_IN_BOUNDS)


def is_direct(m_size, e_size):
    return m_size * e_size <= 64


def round_count(m_size, e_size):
    return max(e_size // 2 - 1, 1) if is_direct(m_size, e_size) else max(e_size // 2 - 2, 0)


def kernel(
    m_size, e_size,
    fwd_in, adj_in, stiff_hbm, proj_hbm, mat_hbm, nb_hbm, dest_hbm, count_hbm, smooth_hbm,
    fwd_out, tiles_out,
    stiff_in, proj_in, mat_in, nb_in, dest_in, count_in, smooth_in,
    F, N, K, A, S, W, M, IDX, RIM, LIVE, send, rim, U, coef, coef_in, msg, mine, part, got, got2,
    in_s, small_s, rim_s, rim_r, coef_s, coef_r, a_s, a_r, b_s, b_r, rounds,
):
    me = lax.axis_index("mesh")
    ev = lax.axis_index("event")
    total = m_size * e_size
    direct = is_direct(m_size, e_size)
    lin = ev * m_size + me
    after = lax.rem(me + 1, m_size)
    before = lax.rem(me + m_size - 1, m_size)

    barrier = pltpu.get_barrier_semaphore()
    core = lax.rem(ev, 2)
    chip = lax.div(ev, 2)
    chips = e_size // 2
    near = [((2 * chip + 1 - core, me), None)]
    for step in (1, -1):
        inside = (chip + step >= 0) & (chip + step < chips)
        near += [((2 * (chip + step) + c, me), inside) for c in range(2)]
    near_count = 1 + 2 * ((chip > 0).astype(jnp.int32) + (chip < chips - 1).astype(jnp.int32))

    def greet(sem):
        for device, inside in near:
            if inside is None:
                pl.semaphore_signal(sem, inc=1, device_id=device, device_id_type=MESH)
            else:

                @pl.when(inside)
                def _():
                    pl.semaphore_signal(sem, inc=1, device_id=device, device_id_type=MESH)

    for o in range(1, m_size):
        pl.semaphore_signal(
            barrier, inc=1, device_id=(ev, lax.rem(me + o, m_size)), device_id_type=MESH
        )
    greet(barrier)

    loads = {}
    for fc in (3, 4, 5, 0, 1, 2):
        source = fwd_in if fc < 3 else adj_in
        load = pltpu.make_async_copy(
            source.at[pl.ds(NODES * (fc % 3), NODES), 0], F.at[fc, pl.ds(PAD, NODES)], in_s.at[fc]
        )
        load.start()
        loads[fc] = load

    small = []
    for n, (src, dst) in enumerate((
        (smooth_hbm, smooth_in), (stiff_hbm, stiff_in), (nb_hbm, nb_in), (count_hbm, count_in),
        (mat_hbm, mat_in), (proj_hbm, proj_in), (dest_hbm, dest_in),
    )):
        load = pltpu.make_async_copy(src, dst, small_s.at[n])
        load.start()
        small.append(load)

    lane = lax.broadcasted_iota(jnp.int32, (1, 128), 1)
    zero8 = jnp.zeros((PAD, 128), f32)
    for fc in range(6):
        F[fc, 0:PAD, :] = zero8
        F[fc, PAD + NODES : 144, :] = jnp.zeros((144 - PAD - NODES, 128), f32)

    def pack(fc):
        wide = [F[fc, PAD + 32 * g : PAD + 32 * g + 32, :] for g in range(4)]
        turned = [wide[0]] + [pltpu.roll(wide[g], 32 * g, 1) for g in range(1, 4)]
        return jnp.where(
            lane < 64, jnp.where(lane < 32, turned[0], turned[1]),
            jnp.where(lane < 96, turned[2], turned[3]),
        )

    def load_field(f):
        for c in range(3):
            loads[3 * f + c].wait()
            send[f, c] = pack(3 * f + c)

    load_field(1)

    pl.semaphore_wait(barrier, near_count + (m_size - 1))

    def remote(src, dst, s, r, device):
        copy = pltpu.make_async_remote_copy(
            src_ref=src, dst_ref=dst, send_sem=s, recv_sem=r, device_id=device, device_id_type=MESH
        )
        copy.start()
        return copy

    paired = m_size == 4
    first = 1 - lax.rem(me, 2) if paired else 0
    second = 1 - first
    sides = (first, second)

    def rim_copy(f, k, c):
        slot = sides[1 - k] if paired else sides[k]
        return pltpu.make_async_remote_copy(
            src_ref=send.at[f, c], dst_ref=rim.at[f, slot, c],
            send_sem=rim_s.at[f, k, c], recv_sem=rim_r.at[f, k, c],
            device_id=(ev, jnp.where(slot == 0, after, before)), device_id_type=MESH,
        )

    def relay_copy(f, c):
        return pltpu.make_async_remote_copy(
            src_ref=rim.at[f, first, c], dst_ref=rim.at[f, second, c],
            send_sem=rim_s.at[f, 1, c], recv_sem=rim_r.at[f, 1, c],
            device_id=(ev, lax.rem(me + 2, m_size)), device_id_type=MESH,
        )

    def send_near(f):
        for c in range(3):
            rim_copy(f, 0, c).start()

    def send_far(f):
        for c in range(3):
            rim_copy(f, 1, c).start()

    def at_core(which, job):
        @pl.when(core == which)
        def _():
            job()

    send_near(1)
    load_field(0)
    coef[...] = jnp.zeros((8, 128), f32)
    small[0].wait()
    coef[0:4, 0:4] = smooth_in[...]
    at_core(0, lambda: (send_far(1), send_near(0), send_far(0)))
    coef_copies = [
        remote(coef, coef_in.at[0], coef_s.at[0], coef_r.at[0], (ev, after)),
        remote(coef, coef_in.at[1], coef_s.at[1], coef_r.at[1], (ev, before)),
    ]
    n_rounds = round_count(m_size, e_size)
    if n_rounds:
        greet(rounds.at[0])

    def next_round(n):
        if n < n_rounds:
            pl.semaphore_wait(rounds.at[n], near_count)
            if n + 1 < n_rounds:
                greet(rounds.at[n + 1])

    for load in small[1:]:
        load.wait()
    live = jnp.where(lane < count_in[0:1, 0:1], 1.0, 0.0).astype(f32)
    LIVE[...] = jnp.broadcast_to(live, (8, 128))
    for fc in range(6):
        F[fc, PAD : PAD + NODES, :] = F[fc, PAD : PAD + NODES, :] * live

    node = lax.broadcasted_iota(jnp.int32, (ROWS, 128), 0).astype(f32)
    i = jnp.floor((node + 0.5) / 25.0)
    rest = node - 25.0 * i
    j = jnp.floor((rest + 0.5) / 5.0)
    k = rest - 5.0 * j
    count = jnp.zeros((ROWS, 128), f32)
    for f, test in enumerate((i == 0.0, i == 4.0, j == 0.0, j == 4.0, k == 0.0, k == 4.0)):
        mask = jnp.where(test & (node < NODES - 0.5), 1.0, 0.0).astype(f32)
        W[f] = mask
        count = count + mask
    W[6] = count
    nb = nb_in[:, 0, :]
    target = lax.shift_right_logical(nb, 7)
    slot = nb & 127
    relative = lax.rem(target - me + m_size, m_size)
    for f in range(6):
        IDX[f] = jnp.broadcast_to(slot[f : f + 1], (8, 128))
        IDX[6 + f] = jnp.broadcast_to(relative[f : f + 1], (8, 128))
        far = jnp.where(relative[f : f + 1] == jnp.where(second == 1, 1, m_size - 1), 32, 0)
        RIM[f] = jnp.broadcast_to((slot[f : f + 1] & 31) + far, (8, 128))
    for c in range(3):
        U[c, 0:PAD, :] = zero8
        U[c, PAD + ROWS : ROWS + 2 * PAD, :] = zero8
    S[...] = jnp.zeros((ROWS, ROWS), f32)
    S[0:NODES, 0:NODES] = stiff_in[...]
    s_hi, s_lo = split(S[...])
    material = mat_in[...]

    def strain(base):
        wide = jnp.concatenate([F[base + c, PAD : PAD + ROWS, :] for c in range(3)], axis=1)
        hi, lo = split(wide)
        both = mm(s_hi, hi) + (mm(s_hi, lo) + mm(s_lo, hi))
        return [both[:, 128 * c : 128 * (c + 1)] for c in range(3)]

    def build_masks(which, here):
        for n, (f, t) in enumerate(FACE_TILES):
            M[which, n] = jnp.where(here(IDX[6 + f]), W[f, 8 * t : 8 * t + 8, :], 0.0)

    def face_sums(read, which):
        sums = [None] * (ROWS // 8)
        for n, (f, t) in enumerate(FACE_TILES):
            g = read(f, 8 * t + SHIFT[f]) * M[which, n]
            sums[t] = g if sums[t] is None else sums[t] + g
        return sums

    def own_pass(base):
        for c in range(3):
            sums = face_sums(lambda f, low: pick(F[base + c, low + PAD : low + 2 * PAD, :], IDX[f]), 0)
            for t in range(ROWS // 8):
                at = pl.ds(8 * t, 8)
                v = F[base + c, 8 * t + PAD : 8 * t + 2 * PAD, :]
                acc = sums[t] - W[6, at, :] * v
                N[base + c, at, :] = N[base + c, at, :] + (time_square * penalty) * acc

    def arrive(f, k):
        for c in range(3):
            rim_copy(f, k, c).wait_recv()
            if k == 0 and paired:

                @pl.when(core == 1)
                def _():
                    relay_copy(f, c).start()

    def unpack(f, k):
        side = sides[k]
        for c in range(3):
            for g in range(4):
                at = pl.ds(PAD + 32 * g, 32)
                turn = (32 * k - 32 * g) % 128
                part = rim[f, side, c]
                part = pltpu.roll(part, turn, 1) if turn else part
                U[c, at, :] = part if k == 0 else jnp.where(lane < 32, U[c, at, :], part)

    def rim_pass(base, store, after_each=None):
        for c in range(3):
            sums = face_sums(lambda face, low: pick(U[c, low + PAD : low + 2 * PAD, :], RIM[face]), 1)
            for t in range(ROWS // 8):
                old = N[base + c, 8 * t : 8 * t + 8, :]
                store(c, t, old + (time_square * penalty) * sums[t])
            if after_each is not None:
                after_each(c)

    def pack_next(c):
        send[2, c] = pack(c)

    build_masks(0, lambda relative: relative == 0)
    st_f = strain(0)
    st_a = strain(3)
    energy = jnp.zeros((ROWS, 128), f32)
    for c in range(3):
        vf = F[c, PAD : PAD + ROWS, :]
        energy = energy + vf * st_a[c]
        N[c] = vf - time_square * material * st_f[c]
        N[3 + c] = F[3 + c, PAD : PAD + ROWS, :] - time_square * material * st_a[c]
    K[...] = energy
    if not paired:
        at_core(1, lambda: (send_far(1), send_near(0), send_far(0)))
    else:
        at_core(1, lambda: send_near(0))
    own_pass(3)
    own_pass(0)
    next_round(0)
    build_masks(1, lambda relative: (relative == 1) | (relative == m_size - 1))

    def keep_adjoint(c, t, value):
        F[3 + c, 8 * t + PAD : 8 * t + 2 * PAD, :] = LIVE[...] * value

    def keep_forward(c, t, value):
        value = LIVE[...] * value
        at = pl.ds(8 * t + PAD, 8)
        line = pl.ds(8 * t, 8)
        N[c, line, :] = 2.0 * value - F[c, at, :]
        F[c, at, :] = value
        K[line, :] = K[line, :] + value * A[c, line, :]

    arrive(1, 0)
    unpack(1, 0)
    next_round(1)
    if paired:
        at_core(1, lambda: arrive(0, 0))
    arrive(1, 1)
    unpack(1, 1)
    rim_pass(3, keep_adjoint)
    for n in range(2, n_rounds):
        next_round(n)
    for c, value in enumerate(strain(3)):
        A[c] = value
    if paired:
        at_core(0, lambda: arrive(0, 0))
    else:
        arrive(0, 0)
    unpack(0, 0)
    arrive(0, 1)
    unpack(0, 1)
    rim_pass(0, keep_forward, pack_next)

    elements = F.shape[-1]
    width = smooth_in.shape[1]
    scale = math.sqrt(width / elements) / STEPS
    twin = jnp.concatenate([proj_in[...], proj_in[...]], axis=0)
    t_hi, t_lo = split(twin)
    k_hi, k_lo = split(K[0:NODES, :])
    blocks = (mm(t_hi, k_hi) + (mm(t_hi, k_lo) + mm(t_lo, k_hi))) * scale
    b_hi, b_lo = split(blocks)
    row = lax.broadcasted_iota(jnp.int32, (total * width, 128), 0)
    owner = lax.div(row, width)
    tile = width * (lax.rem(owner, e_size) * m_size + lax.div(owner, e_size)) + lax.rem(row, width)
    dest = dest_in[...]
    nt = ((1,), (1,))

    def spread(offset):
        hot = jnp.where(tile + offset == dest, 1.0, 0.0).astype(f32).astype(bf16)
        return mm(hot, b_hi, nt) + mm(hot, b_lo, nt)

    packed = jnp.where(lane < 64, spread(-2), spread(2))
    msg[...] = packed.reshape(m_size, e_size, width, 128)

    def peer(oe, om):
        return lax.rem(ev + oe, e_size), lax.rem(me + om, m_size)

    if direct:
        offsets = [(oe, om) for oe in list(range(1, e_size)) + [0] for om in range(m_size) if oe or om]
        for oe, om in offsets:
            e, m = peer(oe, om)
            remote(msg.at[m, e], got.at[oe * m_size + om - 1], a_s.at[0], a_r.at[0], (e, m))
    else:
        a_copies = [
            remote(msg.at[lax.rem(me + o, m_size)], got.at[pl.ds(e_size * (o - 1), e_size)],
                   a_s.at[o - 1], a_r.at[o - 1], (ev, lax.rem(me + o, m_size)))
            for o in range(1, m_size)
        ]

    send_near(2)
    if paired:
        at_core(0, lambda: send_far(2))
    else:
        send_far(2)

    st_f = strain(0)
    for c in range(3):
        N[c] = N[c] - time_square * material * st_f[c]
    own_pass(0)

    for copy in coef_copies:
        copy.wait_recv()
    coef_copies += [
        remote(coef_in.at[0], coef_in.at[2], coef_s.at[2], coef_r.at[2],
               (lax.rem(ev + 1, e_size), me)),
        remote(coef_in.at[1], coef_in.at[3], coef_s.at[3], coef_r.at[3],
               (lax.rem(ev + e_size - 1, e_size), me)),
    ]
    if not direct:
        for copy in a_copies:
            copy.wait_recv()
        mine_sum = msg[me]
        for o in range(m_size - 1):
            mine_sum = mine_sum + got[e_size * o : e_size * (o + 1)]
        part[...] = mine_sum
        b_copies = [
            remote(part.at[lax.rem(ev + o, e_size)], got2.at[o - 1], b_s.at[o - 1], b_r.at[o - 1],
                   (lax.rem(ev + o, e_size), me))
            for o in range(1, e_size)
        ]

    def final(c, t, value):
        fwd_out[c, 8 * t : 8 * t + 8, :] = LIVE[...] * value

    arrive(2, 0)
    unpack(2, 0)
    arrive(2, 1)
    unpack(2, 1)
    rim_pass(0, final)

    for copy in coef_copies[2:]:
        copy.wait_recv()
    own_coef = pltpu.roll(coef[...], 2, 1)
    left = jnp.where(lin > 0, jnp.where(me > 0, coef_in[0], coef_in[2]), 0.0)
    right = jnp.where(
        lin < total - 1, jnp.where(me < m_size - 1, coef_in[1], coef_in[3]), 0.0
    )
    left = jnp.where(lane < 2, pltpu.roll(left, 126, 1), 0.0)
    right = pltpu.roll(right, 6, 1)
    mine[...] = jnp.zeros((128, 128), f32)
    mine[0:8, :] = own_coef + left + right
    coefs = mine[...].T[0:8]

    def smooth(x):
        chain = pltpu.roll(x, 1, 0) + pltpu.roll(x, 7, 0) - 2.0 * x
        new = x + coefs[:, 0:1] * chain
        for d, shift in ((1, 4), (2, 2), (3, 0)):
            digit = lax.shift_right_logical(lane, shift) & 3
            up = jnp.where(digit == 0, 0.0, pltpu.roll(x, 1 << shift, 1))
            down = jnp.where(digit == 3, 0.0, pltpu.roll(x, 128 - (1 << shift), 1))
            new = new + coefs[:, d : d + 1] * (up + down - 2.0 * x)
        return jnp.where(lane < 64, new, 0.0)

    if direct:
        gathered = pltpu.make_async_remote_copy(
            src_ref=got, dst_ref=got, send_sem=a_s.at[0], recv_sem=a_r.at[0],
            device_id=peer(1, 0), device_id_type=MESH,
        )
        gathered.wait_recv()
        parts = [msg[me, ev]] + [got[n] for n in range(total - 1)]
    else:
        for copy in b_copies:
            copy.wait_recv()
        parts = [part[ev]] + [got2[o] for o in range(e_size - 1)]
    while len(parts) > 1:
        parts = [sum(parts[n : n + 2][1:], parts[n]) for n in range(0, len(parts), 2)]
    summed = parts[0]
    x = jnp.concatenate([summed, pltpu.roll(summed, 64, 1)], axis=0)
    x = smooth(smooth(jnp.where(lane < 64, x, 0.0)))
    tiles_out[...] = x[2 : 2 + width, 0:64]

    for f in range(3):
        for k in range(2):
            for c in range(3):
                rim_copy(f, k, c).wait_send()
    if direct:
        gathered.wait_send()
    else:
        for copy in a_copies + b_copies:
            copy.wait_send()
    for copy in coef_copies:
        copy.wait_send()


def write_out(final_vmem, tiles_vmem, final_hbm, tiles_hbm, sems):
    copies = [
        pltpu.make_async_copy(
            final_vmem.at[c, pl.ds(0, NODES)], final_hbm.at[pl.ds(NODES * c, NODES), 0], sems.at[c]
        )
        for c in range(3)
    ]
    copies.append(pltpu.make_async_copy(tiles_vmem, tiles_hbm, sems.at[3]))
    for copy in copies:
        copy.start()
    for copy in copies:
        copy.wait()


def solution(mesh):
    m_size, e_size = mesh.shape["mesh"], mesh.shape["event"]
    in_specs = (
        P("event", None, None, "mesh"),
        P("event", None, None, "mesh"),
        P(),
        P(),
        P("event", "mesh"),
        P("event", None, "mesh"),
        P("event", "mesh"),
        P("event", "mesh"),
        P(None, ("event", "mesh")),
    )
    out_specs = (P("event", None, None, "mesh"), P(None, ("event", "mesh")))

    def per_device(*args):
        fwd, smoothing = args[0], args[-1]
        width = smoothing.shape[1]
        dma = pltpu.SemaphoreType.DMA
        vmem = pl.BlockSpec(memory_space=pltpu.VMEM)
        hbm = pl.BlockSpec(memory_space=pltpu.HBM)
        line = (3 * NODES, 1, fwd.shape[-1])
        args = (args[0].reshape(line), args[1].reshape(line), args[2], args[3].T, args[4],
                args[5].reshape(6, 1, fwd.shape[-1]), *args[6:])
        if is_direct(m_size, e_size):
            a_count, b_count = 1, 1
            part, got, got2 = (1, width, 128), (m_size * e_size - 1, width, 128), (1, width, 128)
        else:
            a_count, b_count = m_size - 1, e_size - 1
            part, got, got2 = (e_size, width, 128), ((m_size - 1) * e_size, width, 128), (e_size - 1, width, 128)
        final, tiles = pl.pallas_call(
            functools.partial(kernel, m_size, e_size),
            out_shape=(
                pltpu.VMEM((3, ROWS, 128), f32),
                pltpu.VMEM((width, 64), f32),
            ),
            in_specs=[hbm] * len(args),
            out_specs=(vmem, vmem),
            scratch_shapes=[pltpu.VMEM(x.shape, x.dtype) for x in args[2:]]
            + [
                pltpu.VMEM((6, 144, 128), f32),
                pltpu.VMEM((6, ROWS, 128), f32),
                pltpu.VMEM((ROWS, 128), f32),
                pltpu.VMEM((3, ROWS, 128), f32),
                pltpu.VMEM((ROWS, ROWS), f32),
                pltpu.VMEM((7, ROWS, 128), f32),
                pltpu.VMEM((2, len(FACE_TILES), 8, 128), f32),
                pltpu.VMEM((12, 8, 128), jnp.int32),
                pltpu.VMEM((6, 8, 128), jnp.int32),
                pltpu.VMEM((8, 128), f32),
                pltpu.VMEM((3, 3, 32, 128), f32),
                pltpu.VMEM((3, 2, 3, 32, 128), f32),
                pltpu.VMEM((3, 144, 128), f32),
                pltpu.VMEM((8, 128), f32),
                pltpu.VMEM((4, 8, 128), f32),
                pltpu.VMEM((m_size, e_size, width, 128), f32),
                pltpu.VMEM((128, 128), f32),
                pltpu.VMEM(part, f32),
                pltpu.VMEM(got, f32),
                pltpu.VMEM(got2, f32),
                dma((6,)), dma((7,)), dma((3, 2, 3)), dma((3, 2, 3)), dma((4,)), dma((4,)),
                dma((a_count,)), dma((a_count,)), dma((b_count,)), dma((b_count,)),
                pltpu.SemaphoreType.REGULAR((max(round_count(m_size, e_size), 1),)),
            ],
            compiler_params=pltpu.CompilerParams(collective_id=0, has_side_effects=True),
        )(*args)
        final, tiles = pl.pallas_call(
            write_out,
            out_shape=(pltpu.HBM(line, f32), pltpu.HBM((width, 64), f32)),
            in_specs=[vmem, vmem],
            out_specs=(hbm, hbm),
            scratch_shapes=[dma((4,))],
        )(
            pltpu.with_memory_space_constraint(final, pltpu.VMEM),
            pltpu.with_memory_space_constraint(tiles, pltpu.VMEM),
        )
        return final.reshape(fwd.shape), tiles.T

    return jax.shard_map(
        per_device, mesh=mesh, in_specs=in_specs, out_specs=out_specs, check_vma=False
    )
```

```python
import functools
import math

import jax
import jax.numpy as jnp
from jax import lax
from jax.experimental import pallas as pl
from jax.experimental.pallas import tpu as pltpu
from jax.sharding import PartitionSpec as P

STEPS = 2
time_square = 0.4
penalty = 0.5

PAD = 8
ROWS = 128
NODES = 125
SHIFT = (100, -100, 20, -20, 4, -4)
MESH = pl.DeviceIdType.MESH
f32 = jnp.float32
bf16 = jnp.bfloat16


def on_face(face, node):
    i, j, k = node // 25, (node // 5) % 5, node % 5
    return (i == 0, i == 4, j == 0, j == 4, k == 0, k == 4)[face]


RIM_NODES = [n for n in range(NODES) if any(on_face(f, n) for f in range(6))]
RIM_PLACE = {n: at for at, n in enumerate(RIM_NODES)}
RIM_ROWS = -(-len(RIM_NODES) // 4)
FACE_TILES = [
    (f, t)
    for f in range(6)
    for t in range(ROWS // 8)
    if any(on_face(f, n) for n in range(8 * t, min(8 * t + 8, NODES)))
]


def split(x):
    high = x.astype(bf16)
    return high, (x - high.astype(f32)).astype(bf16)


def mm(a, b, dims=((1,), (0,))):
    return lax.dot_general(a, b, (dims, ((), ())), preferred_element_type=f32)


def pick(x, index):
    dims = lax.GatherDimensionNumbers(
        offset_dims=(), collapsed_slice_dims=(1,), start_index_map=(1,),
        operand_batching_dims=(0,), start_indices_batching_dims=(0,),
    )
    return lax.gather(x, index[:, :, None], dims, (1, 1), mode=lax.GatherScatterMode.PROMISE_IN_BOUNDS)


def gather_rows(load, places):
    pieces = {}
    for r, place in enumerate(places):
        if place is not None:
            pieces.setdefault(place - r, []).append(r)
    sublane = lax.broadcasted_iota(jnp.int32, (8, 128), 0)
    value = None
    for shift, members in pieces.items():
        piece = load(shift)
        if value is None:
            value = piece
        else:
            value = jnp.where((sublane >= members[0]) & (sublane <= members[-1]), piece, value)
    return load(0) if value is None else value


def is_direct(m_size, e_size):
    return m_size * e_size <= 64


def round_count(m_size, e_size):
    return max(e_size // 2 - 1, 1) if is_direct(m_size, e_size) else max(e_size // 2 - 2, 0)


def kernel(
    m_size, e_size,
    fwd_in, adj_in, stiff_hbm, proj_hbm, mat_hbm, nb_hbm, dest_hbm, count_hbm, smooth_hbm,
    fwd_out, tiles_out,
    stiff_in, proj_in, mat_in, nb_in, dest_in, count_in, smooth_in,
    F, N, K, A, S, W, M, IDX, RIM, LIVE, send, rim, U, coef, coef_in, msg, mine, part, got, got2,
    in_s, small_s, rim_s, rim_r, coef_s, coef_r, a_s, a_r, b_s, b_r, rounds,
):
    me = lax.axis_index("mesh")
    ev = lax.axis_index("event")
    total = m_size * e_size
    direct = is_direct(m_size, e_size)
    lin = ev * m_size + me
    after = lax.rem(me + 1, m_size)
    before = lax.rem(me + m_size - 1, m_size)

    barrier = pltpu.get_barrier_semaphore()
    core = lax.rem(ev, 2)
    chip = lax.div(ev, 2)
    chips = e_size // 2
    near = [((2 * chip + 1 - core, me), None)]
    for step in (1, -1):
        inside = (chip + step >= 0) & (chip + step < chips)
        near += [((2 * (chip + step) + c, me), inside) for c in range(2)]
    near_count = 1 + 2 * ((chip > 0).astype(jnp.int32) + (chip < chips - 1).astype(jnp.int32))

    def greet(sem):
        for device, inside in near:
            if inside is None:
                pl.semaphore_signal(sem, inc=1, device_id=device, device_id_type=MESH)
            else:

                @pl.when(inside)
                def _():
                    pl.semaphore_signal(sem, inc=1, device_id=device, device_id_type=MESH)

    for o in range(1, m_size):
        pl.semaphore_signal(
            barrier, inc=1, device_id=(ev, lax.rem(me + o, m_size)), device_id_type=MESH
        )
    greet(barrier)

    loads = {}
    for fc in (3, 4, 5, 0, 1, 2):
        source = fwd_in if fc < 3 else adj_in
        load = pltpu.make_async_copy(
            source.at[pl.ds(NODES * (fc % 3), NODES), 0], F.at[fc, pl.ds(PAD, NODES)], in_s.at[fc]
        )
        load.start()
        loads[fc] = load

    small = []
    for n, (src, dst) in enumerate((
        (smooth_hbm, smooth_in), (stiff_hbm, stiff_in), (nb_hbm, nb_in), (count_hbm, count_in),
        (mat_hbm, mat_in), (proj_hbm, proj_in), (dest_hbm, dest_in),
    )):
        load = pltpu.make_async_copy(src, dst, small_s.at[n])
        load.start()
        small.append(load)

    lane = lax.broadcasted_iota(jnp.int32, (1, 128), 1)
    zero8 = jnp.zeros((PAD, 128), f32)
    for fc in range(6):
        F[fc, 0:PAD, :] = zero8
        F[fc, PAD + NODES : 144, :] = jnp.zeros((144 - PAD - NODES, 128), f32)

    def pack(f, c, fc):
        for v in range(-(-RIM_ROWS // 8)):
            parts = []
            for g in range(4):
                inside = range(RIM_ROWS * g + 8 * v, min(RIM_ROWS * (g + 1), RIM_ROWS * g + 8 * v + 8))
                places = [RIM_NODES[n] if n < len(RIM_NODES) else None for n in inside]
                part = gather_rows(lambda low: F[fc, low + PAD : low + 2 * PAD, :], places)
                parts.append(pltpu.roll(part, 32 * g, 1) if g else part)
            send[f, c, 8 * v : 8 * v + 8, :] = jnp.where(
                lane < 64, jnp.where(lane < 32, parts[0], parts[1]),
                jnp.where(lane < 96, parts[2], parts[3]),
            )

    def load_field(f, then=None):
        for c in range(3):
            loads[3 * f + c].wait()
            pack(f, c, 3 * f + c)
            if then is not None:
                then(c)


    def remote(src, dst, s, r, device):
        copy = pltpu.make_async_remote_copy(
            src_ref=src, dst_ref=dst, send_sem=s, recv_sem=r, device_id=device, device_id_type=MESH
        )
        copy.start()
        return copy

    paired = m_size == 4
    first = 1 - lax.rem(me, 2) if paired else 0
    second = 1 - first
    sides = (first, second)
    used = pl.ds(0, RIM_ROWS)

    def rim_copy(f, k, c):
        slot = sides[1 - k] if paired else sides[k]
        return pltpu.make_async_remote_copy(
            src_ref=send.at[f, c, used], dst_ref=rim.at[f, slot, c, used],
            send_sem=rim_s.at[f, k, c], recv_sem=rim_r.at[f, k, c],
            device_id=(ev, jnp.where(slot == 0, after, before)), device_id_type=MESH,
        )

    def relay_copy(f, c):
        return pltpu.make_async_remote_copy(
            src_ref=rim.at[f, first, c, used], dst_ref=rim.at[f, second, c, used],
            send_sem=rim_s.at[f, 1, c], recv_sem=rim_r.at[f, 1, c],
            device_id=(ev, lax.rem(me + 2, m_size)), device_id_type=MESH,
        )

    def send_near(f):
        for c in range(3):
            rim_copy(f, 0, c).start()

    def send_far(f):
        for c in range(3):
            rim_copy(f, 1, c).start()

    def at_core(which, job):
        @pl.when(core == which)
        def _():
            job()

    def near_of(c):
        if c == 0:
            pl.semaphore_wait(barrier, near_count + (m_size - 1))
        rim_copy(1, 0, c).start()

    load_field(1, near_of)
    load_field(0)
    coef[...] = jnp.zeros((8, 128), f32)
    small[0].wait()
    coef[0:4, 0:4] = smooth_in[...]
    at_core(0, lambda: (send_far(1), send_near(0), send_far(0)))
    coef_copies = [
        remote(coef, coef_in.at[0], coef_s.at[0], coef_r.at[0], (ev, after)),
        remote(coef, coef_in.at[1], coef_s.at[1], coef_r.at[1], (ev, before)),
    ]
    n_rounds = round_count(m_size, e_size)
    if n_rounds:
        greet(rounds.at[0])

    def next_round(n):
        if n < n_rounds:
            pl.semaphore_wait(rounds.at[n], near_count)
            if n + 1 < n_rounds:
                greet(rounds.at[n + 1])

    for load in small[1:]:
        load.wait()
    live = jnp.where(lane < count_in[0:1, 0:1], 1.0, 0.0).astype(f32)
    LIVE[...] = jnp.broadcast_to(live, (8, 128))
    for fc in range(6):
        F[fc, PAD : PAD + NODES, :] = F[fc, PAD : PAD + NODES, :] * live

    node = lax.broadcasted_iota(jnp.int32, (ROWS, 128), 0).astype(f32)
    i = jnp.floor((node + 0.5) / 25.0)
    rest = node - 25.0 * i
    j = jnp.floor((rest + 0.5) / 5.0)
    k = rest - 5.0 * j
    count = jnp.zeros((ROWS, 128), f32)
    for f, test in enumerate((i == 0.0, i == 4.0, j == 0.0, j == 4.0, k == 0.0, k == 4.0)):
        mask = jnp.where(test & (node < NODES - 0.5), 1.0, 0.0).astype(f32)
        W[f] = mask
        count = count + mask
    W[6] = count
    nb = nb_in[:, 0, :]
    target = lax.shift_right_logical(nb, 7)
    slot = nb & 127
    relative = lax.rem(target - me + m_size, m_size)
    for f in range(6):
        IDX[f] = jnp.broadcast_to(slot[f : f + 1], (8, 128))
        IDX[6 + f] = jnp.broadcast_to(relative[f : f + 1], (8, 128))
        far = jnp.where(relative[f : f + 1] == jnp.where(second == 1, 1, m_size - 1), 32, 0)
        RIM[f] = jnp.broadcast_to((slot[f : f + 1] & 31) + far, (8, 128))
    for c in range(3):
        U[c, 0:PAD, :] = zero8
        U[c, PAD + 4 * RIM_ROWS :, :] = jnp.zeros((U.shape[1] - PAD - 4 * RIM_ROWS, 128), f32)
    S[...] = jnp.zeros((ROWS, ROWS), f32)
    S[0:NODES, 0:NODES] = stiff_in[...]
    s_hi, s_lo = split(S[...])
    material = mat_in[...]

    def strain(base):
        wide = jnp.concatenate([F[base + c, PAD : PAD + ROWS, :] for c in range(3)], axis=1)
        hi, lo = split(wide)
        both = mm(s_hi, hi) + (mm(s_hi, lo) + mm(s_lo, hi))
        return [both[:, 128 * c : 128 * (c + 1)] for c in range(3)]

    def build_masks(which, here):
        for n, (f, t) in enumerate(FACE_TILES):
            M[which, n] = jnp.where(here(IDX[6 + f]), W[f, 8 * t : 8 * t + 8, :], 0.0)

    def face_sums(read, which):
        sums = [None] * (ROWS // 8)
        for n, (f, t) in enumerate(FACE_TILES):
            g = read(f, t) * M[which, n]
            sums[t] = g if sums[t] is None else sums[t] + g
        return sums

    def own_pass(base):
        for c in range(3):
            def read(f, t):
                at = 8 * t + SHIFT[f] + PAD
                return pick(F[base + c, at : at + 8, :], IDX[f])

            sums = face_sums(read, 0)
            for t in range(ROWS // 8):
                at = pl.ds(8 * t, 8)
                v = F[base + c, 8 * t + PAD : 8 * t + 2 * PAD, :]
                acc = sums[t] - W[6, at, :] * v
                N[base + c, at, :] = N[base + c, at, :] + (time_square * penalty) * acc

    def arrive(f, k):
        for c in range(3):
            rim_copy(f, k, c).wait_recv()
            if k == 0 and paired:

                @pl.when(core == 1)
                def _():
                    relay_copy(f, c).start()

    def unpack(f, k):
        side = sides[k]
        for c in range(3):
            for g in range(4):
                at = pl.ds(PAD + RIM_ROWS * g, RIM_ROWS)
                turn = (32 * k - 32 * g) % 128
                part = rim[f, side, c, 0:RIM_ROWS, :]
                part = pltpu.roll(part, turn, 1) if turn else part
                U[c, at, :] = part if k == 0 else jnp.where(lane < 32, U[c, at, :], part)

    def rim_pass(base, store):
        for c in range(3):

            def read(f, t):
                places = [
                    RIM_PLACE[8 * t + r + SHIFT[f]] if 8 * t + r < NODES and on_face(f, 8 * t + r) else None
                    for r in range(8)
                ]
                rows = gather_rows(lambda low: U[c, low + PAD : low + 2 * PAD, :], places)
                return pick(rows, RIM[f])

            sums = face_sums(read, 1)
            for t in range(ROWS // 8):
                old = N[base + c, 8 * t : 8 * t + 8, :]
                store(c, t, old + (time_square * penalty) * sums[t])

    build_masks(0, lambda relative: relative == 0)
    st_f = strain(0)
    st_a = strain(3)
    energy = jnp.zeros((ROWS, 128), f32)
    for c in range(3):
        vf = F[c, PAD : PAD + ROWS, :]
        energy = energy + vf * st_a[c]
        N[c] = vf - time_square * material * st_f[c]
        N[3 + c] = F[3 + c, PAD : PAD + ROWS, :] - time_square * material * st_a[c]
    K[...] = energy
    if not paired:
        at_core(1, lambda: (send_far(1), send_near(0), send_far(0)))
    else:
        at_core(1, lambda: send_near(0))
    own_pass(3)
    own_pass(0)
    next_round(0)
    build_masks(1, lambda relative: (relative == 1) | (relative == m_size - 1))

    def keep_adjoint(c, t, value):
        F[3 + c, 8 * t + PAD : 8 * t + 2 * PAD, :] = LIVE[...] * value

    def keep_forward(c, t, value):
        value = LIVE[...] * value
        at = pl.ds(8 * t + PAD, 8)
        line = pl.ds(8 * t, 8)
        N[c, line, :] = 2.0 * value - F[c, at, :]
        F[c, at, :] = value
        K[line, :] = K[line, :] + value * A[c, line, :]

    arrive(1, 0)
    unpack(1, 0)
    next_round(1)
    if paired:
        at_core(1, lambda: arrive(0, 0))
    arrive(1, 1)
    unpack(1, 1)
    rim_pass(3, keep_adjoint)
    for n in range(2, n_rounds):
        next_round(n)
    for c, value in enumerate(strain(3)):
        A[c] = value
    if paired:
        at_core(0, lambda: arrive(0, 0))
    else:
        arrive(0, 0)
    unpack(0, 0)
    arrive(0, 1)
    unpack(0, 1)
    rim_pass(0, keep_forward)

    elements = F.shape[-1]
    width = smooth_in.shape[1]
    scale = math.sqrt(width / elements) / STEPS
    twin = jnp.concatenate([proj_in[...], proj_in[...]], axis=0)
    t_hi, t_lo = split(twin)
    k_hi, k_lo = split(K[0:NODES, :])
    blocks = (mm(t_hi, k_hi) + (mm(t_hi, k_lo) + mm(t_lo, k_hi))) * scale
    b_hi, b_lo = split(blocks)
    row = lax.broadcasted_iota(jnp.int32, (total * width, 128), 0)
    owner = lax.div(row, width)
    tile = width * (lax.rem(owner, e_size) * m_size + lax.div(owner, e_size)) + lax.rem(row, width)
    dest = dest_in[...]
    nt = ((1,), (1,))

    def spread(offset):
        hot = jnp.where(tile + offset == dest, 1.0, 0.0).astype(f32).astype(bf16)
        return mm(hot, b_hi, nt) + mm(hot, b_lo, nt)

    packed = jnp.where(lane < 64, spread(-2), spread(2))
    msg[...] = packed.reshape(m_size, e_size, width, 128)

    def peer(oe, om):
        return lax.rem(ev + oe, e_size), lax.rem(me + om, m_size)

    if direct:
        offsets = [(oe, om) for oe in list(range(1, e_size)) + [0] for om in range(m_size) if oe or om]
        for oe, om in offsets:
            e, m = peer(oe, om)
            remote(msg.at[m, e], got.at[oe * m_size + om - 1], a_s.at[0], a_r.at[0], (e, m))
    else:
        a_copies = [
            remote(msg.at[lax.rem(me + o, m_size)], got.at[pl.ds(e_size * (o - 1), e_size)],
                   a_s.at[o - 1], a_r.at[o - 1], (ev, lax.rem(me + o, m_size)))
            for o in range(1, m_size)
        ]

    for c in range(3):
        pack(2, c, c)
    send_near(2)
    if paired:
        at_core(0, lambda: send_far(2))
    else:
        send_far(2)

    st_f = strain(0)
    for c in range(3):
        N[c] = N[c] - time_square * material * st_f[c]
    own_pass(0)

    for copy in coef_copies:
        copy.wait_recv()
    coef_copies += [
        remote(coef_in.at[0], coef_in.at[2], coef_s.at[2], coef_r.at[2],
               (lax.rem(ev + 1, e_size), me)),
        remote(coef_in.at[1], coef_in.at[3], coef_s.at[3], coef_r.at[3],
               (lax.rem(ev + e_size - 1, e_size), me)),
    ]
    if not direct:
        for copy in a_copies:
            copy.wait_recv()
        mine_sum = msg[me]
        for o in range(m_size - 1):
            mine_sum = mine_sum + got[e_size * o : e_size * (o + 1)]
        part[...] = mine_sum
        b_copies = [
            remote(part.at[lax.rem(ev + o, e_size)], got2.at[o - 1], b_s.at[o - 1], b_r.at[o - 1],
                   (lax.rem(ev + o, e_size), me))
            for o in range(1, e_size)
        ]

    def final(c, t, value):
        fwd_out[c, 8 * t : 8 * t + 8, :] = LIVE[...] * value

    arrive(2, 0)
    unpack(2, 0)
    arrive(2, 1)
    unpack(2, 1)
    rim_pass(0, final)

    for copy in coef_copies[2:]:
        copy.wait_recv()
    own_coef = pltpu.roll(coef[...], 2, 1)
    left = jnp.where(lin > 0, jnp.where(me > 0, coef_in[0], coef_in[2]), 0.0)
    right = jnp.where(
        lin < total - 1, jnp.where(me < m_size - 1, coef_in[1], coef_in[3]), 0.0
    )
    left = jnp.where(lane < 2, pltpu.roll(left, 126, 1), 0.0)
    right = pltpu.roll(right, 6, 1)
    mine[...] = jnp.zeros((128, 128), f32)
    mine[0:8, :] = own_coef + left + right
    coefs = mine[...].T[0:8]

    def smooth(x):
        chain = pltpu.roll(x, 1, 0) + pltpu.roll(x, 7, 0) - 2.0 * x
        new = x + coefs[:, 0:1] * chain
        for d, shift in ((1, 4), (2, 2), (3, 0)):
            digit = lax.shift_right_logical(lane, shift) & 3
            up = jnp.where(digit == 0, 0.0, pltpu.roll(x, 1 << shift, 1))
            down = jnp.where(digit == 3, 0.0, pltpu.roll(x, 128 - (1 << shift), 1))
            new = new + coefs[:, d : d + 1] * (up + down - 2.0 * x)
        return jnp.where(lane < 64, new, 0.0)

    if direct:
        gathered = pltpu.make_async_remote_copy(
            src_ref=got, dst_ref=got, send_sem=a_s.at[0], recv_sem=a_r.at[0],
            device_id=peer(1, 0), device_id_type=MESH,
        )
        gathered.wait_recv()
        parts = [msg[me, ev]] + [got[n] for n in range(total - 1)]
    else:
        for copy in b_copies:
            copy.wait_recv()
        parts = [part[ev]] + [got2[o] for o in range(e_size - 1)]
    while len(parts) > 1:
        parts = [sum(parts[n : n + 2][1:], parts[n]) for n in range(0, len(parts), 2)]
    summed = parts[0]
    x = jnp.concatenate([summed, pltpu.roll(summed, 64, 1)], axis=0)
    x = smooth(smooth(jnp.where(lane < 64, x, 0.0)))
    tiles_out[...] = x[2 : 2 + width, 0:64]

    for f in range(3):
        for k in range(2):
            for c in range(3):
                rim_copy(f, k, c).wait_send()
    if direct:
        gathered.wait_send()
    else:
        for copy in a_copies + b_copies:
            copy.wait_send()
    for copy in coef_copies:
        copy.wait_send()


def write_out(final_vmem, tiles_vmem, final_hbm, tiles_hbm, sems):
    copies = [
        pltpu.make_async_copy(
            final_vmem.at[c, pl.ds(0, NODES)], final_hbm.at[pl.ds(NODES * c, NODES), 0], sems.at[c]
        )
        for c in range(3)
    ]
    copies.append(pltpu.make_async_copy(tiles_vmem, tiles_hbm, sems.at[3]))
    for copy in copies:
        copy.start()
    for copy in copies:
        copy.wait()


def solution(mesh):
    m_size, e_size = mesh.shape["mesh"], mesh.shape["event"]
    in_specs = (
        P("event", None, None, "mesh"),
        P("event", None, None, "mesh"),
        P(),
        P(),
        P("event", "mesh"),
        P("event", None, "mesh"),
        P("event", "mesh"),
        P("event", "mesh"),
        P(None, ("event", "mesh")),
    )
    out_specs = (P("event", None, None, "mesh"), P(None, ("event", "mesh")))

    def per_device(*args):
        fwd, smoothing = args[0], args[-1]
        width = smoothing.shape[1]
        dma = pltpu.SemaphoreType.DMA
        vmem = pl.BlockSpec(memory_space=pltpu.VMEM)
        hbm = pl.BlockSpec(memory_space=pltpu.HBM)
        line = (3 * NODES, 1, fwd.shape[-1])
        args = (args[0].reshape(line), args[1].reshape(line), args[2], args[3].T, args[4],
                args[5].reshape(6, 1, fwd.shape[-1]), *args[6:])
        if is_direct(m_size, e_size):
            a_count, b_count = 1, 1
            part, got, got2 = (1, width, 128), (m_size * e_size - 1, width, 128), (1, width, 128)
        else:
            a_count, b_count = m_size - 1, e_size - 1
            part, got, got2 = (e_size, width, 128), ((m_size - 1) * e_size, width, 128), (e_size - 1, width, 128)
        final, tiles = pl.pallas_call(
            functools.partial(kernel, m_size, e_size),
            out_shape=(
                pltpu.VMEM((3, ROWS, 128), f32),
                pltpu.VMEM((width, 64), f32),
            ),
            in_specs=[hbm] * len(args),
            out_specs=(vmem, vmem),
            scratch_shapes=[pltpu.VMEM(x.shape, x.dtype) for x in args[2:]]
            + [
                pltpu.VMEM((6, 144, 128), f32),
                pltpu.VMEM((6, ROWS, 128), f32),
                pltpu.VMEM((ROWS, 128), f32),
                pltpu.VMEM((3, ROWS, 128), f32),
                pltpu.VMEM((ROWS, ROWS), f32),
                pltpu.VMEM((7, ROWS, 128), f32),
                pltpu.VMEM((2, len(FACE_TILES), 8, 128), f32),
                pltpu.VMEM((12, 8, 128), jnp.int32),
                pltpu.VMEM((6, 8, 128), jnp.int32),
                pltpu.VMEM((8, 128), f32),
                pltpu.VMEM((3, 3, 32, 128), f32),
                pltpu.VMEM((3, 2, 3, 32, 128), f32),
                pltpu.VMEM((3, 120, 128), f32),
                pltpu.VMEM((8, 128), f32),
                pltpu.VMEM((4, 8, 128), f32),
                pltpu.VMEM((m_size, e_size, width, 128), f32),
                pltpu.VMEM((128, 128), f32),
                pltpu.VMEM(part, f32),
                pltpu.VMEM(got, f32),
                pltpu.VMEM(got2, f32),
                dma((6,)), dma((7,)), dma((3, 2, 3)), dma((3, 2, 3)), dma((4,)), dma((4,)),
                dma((a_count,)), dma((a_count,)), dma((b_count,)), dma((b_count,)),
                pltpu.SemaphoreType.REGULAR((max(round_count(m_size, e_size), 1),)),
            ],
            compiler_params=pltpu.CompilerParams(collective_id=0, has_side_effects=True),
        )(*args)
        final, tiles = pl.pallas_call(
            write_out,
            out_shape=(pltpu.HBM(line, f32), pltpu.HBM((width, 64), f32)),
            in_specs=[vmem, vmem],
            out_specs=(hbm, hbm),
            scratch_shapes=[dma((4,))],
        )(
            pltpu.with_memory_space_constraint(final, pltpu.VMEM),
            pltpu.with_memory_space_constraint(tiles, pltpu.VMEM),
        )
        return final.reshape(fwd.shape), tiles.T

    return jax.shard_map(
        per_device, mesh=mesh, in_specs=in_specs, out_specs=out_specs, check_vma=False
    )
```

```python
import functools
import math

import jax
import jax.numpy as jnp
from jax import lax
from jax.experimental import pallas as pl
from jax.experimental.pallas import tpu as pltpu
from jax.sharding import PartitionSpec as P

STEPS = 2
time_square = 0.4
penalty = 0.5

PAD = 8
ROWS = 128
NODES = 125
SHIFT = (100, -100, 20, -20, 4, -4)
RELAYED = (0,)
MESH = pl.DeviceIdType.MESH
f32 = jnp.float32
bf16 = jnp.bfloat16


def on_face(face, node):
    i, j, k = node // 25, (node // 5) % 5, node % 5
    return (i == 0, i == 4, j == 0, j == 4, k == 0, k == 4)[face]


RIM_NODES = [n for n in range(NODES) if any(on_face(f, n) for f in range(6))]
RIM_PLACE = {n: at for at, n in enumerate(RIM_NODES)}
RIM_ROWS = -(-len(RIM_NODES) // 4)
FACE_TILES = [
    (f, t)
    for f in range(6)
    for t in range(ROWS // 8)
    if any(on_face(f, n) for n in range(8 * t, min(8 * t + 8, NODES)))
]


def split(x):
    high = x.astype(bf16)
    return high, (x - high.astype(f32)).astype(bf16)


def mm(a, b, dims=((1,), (0,))):
    return lax.dot_general(a, b, (dims, ((), ())), preferred_element_type=f32)


def pick(x, index):
    dims = lax.GatherDimensionNumbers(
        offset_dims=(), collapsed_slice_dims=(1,), start_index_map=(1,),
        operand_batching_dims=(0,), start_indices_batching_dims=(0,),
    )
    return lax.gather(x, index[:, :, None], dims, (1, 1), mode=lax.GatherScatterMode.PROMISE_IN_BOUNDS)


def gather_rows(load, places):
    pieces = {}
    for r, place in enumerate(places):
        if place is not None:
            pieces.setdefault(place - r, []).append(r)
    sublane = lax.broadcasted_iota(jnp.int32, (8, 128), 0)
    value = None
    for shift, members in pieces.items():
        piece = load(shift)
        if value is None:
            value = piece
        else:
            value = jnp.where((sublane >= members[0]) & (sublane <= members[-1]), piece, value)
    return load(0) if value is None else value


def is_direct(m_size, e_size):
    return m_size * e_size <= 64


def round_count(m_size, e_size):
    return max(e_size // 2 - 1, 1) if is_direct(m_size, e_size) else max(e_size // 2 - 2, 0)


def kernel(
    m_size, e_size,
    fwd_in, adj_in, stiff_hbm, proj_hbm, mat_hbm, nb_hbm, dest_hbm, count_hbm, smooth_hbm,
    fwd_out, tiles_out,
    stiff_in, proj_in, mat_in, nb_in, dest_in, count_in, smooth_in,
    F, N, K, A, S, W, M, IDX, RIM, LIVE, send, rim, U, coef, coef_in, msg, mine, part, got, got2,
    in_s, small_s, rim_s, rim_r, coef_s, coef_r, a_s, a_r, b_s, b_r, rounds,
):
    me = lax.axis_index("mesh")
    ev = lax.axis_index("event")
    total = m_size * e_size
    direct = is_direct(m_size, e_size)
    lin = ev * m_size + me
    after = lax.rem(me + 1, m_size)
    before = lax.rem(me + m_size - 1, m_size)

    barrier = pltpu.get_barrier_semaphore()
    core = lax.rem(ev, 2)
    chip = lax.div(ev, 2)
    chips = e_size // 2
    near = [((2 * chip + 1 - core, me), None)]
    for step in (1, -1):
        inside = (chip + step >= 0) & (chip + step < chips)
        near += [((2 * (chip + step) + c, me), inside) for c in range(2)]
    near_count = 1 + 2 * ((chip > 0).astype(jnp.int32) + (chip < chips - 1).astype(jnp.int32))

    def greet(sem):
        for device, inside in near:
            if inside is None:
                pl.semaphore_signal(sem, inc=1, device_id=device, device_id_type=MESH)
            else:

                @pl.when(inside)
                def _():
                    pl.semaphore_signal(sem, inc=1, device_id=device, device_id_type=MESH)

    for o in range(1, m_size):
        pl.semaphore_signal(
            barrier, inc=1, device_id=(ev, lax.rem(me + o, m_size)), device_id_type=MESH
        )
    greet(barrier)

    loads = {}
    for fc in (3, 4, 5, 0, 1, 2):
        source = fwd_in if fc < 3 else adj_in
        load = pltpu.make_async_copy(
            source.at[pl.ds(NODES * (fc % 3), NODES), 0], F.at[fc, pl.ds(PAD, NODES)], in_s.at[fc]
        )
        load.start()
        loads[fc] = load

    small = []
    for n, (src, dst) in enumerate((
        (smooth_hbm, smooth_in), (stiff_hbm, stiff_in), (nb_hbm, nb_in), (count_hbm, count_in),
        (mat_hbm, mat_in), (proj_hbm, proj_in), (dest_hbm, dest_in),
    )):
        load = pltpu.make_async_copy(src, dst, small_s.at[n])
        load.start()
        small.append(load)

    lane = lax.broadcasted_iota(jnp.int32, (1, 128), 1)
    zero8 = jnp.zeros((PAD, 128), f32)
    for fc in range(6):
        F[fc, 0:PAD, :] = zero8
        F[fc, PAD + NODES : 144, :] = jnp.zeros((144 - PAD - NODES, 128), f32)

    def pack(f, c, fc):
        for v in range(-(-RIM_ROWS // 8)):
            parts = []
            for g in range(4):
                inside = range(RIM_ROWS * g + 8 * v, min(RIM_ROWS * (g + 1), RIM_ROWS * g + 8 * v + 8))
                places = [RIM_NODES[n] if n < len(RIM_NODES) else None for n in inside]
                part = gather_rows(lambda low: F[fc, low + PAD : low + 2 * PAD, :], places)
                parts.append(pltpu.roll(part, 32 * g, 1) if g else part)
            send[f, c, 8 * v : 8 * v + 8, :] = jnp.where(
                lane < 64, jnp.where(lane < 32, parts[0], parts[1]),
                jnp.where(lane < 96, parts[2], parts[3]),
            )

    def load_field(f, then=None):
        for c in range(3):
            loads[3 * f + c].wait()
            pack(f, c, 3 * f + c)
            if then is not None:
                then(c)


    def remote(src, dst, s, r, device):
        copy = pltpu.make_async_remote_copy(
            src_ref=src, dst_ref=dst, send_sem=s, recv_sem=r, device_id=device, device_id_type=MESH
        )
        copy.start()
        return copy

    paired = m_size == 4
    first = 1 - lax.rem(me, 2) if paired else 0
    second = 1 - first
    sides = (first, second)
    used = pl.ds(0, RIM_ROWS)

    def rim_copy(f, k, c):
        slot = sides[1 - k] if paired else sides[k]
        return pltpu.make_async_remote_copy(
            src_ref=send.at[f, c, used], dst_ref=rim.at[f, slot, c, used],
            send_sem=rim_s.at[f, k, c], recv_sem=rim_r.at[f, k, c],
            device_id=(ev, jnp.where(slot == 0, after, before)), device_id_type=MESH,
        )

    def relay_copy(f, c):
        return pltpu.make_async_remote_copy(
            src_ref=rim.at[f, first, c, used], dst_ref=rim.at[f, second, c, used],
            send_sem=rim_s.at[f, 1, c], recv_sem=rim_r.at[f, 1, c],
            device_id=(ev, lax.rem(me + 2, m_size)), device_id_type=MESH,
        )

    def send_near(f):
        for c in range(3):
            rim_copy(f, 0, c).start()

    def send_far(f):
        for c in range(3):
            rim_copy(f, 1, c).start()

    def at_core(which, job):
        @pl.when(core == which)
        def _():
            job()

    def far_of(c):
        if c == 0:
            pl.semaphore_wait(barrier, near_count + (m_size - 1))
        rim_copy(1, 1, c).start()

    load_field(1, far_of)
    send_near(1)
    load_field(0)
    coef[...] = jnp.zeros((8, 128), f32)
    small[0].wait()
    coef[0:4, 0:4] = smooth_in[...]
    at_core(0, lambda: (send_far(0), send_near(0)))
    coef_copies = [
        remote(coef, coef_in.at[0], coef_s.at[0], coef_r.at[0], (ev, after)),
        remote(coef, coef_in.at[1], coef_s.at[1], coef_r.at[1], (ev, before)),
    ]
    n_rounds = round_count(m_size, e_size)
    if n_rounds:
        greet(rounds.at[0])

    def next_round(n):
        if n < n_rounds:
            pl.semaphore_wait(rounds.at[n], near_count)
            if n + 1 < n_rounds:
                greet(rounds.at[n + 1])

    for load in small[1:]:
        load.wait()
    live = jnp.where(lane < count_in[0:1, 0:1], 1.0, 0.0).astype(f32)
    LIVE[...] = jnp.broadcast_to(live, (8, 128))
    for fc in range(6):
        F[fc, PAD : PAD + NODES, :] = F[fc, PAD : PAD + NODES, :] * live

    node = lax.broadcasted_iota(jnp.int32, (ROWS, 128), 0).astype(f32)
    i = jnp.floor((node + 0.5) / 25.0)
    rest = node - 25.0 * i
    j = jnp.floor((rest + 0.5) / 5.0)
    k = rest - 5.0 * j
    count = jnp.zeros((ROWS, 128), f32)
    for f, test in enumerate((i == 0.0, i == 4.0, j == 0.0, j == 4.0, k == 0.0, k == 4.0)):
        mask = jnp.where(test & (node < NODES - 0.5), 1.0, 0.0).astype(f32)
        W[f] = mask
        count = count + mask
    W[6] = count
    nb = nb_in[:, 0, :]
    target = lax.shift_right_logical(nb, 7)
    slot = nb & 127
    relative = lax.rem(target - me + m_size, m_size)
    for f in range(6):
        IDX[f] = jnp.broadcast_to(slot[f : f + 1], (8, 128))
        IDX[6 + f] = jnp.broadcast_to(relative[f : f + 1], (8, 128))
        far = jnp.where(relative[f : f + 1] == jnp.where(second == 1, 1, m_size - 1), 32, 0)
        RIM[f] = jnp.broadcast_to((slot[f : f + 1] & 31) + far, (8, 128))
    for c in range(3):
        U[c, 0:PAD, :] = zero8
        U[c, PAD + 4 * RIM_ROWS :, :] = jnp.zeros((U.shape[1] - PAD - 4 * RIM_ROWS, 128), f32)
    S[...] = jnp.zeros((ROWS, ROWS), f32)
    S[0:NODES, 0:NODES] = stiff_in[...]
    s_hi, s_lo = split(S[...])
    material = mat_in[...]

    def strain(base):
        wide = jnp.concatenate([F[base + c, PAD : PAD + ROWS, :] for c in range(3)], axis=1)
        hi, lo = split(wide)
        both = mm(s_hi, hi) + (mm(s_hi, lo) + mm(s_lo, hi))
        return [both[:, 128 * c : 128 * (c + 1)] for c in range(3)]

    def build_masks(which, here):
        for n, (f, t) in enumerate(FACE_TILES):
            M[which, n] = jnp.where(here(IDX[6 + f]), W[f, 8 * t : 8 * t + 8, :], 0.0)

    def face_sums(read, which):
        sums = [None] * (ROWS // 8)
        for n, (f, t) in enumerate(FACE_TILES):
            g = read(f, t) * M[which, n]
            sums[t] = g if sums[t] is None else sums[t] + g
        return sums

    def own_pass(base):
        for c in range(3):
            def read(f, t):
                at = 8 * t + SHIFT[f] + PAD
                return pick(F[base + c, at : at + 8, :], IDX[f])

            sums = face_sums(read, 0)
            for t in range(ROWS // 8):
                at = pl.ds(8 * t, 8)
                v = F[base + c, 8 * t + PAD : 8 * t + 2 * PAD, :]
                acc = sums[t] - W[6, at, :] * v
                N[base + c, at, :] = N[base + c, at, :] + (time_square * penalty) * acc

    def arrive(f, k):
        for c in range(3):
            rim_copy(f, k, c).wait_recv()
            if k == 0 and paired and f in RELAYED:

                @pl.when(core == 1)
                def _():
                    relay_copy(f, c).start()

    def unpack(f, k):
        side = sides[k]
        for c in range(3):
            for g in range(4):
                at = pl.ds(PAD + RIM_ROWS * g, RIM_ROWS)
                turn = (32 * k - 32 * g) % 128
                part = rim[f, side, c, 0:RIM_ROWS, :]
                part = pltpu.roll(part, turn, 1) if turn else part
                U[c, at, :] = part if k == 0 else jnp.where(lane < 32, U[c, at, :], part)

    def rim_pass(base, store):
        for c in range(3):

            def read(f, t):
                places = [
                    RIM_PLACE[8 * t + r + SHIFT[f]] if 8 * t + r < NODES and on_face(f, 8 * t + r) else None
                    for r in range(8)
                ]
                rows = gather_rows(lambda low: U[c, low + PAD : low + 2 * PAD, :], places)
                return pick(rows, RIM[f])

            sums = face_sums(read, 1)
            for t in range(ROWS // 8):
                old = N[base + c, 8 * t : 8 * t + 8, :]
                store(c, t, old + (time_square * penalty) * sums[t])

    if paired:
        at_core(1, lambda: send_near(0))
    build_masks(0, lambda relative: relative == 0)
    st_f = strain(0)
    st_a = strain(3)
    energy = jnp.zeros((ROWS, 128), f32)
    for c in range(3):
        vf = F[c, PAD : PAD + ROWS, :]
        energy = energy + vf * st_a[c]
        N[c] = vf - time_square * material * st_f[c]
        N[3 + c] = F[3 + c, PAD : PAD + ROWS, :] - time_square * material * st_a[c]
    K[...] = energy
    if not paired:
        at_core(1, lambda: (send_near(0), send_far(0)))
    else:
        pass
    own_pass(3)
    own_pass(0)
    next_round(0)
    build_masks(1, lambda relative: (relative == 1) | (relative == m_size - 1))

    def keep_adjoint(c, t, value):
        F[3 + c, 8 * t + PAD : 8 * t + 2 * PAD, :] = LIVE[...] * value

    def keep_forward(c, t, value):
        value = LIVE[...] * value
        at = pl.ds(8 * t + PAD, 8)
        line = pl.ds(8 * t, 8)
        N[c, line, :] = 2.0 * value - F[c, at, :]
        F[c, at, :] = value
        K[line, :] = K[line, :] + value * A[c, line, :]

    arrive(1, 0)
    unpack(1, 0)
    next_round(1)
    if paired and 0 in RELAYED:
        at_core(1, lambda: arrive(0, 0))
    arrive(1, 1)
    unpack(1, 1)
    rim_pass(3, keep_adjoint)
    for n in range(2, n_rounds):
        next_round(n)
    for c, value in enumerate(strain(3)):
        A[c] = value
    if paired and 0 in RELAYED:
        at_core(0, lambda: arrive(0, 0))
    else:
        arrive(0, 0)
    unpack(0, 0)
    arrive(0, 1)
    unpack(0, 1)
    rim_pass(0, keep_forward)

    def send_second():
        for c in range(3):
            pack(2, c, c)
        if paired and 2 in RELAYED:
            at_core(0, lambda: send_far(2))
        else:
            send_far(2)
        send_near(2)

    ahead = chip < chips // 2
    pl.when(ahead)(send_second)
    elements = F.shape[-1]
    width = smooth_in.shape[1]
    scale = math.sqrt(width / elements) / STEPS
    twin = jnp.concatenate([proj_in[...], proj_in[...]], axis=0)
    t_hi, t_lo = split(twin)
    k_hi, k_lo = split(K[0:NODES, :])
    blocks = (mm(t_hi, k_hi) + (mm(t_hi, k_lo) + mm(t_lo, k_hi))) * scale
    b_hi, b_lo = split(blocks)
    row = lax.broadcasted_iota(jnp.int32, (total * width, 128), 0)
    owner = lax.div(row, width)
    tile = width * (lax.rem(owner, e_size) * m_size + lax.div(owner, e_size)) + lax.rem(row, width)
    dest = dest_in[...]
    nt = ((1,), (1,))

    def spread(offset):
        hot = jnp.where(tile + offset == dest, 1.0, 0.0).astype(f32).astype(bf16)
        return mm(hot, b_hi, nt) + mm(hot, b_lo, nt)

    packed = jnp.where(lane < 64, spread(-2), spread(2))
    msg[...] = packed.reshape(m_size, e_size, width, 128)

    def peer(oe, om):
        return lax.rem(ev + oe, e_size), lax.rem(me + om, m_size)

    if direct:
        offsets = [(oe, om) for oe in list(range(1, e_size)) + [0] for om in range(m_size) if oe or om]
        for oe, om in offsets:
            e, m = peer(oe, om)
            remote(msg.at[m, e], got.at[oe * m_size + om - 1], a_s.at[0], a_r.at[0], (e, m))
    else:
        a_copies = [
            remote(msg.at[lax.rem(me + o, m_size)], got.at[pl.ds(e_size * (o - 1), e_size)],
                   a_s.at[o - 1], a_r.at[o - 1], (ev, lax.rem(me + o, m_size)))
            for o in range(1, m_size)
        ]

    pl.when(jnp.logical_not(ahead))(send_second)

    st_f = strain(0)
    for c in range(3):
        N[c] = N[c] - time_square * material * st_f[c]
    own_pass(0)

    for copy in coef_copies:
        copy.wait_recv()
    coef_copies += [
        remote(coef_in.at[0], coef_in.at[2], coef_s.at[2], coef_r.at[2],
               (lax.rem(ev + 1, e_size), me)),
        remote(coef_in.at[1], coef_in.at[3], coef_s.at[3], coef_r.at[3],
               (lax.rem(ev + e_size - 1, e_size), me)),
    ]
    if not direct:
        for copy in a_copies:
            copy.wait_recv()
        mine_sum = msg[me]
        for o in range(m_size - 1):
            mine_sum = mine_sum + got[e_size * o : e_size * (o + 1)]
        part[...] = mine_sum
        b_copies = [
            remote(part.at[lax.rem(ev + o, e_size)], got2.at[o - 1], b_s.at[o - 1], b_r.at[o - 1],
                   (lax.rem(ev + o, e_size), me))
            for o in range(1, e_size)
        ]

    def final(c, t, value):
        fwd_out[c, 8 * t : 8 * t + 8, :] = LIVE[...] * value

    arrive(2, 0)
    unpack(2, 0)
    arrive(2, 1)
    unpack(2, 1)
    rim_pass(0, final)

    for copy in coef_copies[2:]:
        copy.wait_recv()
    own_coef = pltpu.roll(coef[...], 2, 1)
    left = jnp.where(lin > 0, jnp.where(me > 0, coef_in[0], coef_in[2]), 0.0)
    right = jnp.where(
        lin < total - 1, jnp.where(me < m_size - 1, coef_in[1], coef_in[3]), 0.0
    )
    left = jnp.where(lane < 2, pltpu.roll(left, 126, 1), 0.0)
    right = pltpu.roll(right, 6, 1)
    mine[...] = jnp.zeros((128, 128), f32)
    mine[0:8, :] = own_coef + left + right
    coefs = mine[...].T[0:8]

    def smooth(x):
        chain = pltpu.roll(x, 1, 0) + pltpu.roll(x, 7, 0) - 2.0 * x
        new = x + coefs[:, 0:1] * chain
        for d, shift in ((1, 4), (2, 2), (3, 0)):
            digit = lax.shift_right_logical(lane, shift) & 3
            up = jnp.where(digit == 0, 0.0, pltpu.roll(x, 1 << shift, 1))
            down = jnp.where(digit == 3, 0.0, pltpu.roll(x, 128 - (1 << shift), 1))
            new = new + coefs[:, d : d + 1] * (up + down - 2.0 * x)
        return jnp.where(lane < 64, new, 0.0)

    if direct:
        gathered = pltpu.make_async_remote_copy(
            src_ref=got, dst_ref=got, send_sem=a_s.at[0], recv_sem=a_r.at[0],
            device_id=peer(1, 0), device_id_type=MESH,
        )
        gathered.wait_recv()
        parts = [msg[me, ev]] + [got[n] for n in range(total - 1)]
    else:
        for copy in b_copies:
            copy.wait_recv()
        parts = [part[ev]] + [got2[o] for o in range(e_size - 1)]
    while len(parts) > 1:
        parts = [sum(parts[n : n + 2][1:], parts[n]) for n in range(0, len(parts), 2)]
    summed = parts[0]
    x = jnp.concatenate([summed, pltpu.roll(summed, 64, 1)], axis=0)
    x = smooth(smooth(jnp.where(lane < 64, x, 0.0)))
    tiles_out[...] = x[2 : 2 + width, 0:64]

    for f in range(3):
        for k in range(2):
            for c in range(3):
                rim_copy(f, k, c).wait_send()
    if direct:
        gathered.wait_send()
    else:
        for copy in a_copies + b_copies:
            copy.wait_send()
    for copy in coef_copies:
        copy.wait_send()


def write_out(final_vmem, tiles_vmem, final_hbm, tiles_hbm, sems):
    copies = [
        pltpu.make_async_copy(
            final_vmem.at[c, pl.ds(0, NODES)], final_hbm.at[pl.ds(NODES * c, NODES), 0], sems.at[c]
        )
        for c in range(3)
    ]
    copies.append(pltpu.make_async_copy(tiles_vmem, tiles_hbm, sems.at[3]))
    for copy in copies:
        copy.start()
    for copy in copies:
        copy.wait()


def solution(mesh):
    m_size, e_size = mesh.shape["mesh"], mesh.shape["event"]
    in_specs = (
        P("event", None, None, "mesh"),
        P("event", None, None, "mesh"),
        P(),
        P(),
        P("event", "mesh"),
        P("event", None, "mesh"),
        P("event", "mesh"),
        P("event", "mesh"),
        P(None, ("event", "mesh")),
    )
    out_specs = (P("event", None, None, "mesh"), P(None, ("event", "mesh")))

    def per_device(*args):
        fwd, smoothing = args[0], args[-1]
        width = smoothing.shape[1]
        dma = pltpu.SemaphoreType.DMA
        vmem = pl.BlockSpec(memory_space=pltpu.VMEM)
        hbm = pl.BlockSpec(memory_space=pltpu.HBM)
        line = (3 * NODES, 1, fwd.shape[-1])
        args = (args[0].reshape(line), args[1].reshape(line), args[2], args[3].T, args[4],
                args[5].reshape(6, 1, fwd.shape[-1]), *args[6:])
        if is_direct(m_size, e_size):
            a_count, b_count = 1, 1
            part, got, got2 = (1, width, 128), (m_size * e_size - 1, width, 128), (1, width, 128)
        else:
            a_count, b_count = m_size - 1, e_size - 1
            part, got, got2 = (e_size, width, 128), ((m_size - 1) * e_size, width, 128), (e_size - 1, width, 128)
        final, tiles = pl.pallas_call(
            functools.partial(kernel, m_size, e_size),
            out_shape=(
                pltpu.VMEM((3, ROWS, 128), f32),
                pltpu.VMEM((width, 64), f32),
            ),
            in_specs=[hbm] * len(args),
            out_specs=(vmem, vmem),
            scratch_shapes=[pltpu.VMEM(x.shape, x.dtype) for x in args[2:]]
            + [
                pltpu.VMEM((6, 144, 128), f32),
                pltpu.VMEM((6, ROWS, 128), f32),
                pltpu.VMEM((ROWS, 128), f32),
                pltpu.VMEM((3, ROWS, 128), f32),
                pltpu.VMEM((ROWS, ROWS), f32),
                pltpu.VMEM((7, ROWS, 128), f32),
                pltpu.VMEM((2, len(FACE_TILES), 8, 128), f32),
                pltpu.VMEM((12, 8, 128), jnp.int32),
                pltpu.VMEM((6, 8, 128), jnp.int32),
                pltpu.VMEM((8, 128), f32),
                pltpu.VMEM((3, 3, 32, 128), f32),
                pltpu.VMEM((3, 2, 3, 32, 128), f32),
                pltpu.VMEM((3, 120, 128), f32),
                pltpu.VMEM((8, 128), f32),
                pltpu.VMEM((4, 8, 128), f32),
                pltpu.VMEM((m_size, e_size, width, 128), f32),
                pltpu.VMEM((128, 128), f32),
                pltpu.VMEM(part, f32),
                pltpu.VMEM(got, f32),
                pltpu.VMEM(got2, f32),
                dma((6,)), dma((7,)), dma((3, 2, 3)), dma((3, 2, 3)), dma((4,)), dma((4,)),
                dma((a_count,)), dma((a_count,)), dma((b_count,)), dma((b_count,)),
                pltpu.SemaphoreType.REGULAR((max(round_count(m_size, e_size), 1),)),
            ],
            compiler_params=pltpu.CompilerParams(collective_id=0, has_side_effects=True),
        )(*args)
        final, tiles = pl.pallas_call(
            write_out,
            out_shape=(pltpu.HBM(line, f32), pltpu.HBM((width, 64), f32)),
            in_specs=[vmem, vmem],
            out_specs=(hbm, hbm),
            scratch_shapes=[dma((4,))],
        )(
            pltpu.with_memory_space_constraint(final, pltpu.VMEM),
            pltpu.with_memory_space_constraint(tiles, pltpu.VMEM),
        )
        return final.reshape(fwd.shape), tiles.T

    return jax.shard_map(
        per_device, mesh=mesh, in_specs=in_specs, out_specs=out_specs, check_vma=False
    )
```

```python
import functools
import math

import jax
import jax.numpy as jnp
from jax import lax
from jax.experimental import pallas as pl
from jax.experimental.pallas import tpu as pltpu
from jax.sharding import PartitionSpec as P

STEPS = 2
time_square = 0.4
penalty = 0.5

PAD = 8
ROWS = 128
NODES = 125
SHIFT = (100, -100, 20, -20, 4, -4)
RELAYED = (0,)
MESH = pl.DeviceIdType.MESH
f32 = jnp.float32
bf16 = jnp.bfloat16


def on_face(face, node):
    i, j, k = node // 25, (node // 5) % 5, node % 5
    return (i == 0, i == 4, j == 0, j == 4, k == 0, k == 4)[face]


RIM_NODES = [n for n in range(NODES) if any(on_face(f, n) for f in range(6))]
RIM_PLACE = {n: at for at, n in enumerate(RIM_NODES)}
RIM_ROWS = -(-len(RIM_NODES) // 4)
FACE_TILES = [
    (f, t)
    for f in range(6)
    for t in range(ROWS // 8)
    if any(on_face(f, n) for n in range(8 * t, min(8 * t + 8, NODES)))
]


def split(x):
    high = x.astype(bf16)
    return high, (x - high.astype(f32)).astype(bf16)


def mm(a, b, dims=((1,), (0,))):
    return lax.dot_general(a, b, (dims, ((), ())), preferred_element_type=f32)


def pick(x, index):
    dims = lax.GatherDimensionNumbers(
        offset_dims=(), collapsed_slice_dims=(1,), start_index_map=(1,),
        operand_batching_dims=(0,), start_indices_batching_dims=(0,),
    )
    return lax.gather(x, index[:, :, None], dims, (1, 1), mode=lax.GatherScatterMode.PROMISE_IN_BOUNDS)


def gather_rows(load, places):
    pieces = {}
    for r, place in enumerate(places):
        if place is not None:
            pieces.setdefault(place - r, []).append(r)
    sublane = lax.broadcasted_iota(jnp.int32, (8, 128), 0)
    value = None
    for shift, members in pieces.items():
        piece = load(shift)
        if value is None:
            value = piece
        else:
            value = jnp.where((sublane >= members[0]) & (sublane <= members[-1]), piece, value)
    return load(0) if value is None else value


def is_direct(m_size, e_size):
    return m_size * e_size <= 64


def kernel(
    m_size, e_size,
    fwd_in, adj_in, stiff_hbm, proj_hbm, mat_hbm, nb_hbm, dest_hbm, count_hbm, smooth_hbm,
    fwd_out, tiles_out,
    stiff_in, proj_in, mat_in, nb_in, dest_in, count_in, smooth_in,
    F, N, K, A, S, W, M, IDX, RIM, LIVE, send, rim, U, coef, coef_in, msg, mine, part, got, got2,
    in_s, small_s, rim_s, rim_r, coef_s, coef_r, a_s, a_r, b_s, b_r, rounds,
):
    me = lax.axis_index("mesh")
    ev = lax.axis_index("event")
    total = m_size * e_size
    direct = is_direct(m_size, e_size)
    lin = ev * m_size + me
    after = lax.rem(me + 1, m_size)
    before = lax.rem(me + m_size - 1, m_size)

    barrier = pltpu.get_barrier_semaphore()
    core = lax.rem(ev, 2)
    chip = lax.div(ev, 2)
    chips = e_size // 2
    near = [((2 * chip + 1 - core, me), None)]
    for step in (1, -1):
        inside = (chip + step >= 0) & (chip + step < chips)
        near += [((2 * (chip + step) + c, me), inside) for c in range(2)]
    near_count = 1 + 2 * ((chip > 0).astype(jnp.int32) + (chip < chips - 1).astype(jnp.int32))

    def greet(sem, devices):
        for device, inside in devices:
            if inside is None:
                pl.semaphore_signal(sem, inc=1, device_id=device, device_id_type=MESH)
            else:

                @pl.when(inside)
                def _():
                    pl.semaphore_signal(sem, inc=1, device_id=device, device_id_type=MESH)

    for o in range(1, m_size):
        pl.semaphore_signal(
            barrier, inc=1, device_id=(ev, lax.rem(me + o, m_size)), device_id_type=MESH
        )
    greet(barrier, near)

    loads = {}
    for fc in (3, 4, 5, 0, 1, 2):
        source = fwd_in if fc < 3 else adj_in
        load = pltpu.make_async_copy(
            source.at[pl.ds(NODES * (fc % 3), NODES), 0], F.at[fc, pl.ds(PAD, NODES)], in_s.at[fc]
        )
        load.start()
        loads[fc] = load

    small = []
    for n, (src, dst) in enumerate((
        (smooth_hbm, smooth_in), (stiff_hbm, stiff_in), (nb_hbm, nb_in), (count_hbm, count_in),
        (mat_hbm, mat_in), (proj_hbm, proj_in), (dest_hbm, dest_in),
    )):
        load = pltpu.make_async_copy(src, dst, small_s.at[n])
        load.start()
        small.append(load)

    lane = lax.broadcasted_iota(jnp.int32, (1, 128), 1)
    zero8 = jnp.zeros((PAD, 128), f32)
    for fc in range(6):
        F[fc, 0:PAD, :] = zero8
        F[fc, PAD + NODES : 144, :] = jnp.zeros((144 - PAD - NODES, 128), f32)

    def pack(f, c, fc):
        for v in range(-(-RIM_ROWS // 8)):
            parts = []
            for g in range(4):
                inside = range(RIM_ROWS * g + 8 * v, min(RIM_ROWS * (g + 1), RIM_ROWS * g + 8 * v + 8))
                places = [RIM_NODES[n] if n < len(RIM_NODES) else None for n in inside]
                part = gather_rows(lambda low: F[fc, low + PAD : low + 2 * PAD, :], places)
                parts.append(pltpu.roll(part, 32 * g, 1) if g else part)
            send[f, c, 8 * v : 8 * v + 8, :] = jnp.where(
                lane < 64, jnp.where(lane < 32, parts[0], parts[1]),
                jnp.where(lane < 96, parts[2], parts[3]),
            )

    def load_field(f, then=None):
        for c in range(3):
            loads[3 * f + c].wait()
            pack(f, c, 3 * f + c)
            if then is not None:
                then(c)


    def remote(src, dst, s, r, device):
        copy = pltpu.make_async_remote_copy(
            src_ref=src, dst_ref=dst, send_sem=s, recv_sem=r, device_id=device, device_id_type=MESH
        )
        copy.start()
        return copy

    paired = m_size == 4
    first = 1 - lax.rem(me, 2) if paired else 0
    second = 1 - first
    sides = (first, second)
    used = pl.ds(0, RIM_ROWS)

    def rim_copy(f, k, c):
        slot = sides[1 - k] if paired else sides[k]
        return pltpu.make_async_remote_copy(
            src_ref=send.at[f, c, used], dst_ref=rim.at[f, slot, c, used],
            send_sem=rim_s.at[f, k, c], recv_sem=rim_r.at[f, k, c],
            device_id=(ev, jnp.where(slot == 0, after, before)), device_id_type=MESH,
        )

    def relay_copy(f, c):
        return pltpu.make_async_remote_copy(
            src_ref=rim.at[f, first, c, used], dst_ref=rim.at[f, second, c, used],
            send_sem=rim_s.at[f, 1, c], recv_sem=rim_r.at[f, 1, c],
            device_id=(ev, lax.rem(me + 2, m_size)), device_id_type=MESH,
        )

    def send_near(f):
        for c in range(3):
            rim_copy(f, 0, c).start()

    def send_far(f):
        for c in range(3):
            rim_copy(f, 1, c).start()

    def at_core(which, job):
        @pl.when(core == which)
        def _():
            job()

    def far_of(c):
        if c == 0:
            pl.semaphore_wait(barrier, near_count + (m_size - 1))
        rim_copy(1, 1, c).start()

    load_field(1, far_of)
    send_near(1)
    load_field(0)
    coef[...] = jnp.zeros((8, 128), f32)

    @pl.when(ev == 0)
    def _():
        coef_in[2] = jnp.zeros((8, 128), f32)

    @pl.when(ev == e_size - 1)
    def _():
        coef_in[3] = jnp.zeros((8, 128), f32)

    small[0].wait()
    coef[0:4, 0:4] = smooth_in[...]
    at_core(0, lambda: (send_far(0), send_near(0)))
    coef_copies = [
        remote(coef, coef_in.at[0], coef_s.at[0], coef_r.at[0], (ev, after)),
        remote(coef, coef_in.at[1], coef_s.at[1], coef_r.at[1], (ev, before)),
    ]
    beside, above, below = near[:1], near[1:3], near[3:]
    is_first, is_last = chip == 0, chip == chips - 1

    def wait_up():
        pl.semaphore_wait(rounds.at[0], 2)
        greet(rounds.at[0], above)

    def wait_down():
        pl.semaphore_wait(rounds.at[1], 2)
        greet(rounds.at[1], below)

    greet(rounds.at[2], beside)
    pl.when(is_first)(lambda: greet(rounds.at[0], above))
    pl.when(is_last)(lambda: greet(rounds.at[1], below))
    between = jnp.logical_not(is_first | is_last)
    turns = between & (chip == chips - 2)

    for load in small[1:]:
        load.wait()
    live = jnp.where(lane < count_in[0:1, 0:1], 1.0, 0.0).astype(f32)
    LIVE[...] = jnp.broadcast_to(live, (8, 128))
    for fc in range(6):
        F[fc, PAD : PAD + NODES, :] = F[fc, PAD : PAD + NODES, :] * live

    node = lax.broadcasted_iota(jnp.int32, (ROWS, 128), 0).astype(f32)
    i = jnp.floor((node + 0.5) / 25.0)
    rest = node - 25.0 * i
    j = jnp.floor((rest + 0.5) / 5.0)
    k = rest - 5.0 * j
    count = jnp.zeros((ROWS, 128), f32)
    for f, test in enumerate((i == 0.0, i == 4.0, j == 0.0, j == 4.0, k == 0.0, k == 4.0)):
        mask = jnp.where(test & (node < NODES - 0.5), 1.0, 0.0).astype(f32)
        W[f] = mask
        count = count + mask
    W[6] = count
    nb = nb_in[:, 0, :]
    target = lax.shift_right_logical(nb, 7)
    slot = nb & 127
    relative = lax.rem(target - me + m_size, m_size)
    for f in range(6):
        IDX[f] = jnp.broadcast_to(slot[f : f + 1], (8, 128))
        IDX[6 + f] = jnp.broadcast_to(relative[f : f + 1], (8, 128))
        far = jnp.where(relative[f : f + 1] == jnp.where(second == 1, 1, m_size - 1), 32, 0)
        RIM[f] = jnp.broadcast_to((slot[f : f + 1] & 31) + far, (8, 128))
    for c in range(3):
        U[c, 0:PAD, :] = zero8
        U[c, PAD + 4 * RIM_ROWS :, :] = jnp.zeros((U.shape[1] - PAD - 4 * RIM_ROWS, 128), f32)
    S[...] = jnp.zeros((ROWS, ROWS), f32)
    S[0:NODES, 0:NODES] = stiff_in[...]
    s_hi, s_lo = split(S[...])
    material = mat_in[...]

    def strain(base):
        wide = jnp.concatenate([F[base + c, PAD : PAD + ROWS, :] for c in range(3)], axis=1)
        hi, lo = split(wide)
        both = mm(s_hi, hi) + (mm(s_hi, lo) + mm(s_lo, hi))
        return [both[:, 128 * c : 128 * (c + 1)] for c in range(3)]

    def build_masks(which, here):
        for n, (f, t) in enumerate(FACE_TILES):
            M[which, n] = jnp.where(here(IDX[6 + f]), W[f, 8 * t : 8 * t + 8, :], 0.0)

    def face_sums(read, which):
        sums = [None] * (ROWS // 8)
        for n, (f, t) in enumerate(FACE_TILES):
            g = read(f, t) * M[which, n]
            sums[t] = g if sums[t] is None else sums[t] + g
        return sums

    def own_pass(base):
        for c in range(3):
            def read(f, t):
                at = 8 * t + SHIFT[f] + PAD
                return pick(F[base + c, at : at + 8, :], IDX[f])

            sums = face_sums(read, 0)
            for t in range(ROWS // 8):
                at = pl.ds(8 * t, 8)
                v = F[base + c, 8 * t + PAD : 8 * t + 2 * PAD, :]
                acc = sums[t] - W[6, at, :] * v
                N[base + c, at, :] = N[base + c, at, :] + (time_square * penalty) * acc

    def arrive(f, k):
        for c in range(3):
            rim_copy(f, k, c).wait_recv()
            if k == 0 and paired and f in RELAYED:

                @pl.when(core == 1)
                def _():
                    relay_copy(f, c).start()

    def unpack(f, k):
        side = sides[k]
        for c in range(3):
            for g in range(4):
                at = pl.ds(PAD + RIM_ROWS * g, RIM_ROWS)
                turn = (32 * k - 32 * g) % 128
                part = rim[f, side, c, 0:RIM_ROWS, :]
                part = pltpu.roll(part, turn, 1) if turn else part
                U[c, at, :] = part if k == 0 else jnp.where(lane < 32, U[c, at, :], part)

    def rim_pass(base, store):
        for c in range(3):

            def read(f, t):
                places = [
                    RIM_PLACE[8 * t + r + SHIFT[f]] if 8 * t + r < NODES and on_face(f, 8 * t + r) else None
                    for r in range(8)
                ]
                rows = gather_rows(lambda low: U[c, low + PAD : low + 2 * PAD, :], places)
                return pick(rows, RIM[f])

            sums = face_sums(read, 1)
            for t in range(ROWS // 8):
                old = N[base + c, 8 * t : 8 * t + 8, :]
                store(c, t, old + (time_square * penalty) * sums[t])

    if paired:
        at_core(1, lambda: send_near(0))
    build_masks(0, lambda relative: relative == 0)
    st_f = strain(0)
    st_a = strain(3)
    energy = jnp.zeros((ROWS, 128), f32)
    for c in range(3):
        vf = F[c, PAD : PAD + ROWS, :]
        energy = energy + vf * st_a[c]
        N[c] = vf - time_square * material * st_f[c]
        N[3 + c] = F[3 + c, PAD : PAD + ROWS, :] - time_square * material * st_a[c]
    K[...] = energy
    if not paired:
        at_core(1, lambda: (send_near(0), send_far(0)))
    else:
        pass
    own_pass(3)
    own_pass(0)
    pl.when(between)(wait_up)
    build_masks(1, lambda relative: (relative == 1) | (relative == m_size - 1))

    def keep_adjoint(c, t, value):
        F[3 + c, 8 * t + PAD : 8 * t + 2 * PAD, :] = LIVE[...] * value

    def keep_forward(c, t, value):
        value = LIVE[...] * value
        at = pl.ds(8 * t + PAD, 8)
        line = pl.ds(8 * t, 8)
        N[c, line, :] = 2.0 * value - F[c, at, :]
        F[c, at, :] = value
        K[line, :] = K[line, :] + value * A[c, line, :]

    arrive(1, 0)
    unpack(1, 0)
    pl.when(turns)(wait_down)
    if paired and 0 in RELAYED:
        at_core(1, lambda: arrive(0, 0))
    arrive(1, 1)
    unpack(1, 1)
    rim_pass(3, keep_adjoint)
    pl.when(between & jnp.logical_not(turns))(wait_down)
    for c, value in enumerate(strain(3)):
        A[c] = value
    if paired and 0 in RELAYED:
        at_core(0, lambda: arrive(0, 0))
    else:
        arrive(0, 0)
    unpack(0, 0)
    arrive(0, 1)
    unpack(0, 1)
    rim_pass(0, keep_forward)

    def send_second():
        for c in range(3):
            pack(2, c, c)
        if paired and 2 in RELAYED:
            at_core(0, lambda: send_far(2))
        else:
            send_far(2)
        send_near(2)

    ahead = chip < chips // 2
    pl.when(ahead)(send_second)
    elements = F.shape[-1]
    width = smooth_in.shape[1]
    scale = math.sqrt(width / elements) / STEPS
    twin = jnp.concatenate([proj_in[...], proj_in[...]], axis=0)
    t_hi, t_lo = split(twin)
    k_hi, k_lo = split(K[0:NODES, :])
    blocks = (mm(t_hi, k_hi) + (mm(t_hi, k_lo) + mm(t_lo, k_hi))) * scale
    b_hi, b_lo = split(blocks)
    row = lax.broadcasted_iota(jnp.int32, (total * width, 128), 0)
    owner = lax.div(row, width)
    tile = width * (lax.rem(owner, e_size) * m_size + lax.div(owner, e_size)) + lax.rem(row, width)
    dest = dest_in[...]
    nt = ((1,), (1,))

    def spread(offset):
        hot = jnp.where(tile + offset == dest, 1.0, 0.0).astype(f32).astype(bf16)
        return mm(hot, b_hi, nt) + mm(hot, b_lo, nt)

    packed = jnp.where(lane < 64, spread(-2), spread(2))
    msg[...] = packed.reshape(m_size, e_size, width, 128)

    pl.semaphore_wait(rounds.at[2], 1)
    if chips > 1:
        pl.when(is_last)(wait_up)
        pl.when(is_first)(wait_down)

    def peer(oe, om):
        return lax.rem(ev + oe, e_size), lax.rem(me + om, m_size)

    if direct:
        offsets = [(oe, om) for oe in list(range(1, e_size)) + [0] for om in range(m_size) if oe or om]
        for oe, om in offsets:
            e, m = peer(oe, om)
            remote(msg.at[m, e], got.at[oe * m_size + om - 1], a_s.at[0], a_r.at[0], (e, m))
    else:
        a_copies = [
            remote(msg.at[lax.rem(me + o, m_size)], got.at[pl.ds(e_size * (o - 1), e_size)],
                   a_s.at[o - 1], a_r.at[o - 1], (ev, lax.rem(me + o, m_size)))
            for o in range(1, m_size)
        ]

    pl.when(jnp.logical_not(ahead))(send_second)

    st_f = strain(0)
    for c in range(3):
        N[c] = N[c] - time_square * material * st_f[c]
    own_pass(0)

    for copy in coef_copies:
        copy.wait_recv()
    has_next, has_last = ev < e_size - 1, ev > 0

    def chain_copy(n, step):
        return pltpu.make_async_remote_copy(
            src_ref=coef_in.at[n], dst_ref=coef_in.at[2 + n], send_sem=coef_s.at[2 + n],
            recv_sem=coef_r.at[2 + n], device_id=(lax.rem(ev + step + e_size, e_size), me),
            device_id_type=MESH,
        )

    to_next, to_last = chain_copy(0, 1), chain_copy(1, -1)
    pl.when(has_next)(lambda: to_next.start())
    pl.when(has_last)(lambda: to_last.start())
    if not direct:
        for copy in a_copies:
            copy.wait_recv()
        mine_sum = msg[me]
        for o in range(m_size - 1):
            mine_sum = mine_sum + got[e_size * o : e_size * (o + 1)]
        part[...] = mine_sum
        b_copies = [
            remote(part.at[lax.rem(ev + o, e_size)], got2.at[o - 1], b_s.at[o - 1], b_r.at[o - 1],
                   (lax.rem(ev + o, e_size), me))
            for o in range(1, e_size)
        ]

    def final(c, t, value):
        fwd_out[c, 8 * t : 8 * t + 8, :] = LIVE[...] * value

    arrive(2, 0)
    unpack(2, 0)
    arrive(2, 1)
    unpack(2, 1)
    rim_pass(0, final)

    pl.when(has_last)(lambda: to_next.wait_recv())
    pl.when(has_next)(lambda: to_last.wait_recv())
    own_coef = pltpu.roll(coef[...], 2, 1)
    left = jnp.where(lin > 0, jnp.where(me > 0, coef_in[0], coef_in[2]), 0.0)
    right = jnp.where(
        lin < total - 1, jnp.where(me < m_size - 1, coef_in[1], coef_in[3]), 0.0
    )
    left = jnp.where(lane < 2, pltpu.roll(left, 126, 1), 0.0)
    right = pltpu.roll(right, 6, 1)
    mine[...] = jnp.zeros((128, 128), f32)
    mine[0:8, :] = own_coef + left + right
    coefs = mine[...].T[0:8]

    def smooth(x):
        chain = pltpu.roll(x, 1, 0) + pltpu.roll(x, 7, 0) - 2.0 * x
        new = x + coefs[:, 0:1] * chain
        for d, shift in ((1, 4), (2, 2), (3, 0)):
            digit = lax.shift_right_logical(lane, shift) & 3
            up = jnp.where(digit == 0, 0.0, pltpu.roll(x, 1 << shift, 1))
            down = jnp.where(digit == 3, 0.0, pltpu.roll(x, 128 - (1 << shift), 1))
            new = new + coefs[:, d : d + 1] * (up + down - 2.0 * x)
        return jnp.where(lane < 64, new, 0.0)

    if direct:
        gathered = pltpu.make_async_remote_copy(
            src_ref=got, dst_ref=got, send_sem=a_s.at[0], recv_sem=a_r.at[0],
            device_id=peer(1, 0), device_id_type=MESH,
        )
        gathered.wait_recv()
        parts = [msg[me, ev]] + [got[n] for n in range(total - 1)]
    else:
        for copy in b_copies:
            copy.wait_recv()
        parts = [part[ev]] + [got2[o] for o in range(e_size - 1)]
    while len(parts) > 1:
        parts = [sum(parts[n : n + 2][1:], parts[n]) for n in range(0, len(parts), 2)]
    summed = parts[0]
    x = jnp.concatenate([summed, pltpu.roll(summed, 64, 1)], axis=0)
    x = smooth(smooth(jnp.where(lane < 64, x, 0.0)))
    tiles_out[...] = x[2 : 2 + width, 0:64]

    for f in range(3):
        for k in range(2):
            for c in range(3):
                rim_copy(f, k, c).wait_send()
    if direct:
        gathered.wait_send()
    else:
        for copy in a_copies + b_copies:
            copy.wait_send()
    for copy in coef_copies:
        copy.wait_send()
    pl.when(has_next)(lambda: to_next.wait_send())
    pl.when(has_last)(lambda: to_last.wait_send())


def write_out(final_vmem, tiles_vmem, final_hbm, tiles_hbm, sems):
    copies = [
        pltpu.make_async_copy(
            final_vmem.at[c, pl.ds(0, NODES)], final_hbm.at[pl.ds(NODES * c, NODES), 0], sems.at[c]
        )
        for c in range(3)
    ]
    copies.append(pltpu.make_async_copy(tiles_vmem, tiles_hbm, sems.at[3]))
    for copy in copies:
        copy.start()
    for copy in copies:
        copy.wait()


def solution(mesh):
    m_size, e_size = mesh.shape["mesh"], mesh.shape["event"]
    in_specs = (
        P("event", None, None, "mesh"),
        P("event", None, None, "mesh"),
        P(),
        P(),
        P("event", "mesh"),
        P("event", None, "mesh"),
        P("event", "mesh"),
        P("event", "mesh"),
        P(None, ("event", "mesh")),
    )
    out_specs = (P("event", None, None, "mesh"), P(None, ("event", "mesh")))

    def per_device(*args):
        fwd, smoothing = args[0], args[-1]
        width = smoothing.shape[1]
        dma = pltpu.SemaphoreType.DMA
        vmem = pl.BlockSpec(memory_space=pltpu.VMEM)
        hbm = pl.BlockSpec(memory_space=pltpu.HBM)
        line = (3 * NODES, 1, fwd.shape[-1])
        args = (args[0].reshape(line), args[1].reshape(line), args[2], args[3].T, args[4],
                args[5].reshape(6, 1, fwd.shape[-1]), *args[6:])
        if is_direct(m_size, e_size):
            a_count, b_count = 1, 1
            part, got, got2 = (1, width, 128), (m_size * e_size - 1, width, 128), (1, width, 128)
        else:
            a_count, b_count = m_size - 1, e_size - 1
            part, got, got2 = (e_size, width, 128), ((m_size - 1) * e_size, width, 128), (e_size - 1, width, 128)
        final, tiles = pl.pallas_call(
            functools.partial(kernel, m_size, e_size),
            out_shape=(
                pltpu.VMEM((3, ROWS, 128), f32),
                pltpu.VMEM((width, 64), f32),
            ),
            in_specs=[hbm] * len(args),
            out_specs=(vmem, vmem),
            scratch_shapes=[pltpu.VMEM(x.shape, x.dtype) for x in args[2:]]
            + [
                pltpu.VMEM((6, 144, 128), f32),
                pltpu.VMEM((6, ROWS, 128), f32),
                pltpu.VMEM((ROWS, 128), f32),
                pltpu.VMEM((3, ROWS, 128), f32),
                pltpu.VMEM((ROWS, ROWS), f32),
                pltpu.VMEM((7, ROWS, 128), f32),
                pltpu.VMEM((2, len(FACE_TILES), 8, 128), f32),
                pltpu.VMEM((12, 8, 128), jnp.int32),
                pltpu.VMEM((6, 8, 128), jnp.int32),
                pltpu.VMEM((8, 128), f32),
                pltpu.VMEM((3, 3, 32, 128), f32),
                pltpu.VMEM((3, 2, 3, 32, 128), f32),
                pltpu.VMEM((3, 120, 128), f32),
                pltpu.VMEM((8, 128), f32),
                pltpu.VMEM((4, 8, 128), f32),
                pltpu.VMEM((m_size, e_size, width, 128), f32),
                pltpu.VMEM((128, 128), f32),
                pltpu.VMEM(part, f32),
                pltpu.VMEM(got, f32),
                pltpu.VMEM(got2, f32),
                dma((6,)), dma((7,)), dma((3, 2, 3)), dma((3, 2, 3)), dma((4,)), dma((4,)),
                dma((a_count,)), dma((a_count,)), dma((b_count,)), dma((b_count,)),
                pltpu.SemaphoreType.REGULAR((3,)),
            ],
            compiler_params=pltpu.CompilerParams(collective_id=0, has_side_effects=True),
        )(*args)
        final, tiles = pl.pallas_call(
            write_out,
            out_shape=(pltpu.HBM(line, f32), pltpu.HBM((width, 64), f32)),
            in_specs=[vmem, vmem],
            out_specs=(hbm, hbm),
            scratch_shapes=[dma((4,))],
        )(
            pltpu.with_memory_space_constraint(final, pltpu.VMEM),
            pltpu.with_memory_space_constraint(tiles, pltpu.VMEM),
        )
        return final.reshape(fwd.shape), tiles.T

    return jax.shard_map(
        per_device, mesh=mesh, in_specs=in_specs, out_specs=out_specs, check_vma=False
    )
```

```python
import functools
import math

import jax
import jax.numpy as jnp
from jax import lax
from jax.experimental import pallas as pl
from jax.experimental.pallas import tpu as pltpu
from jax.sharding import PartitionSpec as P

STEPS = 2
time_square = 0.4
penalty = 0.5

PAD = 8
ROWS = 128
NODES = 125
SHIFT = (100, -100, 20, -20, 4, -4)
RELAYED = (0,)
MESH = pl.DeviceIdType.MESH
f32 = jnp.float32
bf16 = jnp.bfloat16


def on_face(face, node):
    i, j, k = node // 25, (node // 5) % 5, node % 5
    return (i == 0, i == 4, j == 0, j == 4, k == 0, k == 4)[face]


RIM_NODES = [n for n in range(NODES) if any(on_face(f, n) for f in range(6))]
RIM_PLACE = {n: at for at, n in enumerate(RIM_NODES)}
RIM_ROWS = -(-len(RIM_NODES) // 4)
FACE_TILES = [
    (f, t)
    for f in range(6)
    for t in range(ROWS // 8)
    if any(on_face(f, n) for n in range(8 * t, min(8 * t + 8, NODES)))
]


def split(x):
    high = x.astype(bf16)
    return high, (x - high.astype(f32)).astype(bf16)


def mm(a, b, dims=((1,), (0,))):
    return lax.dot_general(a, b, (dims, ((), ())), preferred_element_type=f32)


def pick(x, index):
    dims = lax.GatherDimensionNumbers(
        offset_dims=(), collapsed_slice_dims=(1,), start_index_map=(1,),
        operand_batching_dims=(0,), start_indices_batching_dims=(0,),
    )
    return lax.gather(x, index[:, :, None], dims, (1, 1), mode=lax.GatherScatterMode.PROMISE_IN_BOUNDS)


def gather_rows(load, places):
    pieces = {}
    for r, place in enumerate(places):
        if place is not None:
            pieces.setdefault(place - r, []).append(r)
    sublane = lax.broadcasted_iota(jnp.int32, (8, 128), 0)
    value = None
    for shift, members in pieces.items():
        piece = load(shift)
        if value is None:
            value = piece
        else:
            value = jnp.where((sublane >= members[0]) & (sublane <= members[-1]), piece, value)
    return load(0) if value is None else value


def is_direct(m_size, e_size):
    return m_size * e_size <= 64


def kernel(
    m_size, e_size,
    fwd_in, adj_in, stiff_hbm, proj_hbm, mat_hbm, nb_hbm, dest_hbm, count_hbm, smooth_hbm,
    fwd_out, tiles_out,
    stiff_in, proj_in, mat_in, nb_in, dest_in, count_in, smooth_in,
    F, N, K, A, S, W, M, IDX, RIM, LIVE, send, rim, U, coef, coef_in, msg, mine, part, got, got2,
    in_s, small_s, rim_s, rim_r, coef_s, coef_r, a_s, a_r, b_s, b_r, rounds,
):
    me = lax.axis_index("mesh")
    ev = lax.axis_index("event")
    total = m_size * e_size
    direct = is_direct(m_size, e_size)
    lin = ev * m_size + me
    after = lax.rem(me + 1, m_size)
    before = lax.rem(me + m_size - 1, m_size)

    barrier = pltpu.get_barrier_semaphore()
    core = lax.rem(ev, 2)
    chip = lax.div(ev, 2)
    chips = e_size // 2
    near = [((2 * chip + 1 - core, me), None)]
    for step in (1, -1):
        inside = (chip + step >= 0) & (chip + step < chips)
        near += [((2 * (chip + step) + c, me), inside) for c in range(2)]
    near_count = 1 + 2 * ((chip > 0).astype(jnp.int32) + (chip < chips - 1).astype(jnp.int32))

    def greet(sem, devices):
        for device, inside in devices:
            if inside is None:
                pl.semaphore_signal(sem, inc=1, device_id=device, device_id_type=MESH)
            else:

                @pl.when(inside)
                def _():
                    pl.semaphore_signal(sem, inc=1, device_id=device, device_id_type=MESH)

    for o in range(1, m_size):
        pl.semaphore_signal(
            barrier, inc=1, device_id=(ev, lax.rem(me + o, m_size)), device_id_type=MESH
        )
    greet(barrier, near)

    loads = {}
    for fc in (3, 4, 5, 0, 1, 2):
        source = fwd_in if fc < 3 else adj_in
        load = pltpu.make_async_copy(
            source.at[pl.ds(NODES * (fc % 3), NODES), 0], F.at[fc, pl.ds(PAD, NODES)], in_s.at[fc]
        )
        load.start()
        loads[fc] = load

    small = []
    for n, (src, dst) in enumerate((
        (smooth_hbm, smooth_in), (stiff_hbm, stiff_in), (nb_hbm, nb_in), (count_hbm, count_in),
        (mat_hbm, mat_in), (proj_hbm, proj_in), (dest_hbm, dest_in),
    )):
        load = pltpu.make_async_copy(src, dst, small_s.at[n])
        load.start()
        small.append(load)

    lane = lax.broadcasted_iota(jnp.int32, (1, 128), 1)
    zero8 = jnp.zeros((PAD, 128), f32)
    for fc in range(6):
        F[fc, 0:PAD, :] = zero8
        F[fc, PAD + NODES : 144, :] = jnp.zeros((144 - PAD - NODES, 128), f32)

    def pack(f, c, fc):
        for v in range(-(-RIM_ROWS // 8)):
            parts = []
            for g in range(4):
                inside = range(RIM_ROWS * g + 8 * v, min(RIM_ROWS * (g + 1), RIM_ROWS * g + 8 * v + 8))
                places = [RIM_NODES[n] if n < len(RIM_NODES) else None for n in inside]
                part = gather_rows(lambda low: F[fc, low + PAD : low + 2 * PAD, :], places)
                parts.append(pltpu.roll(part, 32 * g, 1) if g else part)
            send[f, c, 8 * v : 8 * v + 8, :] = jnp.where(
                lane < 64, jnp.where(lane < 32, parts[0], parts[1]),
                jnp.where(lane < 96, parts[2], parts[3]),
            )

    def load_field(f, then=None):
        for c in range(3):
            loads[3 * f + c].wait()
            pack(f, c, 3 * f + c)
            if then is not None:
                then(c)


    def remote(src, dst, s, r, device):
        copy = pltpu.make_async_remote_copy(
            src_ref=src, dst_ref=dst, send_sem=s, recv_sem=r, device_id=device, device_id_type=MESH
        )
        copy.start()
        return copy

    paired = m_size == 4
    first = 1 - lax.rem(me, 2) if paired else 0
    second = 1 - first
    sides = (first, second)
    used = pl.ds(0, RIM_ROWS)

    def rim_copy(f, k, c):
        slot = sides[1 - k] if paired else sides[k]
        return pltpu.make_async_remote_copy(
            src_ref=send.at[f, c, used], dst_ref=rim.at[f, slot, c, used],
            send_sem=rim_s.at[f, k, c], recv_sem=rim_r.at[f, k, c],
            device_id=(ev, jnp.where(slot == 0, after, before)), device_id_type=MESH,
        )

    def relay_copy(f, c):
        return pltpu.make_async_remote_copy(
            src_ref=rim.at[f, first, c, used], dst_ref=rim.at[f, second, c, used],
            send_sem=rim_s.at[f, 1, c], recv_sem=rim_r.at[f, 1, c],
            device_id=(ev, lax.rem(me + 2, m_size)), device_id_type=MESH,
        )

    def send_near(f):
        for c in range(3):
            rim_copy(f, 0, c).start()

    def send_far(f):
        for c in range(3):
            rim_copy(f, 1, c).start()

    def at_core(which, job):
        @pl.when(core == which)
        def _():
            job()

    def far_of(c):
        if c == 0:
            pl.semaphore_wait(barrier, near_count + (m_size - 1))
        rim_copy(1, 1, c).start()

    load_field(1, far_of)
    send_near(1)
    load_field(0)
    coef[...] = jnp.zeros((8, 128), f32)

    @pl.when(ev == 0)
    def _():
        coef_in[2] = jnp.zeros((8, 128), f32)

    @pl.when(ev == e_size - 1)
    def _():
        coef_in[3] = jnp.zeros((8, 128), f32)

    small[0].wait()
    coef[0:4, 0:4] = smooth_in[...]
    at_core(0, lambda: (send_far(0), send_near(0)))
    coef_copies = [
        remote(coef, coef_in.at[0], coef_s.at[0], coef_r.at[0], (ev, after)),
        remote(coef, coef_in.at[1], coef_s.at[1], coef_r.at[1], (ev, before)),
    ]
    beside, above, below = near[:1], near[1:3], near[3:]
    is_first, is_last = chip == 0, chip == chips - 1

    def wait_up():
        pl.semaphore_wait(rounds.at[0], 2)
        greet(rounds.at[0], above)

    def wait_down():
        pl.semaphore_wait(rounds.at[1], 2)
        greet(rounds.at[1], below)

    greet(rounds.at[2], beside)
    pl.when(is_first)(lambda: greet(rounds.at[0], above))
    pl.when(is_last)(lambda: greet(rounds.at[1], below))
    between = jnp.logical_not(is_first | is_last)
    turns = between & (chip == chips - 2)

    for load in small[1:]:
        load.wait()
    live = jnp.where(lane < count_in[0:1, 0:1], 1.0, 0.0).astype(f32)
    LIVE[...] = jnp.broadcast_to(live, (8, 128))
    for fc in range(6):
        F[fc, PAD : PAD + NODES, :] = F[fc, PAD : PAD + NODES, :] * live

    node = lax.broadcasted_iota(jnp.int32, (ROWS, 128), 0).astype(f32)
    i = jnp.floor((node + 0.5) / 25.0)
    rest = node - 25.0 * i
    j = jnp.floor((rest + 0.5) / 5.0)
    k = rest - 5.0 * j
    count = jnp.zeros((ROWS, 128), f32)
    for f, test in enumerate((i == 0.0, i == 4.0, j == 0.0, j == 4.0, k == 0.0, k == 4.0)):
        mask = jnp.where(test & (node < NODES - 0.5), 1.0, 0.0).astype(f32)
        W[f] = mask
        count = count + mask
    W[6] = count
    nb = nb_in[:, 0, :]
    target = lax.shift_right_logical(nb, 7)
    slot = nb & 127
    relative = lax.rem(target - me + m_size, m_size)
    for f in range(6):
        IDX[f] = jnp.broadcast_to(slot[f : f + 1], (8, 128))
        IDX[6 + f] = jnp.broadcast_to(relative[f : f + 1], (8, 128))
        far = jnp.where(relative[f : f + 1] == jnp.where(second == 1, 1, m_size - 1), 32, 0)
        RIM[f] = jnp.broadcast_to((slot[f : f + 1] & 31) + far, (8, 128))
    for c in range(3):
        U[c, 0:PAD, :] = zero8
        U[c, PAD + 4 * RIM_ROWS :, :] = jnp.zeros((U.shape[1] - PAD - 4 * RIM_ROWS, 128), f32)
    S[...] = jnp.zeros((ROWS, ROWS), f32)
    S[0:NODES, 0:NODES] = stiff_in[...]
    s_hi, s_lo = split(S[...])
    material = mat_in[...]

    def strain(base):
        wide = jnp.concatenate([F[base + c, PAD : PAD + ROWS, :] for c in range(3)], axis=1)
        hi, lo = split(wide)
        both = mm(s_hi, hi) + (mm(s_hi, lo) + mm(s_lo, hi))
        return [both[:, 128 * c : 128 * (c + 1)] for c in range(3)]

    def build_masks(which, here):
        for n, (f, t) in enumerate(FACE_TILES):
            M[which, n] = jnp.where(here(IDX[6 + f]), W[f, 8 * t : 8 * t + 8, :], 0.0)

    def face_sums(read, which):
        sums = [None] * (ROWS // 8)
        for n, (f, t) in enumerate(FACE_TILES):
            g = read(f, t) * M[which, n]
            sums[t] = g if sums[t] is None else sums[t] + g
        return sums

    def own_pass(base):
        for c in range(3):
            def read(f, t):
                at = 8 * t + SHIFT[f] + PAD
                return pick(F[base + c, at : at + 8, :], IDX[f])

            sums = face_sums(read, 0)
            for t in range(ROWS // 8):
                at = pl.ds(8 * t, 8)
                v = F[base + c, 8 * t + PAD : 8 * t + 2 * PAD, :]
                acc = sums[t] - W[6, at, :] * v
                N[base + c, at, :] = N[base + c, at, :] + (time_square * penalty) * acc

    def arrive(f, k):
        for c in range(3):
            rim_copy(f, k, c).wait_recv()
            if k == 0 and paired and f in RELAYED:

                @pl.when(core == 1)
                def _():
                    relay_copy(f, c).start()

    def unpack(f, k):
        side = sides[k]
        for c in range(3):
            for g in range(4):
                at = pl.ds(PAD + RIM_ROWS * g, RIM_ROWS)
                turn = (32 * k - 32 * g) % 128
                part = rim[f, side, c, 0:RIM_ROWS, :]
                part = pltpu.roll(part, turn, 1) if turn else part
                U[c, at, :] = part if k == 0 else jnp.where(lane < 32, U[c, at, :], part)

    def rim_pass(base, store):
        for c in range(3):

            def read(f, t):
                places = [
                    RIM_PLACE[8 * t + r + SHIFT[f]] if 8 * t + r < NODES and on_face(f, 8 * t + r) else None
                    for r in range(8)
                ]
                rows = gather_rows(lambda low: U[c, low + PAD : low + 2 * PAD, :], places)
                return pick(rows, RIM[f])

            sums = face_sums(read, 1)
            for t in range(ROWS // 8):
                old = N[base + c, 8 * t : 8 * t + 8, :]
                store(c, t, old + (time_square * penalty) * sums[t])

    if paired:
        at_core(1, lambda: send_near(0))
    build_masks(0, lambda relative: relative == 0)
    st_f = strain(0)
    st_a = strain(3)
    energy = jnp.zeros((ROWS, 128), f32)
    for c in range(3):
        vf = F[c, PAD : PAD + ROWS, :]
        energy = energy + vf * st_a[c]
        N[c] = vf - time_square * material * st_f[c]
        N[3 + c] = F[3 + c, PAD : PAD + ROWS, :] - time_square * material * st_a[c]
    K[...] = energy
    if not paired:
        at_core(1, lambda: (send_near(0), send_far(0)))
    else:
        pass
    own_pass(3)
    own_pass(0)
    pl.when(between)(wait_up)
    pl.when(turns)(wait_down)
    build_masks(1, lambda relative: (relative == 1) | (relative == m_size - 1))

    def keep_adjoint(c, t, value):
        F[3 + c, 8 * t + PAD : 8 * t + 2 * PAD, :] = LIVE[...] * value

    def keep_forward(c, t, value):
        value = LIVE[...] * value
        at = pl.ds(8 * t + PAD, 8)
        line = pl.ds(8 * t, 8)
        N[c, line, :] = 2.0 * value - F[c, at, :]
        F[c, at, :] = value
        K[line, :] = K[line, :] + value * A[c, line, :]

    arrive(1, 0)
    unpack(1, 0)
    if paired and 0 in RELAYED:
        at_core(1, lambda: arrive(0, 0))
    arrive(1, 1)
    unpack(1, 1)
    rim_pass(3, keep_adjoint)
    pl.when(between & jnp.logical_not(turns))(wait_down)
    for c, value in enumerate(strain(3)):
        A[c] = value
    if paired and 0 in RELAYED:
        at_core(0, lambda: arrive(0, 0))
    else:
        arrive(0, 0)
    unpack(0, 0)
    arrive(0, 1)
    unpack(0, 1)
    rim_pass(0, keep_forward)

    def send_second():
        for c in range(3):
            pack(2, c, c)
        if paired and 2 in RELAYED:
            at_core(0, lambda: send_far(2))
        else:
            send_far(2)
        send_near(2)

    ahead = chip == 0
    pl.when(ahead)(send_second)
    elements = F.shape[-1]
    width = smooth_in.shape[1]
    scale = math.sqrt(width / elements) / STEPS
    twin = jnp.concatenate([proj_in[...], proj_in[...]], axis=0)
    t_hi, t_lo = split(twin)
    k_hi, k_lo = split(K[0:NODES, :])
    blocks = (mm(t_hi, k_hi) + (mm(t_hi, k_lo) + mm(t_lo, k_hi))) * scale
    b_hi, b_lo = split(blocks)
    row = lax.broadcasted_iota(jnp.int32, (total * width, 128), 0)
    owner = lax.div(row, width)
    tile = width * (lax.rem(owner, e_size) * m_size + lax.div(owner, e_size)) + lax.rem(row, width)
    dest = dest_in[...]
    nt = ((1,), (1,))

    def spread(offset):
        hot = jnp.where(tile + offset == dest, 1.0, 0.0).astype(f32).astype(bf16)
        return mm(hot, b_hi, nt) + mm(hot, b_lo, nt)

    packed = jnp.where(lane < 64, spread(-2), spread(2))
    msg[...] = packed.reshape(m_size, e_size, width, 128)

    pl.semaphore_wait(rounds.at[2], 1)
    if chips > 1:
        pl.when(is_last)(wait_up)
        pl.when(is_first)(wait_down)

    def peer(oe, om):
        return lax.rem(ev + oe, e_size), lax.rem(me + om, m_size)

    if direct:
        offsets = [(oe, om) for oe in list(range(1, e_size)) + [0] for om in range(m_size) if oe or om]
        for oe, om in offsets:
            e, m = peer(oe, om)
            remote(msg.at[m, e], got.at[oe * m_size + om - 1], a_s.at[0], a_r.at[0], (e, m))
    else:
        a_copies = [
            remote(msg.at[lax.rem(me + o, m_size)], got.at[pl.ds(e_size * (o - 1), e_size)],
                   a_s.at[o - 1], a_r.at[o - 1], (ev, lax.rem(me + o, m_size)))
            for o in range(1, m_size)
        ]

    pl.when(jnp.logical_not(ahead))(send_second)

    st_f = strain(0)
    for c in range(3):
        N[c] = N[c] - time_square * material * st_f[c]
    own_pass(0)

    for copy in coef_copies:
        copy.wait_recv()
    has_next, has_last = ev < e_size - 1, ev > 0

    def chain_copy(n, step):
        return pltpu.make_async_remote_copy(
            src_ref=coef_in.at[n], dst_ref=coef_in.at[2 + n], send_sem=coef_s.at[2 + n],
            recv_sem=coef_r.at[2 + n], device_id=(lax.rem(ev + step + e_size, e_size), me),
            device_id_type=MESH,
        )

    to_next, to_last = chain_copy(0, 1), chain_copy(1, -1)
    pl.when(has_next)(lambda: to_next.start())
    pl.when(has_last)(lambda: to_last.start())
    if not direct:
        for copy in a_copies:
            copy.wait_recv()
        mine_sum = msg[me]
        for o in range(m_size - 1):
            mine_sum = mine_sum + got[e_size * o : e_size * (o + 1)]
        part[...] = mine_sum
        b_copies = [
            remote(part.at[lax.rem(ev + o, e_size)], got2.at[o - 1], b_s.at[o - 1], b_r.at[o - 1],
                   (lax.rem(ev + o, e_size), me))
            for o in range(1, e_size)
        ]

    def final(c, t, value):
        fwd_out[c, 8 * t : 8 * t + 8, :] = LIVE[...] * value

    arrive(2, 0)
    unpack(2, 0)
    arrive(2, 1)
    unpack(2, 1)
    rim_pass(0, final)

    pl.when(has_last)(lambda: to_next.wait_recv())
    pl.when(has_next)(lambda: to_last.wait_recv())
    own_coef = pltpu.roll(coef[...], 2, 1)
    left = jnp.where(lin > 0, jnp.where(me > 0, coef_in[0], coef_in[2]), 0.0)
    right = jnp.where(
        lin < total - 1, jnp.where(me < m_size - 1, coef_in[1], coef_in[3]), 0.0
    )
    left = jnp.where(lane < 2, pltpu.roll(left, 126, 1), 0.0)
    right = pltpu.roll(right, 6, 1)
    mine[...] = jnp.zeros((128, 128), f32)
    mine[0:8, :] = own_coef + left + right
    coefs = mine[...].T[0:8]

    def smooth(x):
        chain = pltpu.roll(x, 1, 0) + pltpu.roll(x, 7, 0) - 2.0 * x
        new = x + coefs[:, 0:1] * chain
        for d, shift in ((1, 4), (2, 2), (3, 0)):
            digit = lax.shift_right_logical(lane, shift) & 3
            up = jnp.where(digit == 0, 0.0, pltpu.roll(x, 1 << shift, 1))
            down = jnp.where(digit == 3, 0.0, pltpu.roll(x, 128 - (1 << shift), 1))
            new = new + coefs[:, d : d + 1] * (up + down - 2.0 * x)
        return jnp.where(lane < 64, new, 0.0)

    if direct:
        gathered = pltpu.make_async_remote_copy(
            src_ref=got, dst_ref=got, send_sem=a_s.at[0], recv_sem=a_r.at[0],
            device_id=peer(1, 0), device_id_type=MESH,
        )
        gathered.wait_recv()
        parts = [msg[me, ev]] + [got[n] for n in range(total - 1)]
    else:
        for copy in b_copies:
            copy.wait_recv()
        parts = [part[ev]] + [got2[o] for o in range(e_size - 1)]
    while len(parts) > 1:
        parts = [sum(parts[n : n + 2][1:], parts[n]) for n in range(0, len(parts), 2)]
    summed = parts[0]
    x = jnp.concatenate([summed, pltpu.roll(summed, 64, 1)], axis=0)
    x = smooth(smooth(jnp.where(lane < 64, x, 0.0)))
    tiles_out[...] = x[2 : 2 + width, 0:64]

    for f in range(3):
        for k in range(2):
            for c in range(3):
                rim_copy(f, k, c).wait_send()
    if direct:
        gathered.wait_send()
    else:
        for copy in a_copies + b_copies:
            copy.wait_send()
    for copy in coef_copies:
        copy.wait_send()
    pl.when(has_next)(lambda: to_next.wait_send())
    pl.when(has_last)(lambda: to_last.wait_send())


def write_out(final_vmem, tiles_vmem, final_hbm, tiles_hbm, sems):
    copies = [
        pltpu.make_async_copy(
            final_vmem.at[c, pl.ds(0, NODES)], final_hbm.at[pl.ds(NODES * c, NODES), 0], sems.at[c]
        )
        for c in range(3)
    ]
    copies.append(pltpu.make_async_copy(tiles_vmem, tiles_hbm, sems.at[3]))
    for copy in copies:
        copy.start()
    for copy in copies:
        copy.wait()


def solution(mesh):
    m_size, e_size = mesh.shape["mesh"], mesh.shape["event"]
    in_specs = (
        P("event", None, None, "mesh"),
        P("event", None, None, "mesh"),
        P(),
        P(),
        P("event", "mesh"),
        P("event", None, "mesh"),
        P("event", "mesh"),
        P("event", "mesh"),
        P(None, ("event", "mesh")),
    )
    out_specs = (P("event", None, None, "mesh"), P(None, ("event", "mesh")))

    def per_device(*args):
        fwd, smoothing = args[0], args[-1]
        width = smoothing.shape[1]
        dma = pltpu.SemaphoreType.DMA
        vmem = pl.BlockSpec(memory_space=pltpu.VMEM)
        hbm = pl.BlockSpec(memory_space=pltpu.HBM)
        line = (3 * NODES, 1, fwd.shape[-1])
        args = (args[0].reshape(line), args[1].reshape(line), args[2], args[3].T, args[4],
                args[5].reshape(6, 1, fwd.shape[-1]), *args[6:])
        if is_direct(m_size, e_size):
            a_count, b_count = 1, 1
            part, got, got2 = (1, width, 128), (m_size * e_size - 1, width, 128), (1, width, 128)
        else:
            a_count, b_count = m_size - 1, e_size - 1
            part, got, got2 = (e_size, width, 128), ((m_size - 1) * e_size, width, 128), (e_size - 1, width, 128)
        final, tiles = pl.pallas_call(
            functools.partial(kernel, m_size, e_size),
            out_shape=(
                pltpu.VMEM((3, ROWS, 128), f32),
                pltpu.VMEM((width, 64), f32),
            ),
            in_specs=[hbm] * len(args),
            out_specs=(vmem, vmem),
            scratch_shapes=[pltpu.VMEM(x.shape, x.dtype) for x in args[2:]]
            + [
                pltpu.VMEM((6, 144, 128), f32),
                pltpu.VMEM((6, ROWS, 128), f32),
                pltpu.VMEM((ROWS, 128), f32),
                pltpu.VMEM((3, ROWS, 128), f32),
                pltpu.VMEM((ROWS, ROWS), f32),
                pltpu.VMEM((7, ROWS, 128), f32),
                pltpu.VMEM((2, len(FACE_TILES), 8, 128), f32),
                pltpu.VMEM((12, 8, 128), jnp.int32),
                pltpu.VMEM((6, 8, 128), jnp.int32),
                pltpu.VMEM((8, 128), f32),
                pltpu.VMEM((3, 3, 32, 128), f32),
                pltpu.VMEM((3, 2, 3, 32, 128), f32),
                pltpu.VMEM((3, 120, 128), f32),
                pltpu.VMEM((8, 128), f32),
                pltpu.VMEM((4, 8, 128), f32),
                pltpu.VMEM((m_size, e_size, width, 128), f32),
                pltpu.VMEM((128, 128), f32),
                pltpu.VMEM(part, f32),
                pltpu.VMEM(got, f32),
                pltpu.VMEM(got2, f32),
                dma((6,)), dma((7,)), dma((3, 2, 3)), dma((3, 2, 3)), dma((4,)), dma((4,)),
                dma((a_count,)), dma((a_count,)), dma((b_count,)), dma((b_count,)),
                pltpu.SemaphoreType.REGULAR((3,)),
            ],
            compiler_params=pltpu.CompilerParams(collective_id=0, has_side_effects=True),
        )(*args)
        final, tiles = pl.pallas_call(
            write_out,
            out_shape=(pltpu.HBM(line, f32), pltpu.HBM((width, 64), f32)),
            in_specs=[vmem, vmem],
            out_specs=(hbm, hbm),
            scratch_shapes=[dma((4,))],
        )(
            pltpu.with_memory_space_constraint(final, pltpu.VMEM),
            pltpu.with_memory_space_constraint(tiles, pltpu.VMEM),
        )
        return final.reshape(fwd.shape), tiles.T

    return jax.shard_map(
        per_device, mesh=mesh, in_specs=in_specs, out_specs=out_specs, check_vma=False
    )
```

```python
import functools
import math

import jax
import jax.numpy as jnp
from jax import lax
from jax.experimental import pallas as pl
from jax.experimental.pallas import tpu as pltpu
from jax.sharding import PartitionSpec as P

STEPS = 2
time_square = 0.4
penalty = 0.5

PAD = 8
ROWS = 128
NODES = 125
SHIFT = (100, -100, 20, -20, 4, -4)
RELAYED = (0,)
MESH = pl.DeviceIdType.MESH
f32 = jnp.float32
bf16 = jnp.bfloat16


def on_face(face, node):
    i, j, k = node // 25, (node // 5) % 5, node % 5
    return (i == 0, i == 4, j == 0, j == 4, k == 0, k == 4)[face]


RIM_NODES = [n for n in range(NODES) if any(on_face(f, n) for f in range(6))]
RIM_PLACE = {n: at for at, n in enumerate(RIM_NODES)}
RIM_ROWS = -(-len(RIM_NODES) // 4)
FACE_TILES = [
    (f, t)
    for f in range(6)
    for t in range(ROWS // 8)
    if any(on_face(f, n) for n in range(8 * t, min(8 * t + 8, NODES)))
]


def split(x):
    high = x.astype(bf16)
    return high, (x - high.astype(f32)).astype(bf16)


def mm(a, b, dims=((1,), (0,))):
    return lax.dot_general(a, b, (dims, ((), ())), preferred_element_type=f32)


def pick(x, index):
    dims = lax.GatherDimensionNumbers(
        offset_dims=(), collapsed_slice_dims=(1,), start_index_map=(1,),
        operand_batching_dims=(0,), start_indices_batching_dims=(0,),
    )
    return lax.gather(x, index[:, :, None], dims, (1, 1), mode=lax.GatherScatterMode.PROMISE_IN_BOUNDS)


def gather_rows(load, places):
    pieces = {}
    for r, place in enumerate(places):
        if place is not None:
            pieces.setdefault(place - r, []).append(r)
    sublane = lax.broadcasted_iota(jnp.int32, (8, 128), 0)
    value = None
    for shift, members in pieces.items():
        piece = load(shift)
        if value is None:
            value = piece
        else:
            value = jnp.where((sublane >= members[0]) & (sublane <= members[-1]), piece, value)
    return load(0) if value is None else value


def is_direct(m_size, e_size):
    return m_size * e_size <= 64


def kernel(
    m_size, e_size,
    fwd_in, adj_in, stiff_hbm, proj_hbm, mat_hbm, nb_hbm, dest_hbm, count_hbm, smooth_hbm,
    fwd_out, tiles_out,
    stiff_in, proj_in, mat_in, nb_in, dest_in, count_in, smooth_in,
    F, N, K, A, S, T, HOT, W, M, IDX, RIM, LIVE, send, rim, U, coef, coef_in, msg, mine, part, got, got2,
    in_s, small_s, rim_s, rim_r, coef_s, coef_r, a_s, a_r, b_s, b_r, rounds,
):
    me = lax.axis_index("mesh")
    ev = lax.axis_index("event")
    total = m_size * e_size
    direct = is_direct(m_size, e_size)
    lin = ev * m_size + me
    after = lax.rem(me + 1, m_size)
    before = lax.rem(me + m_size - 1, m_size)

    barrier = pltpu.get_barrier_semaphore()
    core = lax.rem(ev, 2)
    chip = lax.div(ev, 2)
    chips = e_size // 2
    near = [((2 * chip + 1 - core, me), None)]
    for step in (1, -1):
        inside = (chip + step >= 0) & (chip + step < chips)
        near += [((2 * (chip + step) + c, me), inside) for c in range(2)]
    near_count = 1 + 2 * ((chip > 0).astype(jnp.int32) + (chip < chips - 1).astype(jnp.int32))

    def greet(sem, devices):
        for device, inside in devices:
            if inside is None:
                pl.semaphore_signal(sem, inc=1, device_id=device, device_id_type=MESH)
            else:

                @pl.when(inside)
                def _():
                    pl.semaphore_signal(sem, inc=1, device_id=device, device_id_type=MESH)

    for o in range(1, m_size):
        pl.semaphore_signal(
            barrier, inc=1, device_id=(ev, lax.rem(me + o, m_size)), device_id_type=MESH
        )
    greet(barrier, near)

    loads = {}
    for fc in (3, 4, 5, 0, 1, 2):
        source = fwd_in if fc < 3 else adj_in
        load = pltpu.make_async_copy(
            source.at[pl.ds(NODES * (fc % 3), NODES), 0], F.at[fc, pl.ds(PAD, NODES)], in_s.at[fc]
        )
        load.start()
        loads[fc] = load

    small = []
    for n, (src, dst) in enumerate((
        (smooth_hbm, smooth_in), (stiff_hbm, stiff_in), (nb_hbm, nb_in), (count_hbm, count_in),
        (mat_hbm, mat_in), (proj_hbm, proj_in), (dest_hbm, dest_in),
    )):
        load = pltpu.make_async_copy(src, dst, small_s.at[n])
        load.start()
        small.append(load)

    lane = lax.broadcasted_iota(jnp.int32, (1, 128), 1)
    zero8 = jnp.zeros((PAD, 128), f32)
    for fc in range(6):
        F[fc, 0:PAD, :] = zero8
        F[fc, PAD + NODES : 144, :] = jnp.zeros((144 - PAD - NODES, 128), f32)

    def pack(f, c, fc):
        for v in range(-(-RIM_ROWS // 8)):
            parts = []
            for g in range(4):
                inside = range(RIM_ROWS * g + 8 * v, min(RIM_ROWS * (g + 1), RIM_ROWS * g + 8 * v + 8))
                places = [RIM_NODES[n] if n < len(RIM_NODES) else None for n in inside]
                part = gather_rows(lambda low: F[fc, low + PAD : low + 2 * PAD, :], places)
                parts.append(pltpu.roll(part, 32 * g, 1) if g else part)
            send[f, c, 8 * v : 8 * v + 8, :] = jnp.where(
                lane < 64, jnp.where(lane < 32, parts[0], parts[1]),
                jnp.where(lane < 96, parts[2], parts[3]),
            )

    def load_field(f, then=None):
        for c in range(3):
            loads[3 * f + c].wait()
            pack(f, c, 3 * f + c)
            if then is not None:
                then(c)


    def remote(src, dst, s, r, device):
        copy = pltpu.make_async_remote_copy(
            src_ref=src, dst_ref=dst, send_sem=s, recv_sem=r, device_id=device, device_id_type=MESH
        )
        copy.start()
        return copy

    paired = m_size == 4
    first = 1 - lax.rem(me, 2) if paired else 0
    second = 1 - first
    sides = (first, second)
    used = pl.ds(0, RIM_ROWS)

    def rim_copy(f, k, c):
        slot = sides[1 - k] if paired else sides[k]
        return pltpu.make_async_remote_copy(
            src_ref=send.at[f, c, used], dst_ref=rim.at[f, slot, c, used],
            send_sem=rim_s.at[f, k, c], recv_sem=rim_r.at[f, k, c],
            device_id=(ev, jnp.where(slot == 0, after, before)), device_id_type=MESH,
        )

    def relay_copy(f, c):
        return pltpu.make_async_remote_copy(
            src_ref=rim.at[f, first, c, used], dst_ref=rim.at[f, second, c, used],
            send_sem=rim_s.at[f, 1, c], recv_sem=rim_r.at[f, 1, c],
            device_id=(ev, lax.rem(me + 2, m_size)), device_id_type=MESH,
        )

    def send_near(f):
        for c in range(3):
            rim_copy(f, 0, c).start()

    def send_far(f):
        for c in range(3):
            rim_copy(f, 1, c).start()

    def at_core(which, job):
        @pl.when(core == which)
        def _():
            job()

    def far_of(c):
        if c == 0:
            pl.semaphore_wait(barrier, near_count + (m_size - 1))
        rim_copy(1, 1, c).start()

    load_field(1, far_of)
    send_near(1)
    def forward_of(c):
        at_core(0, lambda: rim_copy(0, 1, c).start())

    load_field(0, forward_of)
    at_core(0, lambda: send_near(0))
    coef[...] = jnp.zeros((8, 128), f32)

    @pl.when(ev == 0)
    def _():
        coef_in[2] = jnp.zeros((8, 128), f32)

    @pl.when(ev == e_size - 1)
    def _():
        coef_in[3] = jnp.zeros((8, 128), f32)

    small[0].wait()
    coef[0:4, 0:4] = smooth_in[...]
    coef_copies = [
        remote(coef, coef_in.at[0], coef_s.at[0], coef_r.at[0], (ev, after)),
        remote(coef, coef_in.at[1], coef_s.at[1], coef_r.at[1], (ev, before)),
    ]
    beside, above, below = near[:1], near[1:3], near[3:]
    is_first, is_last = chip == 0, chip == chips - 1

    def wait_up():
        pl.semaphore_wait(rounds.at[0], 2)
        greet(rounds.at[0], above)

    def wait_down():
        pl.semaphore_wait(rounds.at[1], 2)
        greet(rounds.at[1], below)

    greet(rounds.at[2], beside)
    pl.when(is_first)(lambda: greet(rounds.at[0], above))
    pl.when(is_last)(lambda: greet(rounds.at[1], below))
    between = jnp.logical_not(is_first | is_last)
    turns = between & (chip == chips - 2)

    for load in small[1:]:
        load.wait()
    live = jnp.where(lane < count_in[0:1, 0:1], 1.0, 0.0).astype(f32)
    LIVE[...] = jnp.broadcast_to(live, (8, 128))
    for fc in range(6):
        F[fc, PAD : PAD + NODES, :] = F[fc, PAD : PAD + NODES, :] * live

    node = lax.broadcasted_iota(jnp.int32, (ROWS, 128), 0).astype(f32)
    i = jnp.floor((node + 0.5) / 25.0)
    rest = node - 25.0 * i
    j = jnp.floor((rest + 0.5) / 5.0)
    k = rest - 5.0 * j
    count = jnp.zeros((ROWS, 128), f32)
    for f, test in enumerate((i == 0.0, i == 4.0, j == 0.0, j == 4.0, k == 0.0, k == 4.0)):
        mask = jnp.where(test & (node < NODES - 0.5), 1.0, 0.0).astype(f32)
        W[f] = mask
        count = count + mask
    W[6] = count
    nb = nb_in[:, 0, :]
    target = lax.shift_right_logical(nb, 7)
    slot = nb & 127
    relative = lax.rem(target - me + m_size, m_size)
    for f in range(6):
        IDX[f] = jnp.broadcast_to(slot[f : f + 1], (8, 128))
        IDX[6 + f] = jnp.broadcast_to(relative[f : f + 1], (8, 128))
        far = jnp.where(relative[f : f + 1] == jnp.where(second == 1, 1, m_size - 1), 32, 0)
        RIM[f] = jnp.broadcast_to((slot[f : f + 1] & 31) + far, (8, 128))
    for c in range(3):
        U[c, 0:PAD, :] = zero8
        U[c, PAD + 4 * RIM_ROWS :, :] = jnp.zeros((U.shape[1] - PAD - 4 * RIM_ROWS, 128), f32)
    S[...] = jnp.zeros((ROWS, ROWS), f32)
    S[0:NODES, 0:NODES] = stiff_in[...]
    s_hi, s_lo = split(S[...])
    material = mat_in[...]

    def strain(base):
        wide = jnp.concatenate([F[base + c, PAD : PAD + ROWS, :] for c in range(3)], axis=1)
        hi, lo = split(wide)
        both = mm(s_hi, hi) + (mm(s_hi, lo) + mm(s_lo, hi))
        return [both[:, 128 * c : 128 * (c + 1)] for c in range(3)]

    def build_masks(which, here):
        for n, (f, t) in enumerate(FACE_TILES):
            M[which, n] = jnp.where(here(IDX[6 + f]), W[f, 8 * t : 8 * t + 8, :], 0.0)

    def face_sums(read, which):
        sums = [None] * (ROWS // 8)
        for n, (f, t) in enumerate(FACE_TILES):
            g = read(f, t) * M[which, n]
            sums[t] = g if sums[t] is None else sums[t] + g
        return sums

    def own_pass(base):
        for c in range(3):
            def read(f, t):
                at = 8 * t + SHIFT[f] + PAD
                return pick(F[base + c, at : at + 8, :], IDX[f])

            sums = face_sums(read, 0)
            for t in range(ROWS // 8):
                at = pl.ds(8 * t, 8)
                v = F[base + c, 8 * t + PAD : 8 * t + 2 * PAD, :]
                acc = sums[t] - W[6, at, :] * v
                N[base + c, at, :] = N[base + c, at, :] + (time_square * penalty) * acc

    def arrive(f, k):
        for c in range(3):
            rim_copy(f, k, c).wait_recv()
            if k == 0 and paired and f in RELAYED:

                @pl.when(core == 1)
                def _():
                    relay_copy(f, c).start()

    def unpack(f, k):
        side = sides[k]
        for c in range(3):
            for g in range(4):
                at = pl.ds(PAD + RIM_ROWS * g, RIM_ROWS)
                turn = (32 * k - 32 * g) % 128
                part = rim[f, side, c, 0:RIM_ROWS, :]
                part = pltpu.roll(part, turn, 1) if turn else part
                U[c, at, :] = part if k == 0 else jnp.where(lane < 32, U[c, at, :], part)

    def rim_pass(base, store):
        for c in range(3):

            def read(f, t):
                places = [
                    RIM_PLACE[8 * t + r + SHIFT[f]] if 8 * t + r < NODES and on_face(f, 8 * t + r) else None
                    for r in range(8)
                ]
                rows = gather_rows(lambda low: U[c, low + PAD : low + 2 * PAD, :], places)
                return pick(rows, RIM[f])

            sums = face_sums(read, 1)
            for t in range(ROWS // 8):
                old = N[base + c, 8 * t : 8 * t + 8, :]
                store(c, t, old + (time_square * penalty) * sums[t])

    if paired:
        at_core(1, lambda: send_near(0))
    build_masks(0, lambda relative: relative == 0)
    st_f = strain(0)
    st_a = strain(3)
    energy = jnp.zeros((ROWS, 128), f32)
    for c in range(3):
        vf = F[c, PAD : PAD + ROWS, :]
        energy = energy + vf * st_a[c]
        N[c] = vf - time_square * material * st_f[c]
        N[3 + c] = F[3 + c, PAD : PAD + ROWS, :] - time_square * material * st_a[c]
    K[...] = energy
    if not paired:
        at_core(1, lambda: (send_near(0), send_far(0)))
    else:
        pass
    own_pass(3)
    own_pass(0)
    pl.when(between)(wait_up)
    pl.when(turns)(wait_down)
    build_masks(1, lambda relative: (relative == 1) | (relative == m_size - 1))

    def keep_adjoint(c, t, value):
        F[3 + c, 8 * t + PAD : 8 * t + 2 * PAD, :] = LIVE[...] * value

    def keep_forward(c, t, value):
        value = LIVE[...] * value
        at = pl.ds(8 * t + PAD, 8)
        line = pl.ds(8 * t, 8)
        N[c, line, :] = 2.0 * value - F[c, at, :]
        F[c, at, :] = value
        K[line, :] = K[line, :] + value * A[c, line, :]

    elements = F.shape[-1]
    width = smooth_in.shape[1]
    scale = math.sqrt(width / elements) / STEPS
    pad = jnp.zeros((proj_in.shape[0], ROWS - NODES), f32)
    half = jnp.concatenate([proj_in[...], pad], axis=1)
    t_hi, t_lo = split(jnp.concatenate([half, half], axis=0))
    T[...] = jnp.concatenate([t_hi, t_hi, t_lo], axis=1)
    row = lax.broadcasted_iota(jnp.int32, (total * width, 128), 0)
    owner = lax.div(row, width)
    tile = width * (lax.rem(owner, e_size) * m_size + lax.div(owner, e_size)) + lax.rem(row, width)
    dest = dest_in[...]
    nt = ((1,), (1,))
    for at, offset in ((0, -2), (128, 2)):
        HOT[:, at : at + 128] = jnp.where(tile + offset == dest, 1.0, 0.0).astype(f32).astype(bf16)

    arrive(1, 0)
    unpack(1, 0)
    if paired and 0 in RELAYED:
        at_core(1, lambda: arrive(0, 0))
    arrive(1, 1)
    unpack(1, 1)
    rim_pass(3, keep_adjoint)
    pl.when(between & jnp.logical_not(turns))(wait_down)
    for c, value in enumerate(strain(3)):
        A[c] = value
    if paired and 0 in RELAYED:
        at_core(0, lambda: arrive(0, 0))
    else:
        arrive(0, 0)
    unpack(0, 0)
    arrive(0, 1)
    unpack(0, 1)
    rim_pass(0, keep_forward)

    def send_second():
        for c in range(3):
            pack(2, c, c)
        if paired and 2 in RELAYED:
            at_core(0, lambda: send_far(2))
        else:
            send_far(2)
        send_near(2)

    ahead = chip == 0
    pl.when(ahead)(send_second)
    k_hi, k_lo = split(K[...])
    blocks = mm(T[:, 0:256], jnp.concatenate([k_hi, k_lo], axis=0)) + mm(T[:, 256:384], k_hi)
    blocks = blocks * scale
    low_half = lax.broadcasted_iota(jnp.int32, (128, 128), 0) < 64
    b_hi, b_lo = split(jnp.concatenate(
        [jnp.where(low_half, blocks, 0.0), jnp.where(low_half, 0.0, blocks)], axis=1
    ))
    packed = mm(HOT[...], b_hi, nt) + mm(HOT[...], b_lo, nt)
    msg[...] = packed.reshape(m_size, e_size, width, 128)

    pl.semaphore_wait(rounds.at[2], 1)
    if chips > 1:
        pl.when(is_last)(wait_up)
        pl.when(is_first)(wait_down)

    def peer(oe, om):
        return lax.rem(ev + oe, e_size), lax.rem(me + om, m_size)

    if direct:
        def to_owner(e, om):
            m = lax.rem(me + om, m_size)
            slot = lax.rem(e - ev + e_size, e_size) * m_size + om - 1
            remote(msg.at[m, e], got.at[slot], a_s.at[0], a_r.at[0], (e, m))

        for e in range(e_size):

            @pl.when(ev != e)
            def _():
                for om in range(m_size):
                    to_owner(jnp.int32(e), om)

        for om in range(1, m_size):
            to_owner(ev, om)
    else:
        a_copies = [
            remote(msg.at[lax.rem(me + o, m_size)], got.at[pl.ds(e_size * (o - 1), e_size)],
                   a_s.at[o - 1], a_r.at[o - 1], (ev, lax.rem(me + o, m_size)))
            for o in range(1, m_size)
        ]

    pl.when(jnp.logical_not(ahead))(send_second)

    st_f = strain(0)
    for c in range(3):
        N[c] = N[c] - time_square * material * st_f[c]
    own_pass(0)

    for copy in coef_copies:
        copy.wait_recv()
    has_next, has_last = ev < e_size - 1, ev > 0

    def chain_copy(n, step):
        return pltpu.make_async_remote_copy(
            src_ref=coef_in.at[n], dst_ref=coef_in.at[2 + n], send_sem=coef_s.at[2 + n],
            recv_sem=coef_r.at[2 + n], device_id=(lax.rem(ev + step + e_size, e_size), me),
            device_id_type=MESH,
        )

    to_next, to_last = chain_copy(0, 1), chain_copy(1, -1)
    pl.when(has_next)(lambda: to_next.start())
    pl.when(has_last)(lambda: to_last.start())
    if not direct:
        for copy in a_copies:
            copy.wait_recv()
        mine_sum = msg[me]
        for o in range(m_size - 1):
            mine_sum = mine_sum + got[e_size * o : e_size * (o + 1)]
        part[...] = mine_sum
        b_copies = [
            remote(part.at[lax.rem(ev + o, e_size)], got2.at[o - 1], b_s.at[o - 1], b_r.at[o - 1],
                   (lax.rem(ev + o, e_size), me))
            for o in range(1, e_size)
        ]

    def final(c, t, value):
        fwd_out[c, 8 * t : 8 * t + 8, :] = LIVE[...] * value

    arrive(2, 0)
    unpack(2, 0)
    arrive(2, 1)
    unpack(2, 1)
    rim_pass(0, final)

    pl.when(has_last)(lambda: to_next.wait_recv())
    pl.when(has_next)(lambda: to_last.wait_recv())
    own_coef = pltpu.roll(coef[...], 2, 1)
    left = jnp.where(lin > 0, jnp.where(me > 0, coef_in[0], coef_in[2]), 0.0)
    right = jnp.where(
        lin < total - 1, jnp.where(me < m_size - 1, coef_in[1], coef_in[3]), 0.0
    )
    left = jnp.where(lane < 2, pltpu.roll(left, 126, 1), 0.0)
    right = pltpu.roll(right, 6, 1)
    mine[...] = jnp.zeros((128, 128), f32)
    mine[0:8, :] = own_coef + left + right
    coefs = mine[...].T[0:8]

    def smooth(x):
        chain = pltpu.roll(x, 1, 0) + pltpu.roll(x, 7, 0) - 2.0 * x
        new = x + coefs[:, 0:1] * chain
        for d, shift in ((1, 4), (2, 2), (3, 0)):
            digit = lax.shift_right_logical(lane, shift) & 3
            up = jnp.where(digit == 0, 0.0, pltpu.roll(x, 1 << shift, 1))
            down = jnp.where(digit == 3, 0.0, pltpu.roll(x, 128 - (1 << shift), 1))
            new = new + coefs[:, d : d + 1] * (up + down - 2.0 * x)
        return jnp.where(lane < 64, new, 0.0)

    if direct:
        gathered = pltpu.make_async_remote_copy(
            src_ref=got, dst_ref=got, send_sem=a_s.at[0], recv_sem=a_r.at[0],
            device_id=peer(1, 0), device_id_type=MESH,
        )
        gathered.wait_recv()
        parts = [msg[me, ev]] + [got[n] for n in range(total - 1)]
    else:
        for copy in b_copies:
            copy.wait_recv()
        parts = [part[ev]] + [got2[o] for o in range(e_size - 1)]
    while len(parts) > 1:
        parts = [sum(parts[n : n + 2][1:], parts[n]) for n in range(0, len(parts), 2)]
    summed = parts[0]
    x = jnp.concatenate([summed, pltpu.roll(summed, 64, 1)], axis=0)
    x = smooth(smooth(jnp.where(lane < 64, x, 0.0)))
    tiles_out[...] = x[2 : 2 + width, 0:64]

    for f in range(3):
        for k in range(2):
            for c in range(3):
                rim_copy(f, k, c).wait_send()
    if direct:
        gathered.wait_send()
    else:
        for copy in a_copies + b_copies:
            copy.wait_send()
    for copy in coef_copies:
        copy.wait_send()
    pl.when(has_next)(lambda: to_next.wait_send())
    pl.when(has_last)(lambda: to_last.wait_send())


def write_out(final_vmem, tiles_vmem, final_hbm, tiles_hbm, sems):
    copies = [
        pltpu.make_async_copy(
            final_vmem.at[c, pl.ds(0, NODES)], final_hbm.at[pl.ds(NODES * c, NODES), 0], sems.at[c]
        )
        for c in range(3)
    ]
    copies.append(pltpu.make_async_copy(tiles_vmem, tiles_hbm, sems.at[3]))
    for copy in copies:
        copy.start()
    for copy in copies:
        copy.wait()


def solution(mesh):
    m_size, e_size = mesh.shape["mesh"], mesh.shape["event"]
    in_specs = (
        P("event", None, None, "mesh"),
        P("event", None, None, "mesh"),
        P(),
        P(),
        P("event", "mesh"),
        P("event", None, "mesh"),
        P("event", "mesh"),
        P("event", "mesh"),
        P(None, ("event", "mesh")),
    )
    out_specs = (P("event", None, None, "mesh"), P(None, ("event", "mesh")))

    def per_device(*args):
        fwd, smoothing = args[0], args[-1]
        width = smoothing.shape[1]
        dma = pltpu.SemaphoreType.DMA
        vmem = pl.BlockSpec(memory_space=pltpu.VMEM)
        hbm = pl.BlockSpec(memory_space=pltpu.HBM)
        line = (3 * NODES, 1, fwd.shape[-1])
        args = (args[0].reshape(line), args[1].reshape(line), args[2], args[3].T, args[4],
                args[5].reshape(6, 1, fwd.shape[-1]), *args[6:])
        if is_direct(m_size, e_size):
            a_count, b_count = 1, 1
            part, got, got2 = (1, width, 128), (m_size * e_size - 1, width, 128), (1, width, 128)
        else:
            a_count, b_count = m_size - 1, e_size - 1
            part, got, got2 = (e_size, width, 128), ((m_size - 1) * e_size, width, 128), (e_size - 1, width, 128)
        final, tiles = pl.pallas_call(
            functools.partial(kernel, m_size, e_size),
            out_shape=(
                pltpu.VMEM((3, ROWS, 128), f32),
                pltpu.VMEM((width, 64), f32),
            ),
            in_specs=[hbm] * len(args),
            out_specs=(vmem, vmem),
            scratch_shapes=[pltpu.VMEM(x.shape, x.dtype) for x in args[2:]]
            + [
                pltpu.VMEM((6, 144, 128), f32),
                pltpu.VMEM((6, ROWS, 128), f32),
                pltpu.VMEM((ROWS, 128), f32),
                pltpu.VMEM((3, ROWS, 128), f32),
                pltpu.VMEM((ROWS, ROWS), f32),
                pltpu.VMEM((128, 3 * ROWS), bf16),
                pltpu.VMEM((m_size * e_size * width, 256), bf16),
                pltpu.VMEM((7, ROWS, 128), f32),
                pltpu.VMEM((2, len(FACE_TILES), 8, 128), f32),
                pltpu.VMEM((12, 8, 128), jnp.int32),
                pltpu.VMEM((6, 8, 128), jnp.int32),
                pltpu.VMEM((8, 128), f32),
                pltpu.VMEM((3, 3, 32, 128), f32),
                pltpu.VMEM((3, 2, 3, 32, 128), f32),
                pltpu.VMEM((3, 120, 128), f32),
                pltpu.VMEM((8, 128), f32),
                pltpu.VMEM((4, 8, 128), f32),
                pltpu.VMEM((m_size, e_size, width, 128), f32),
                pltpu.VMEM((128, 128), f32),
                pltpu.VMEM(part, f32),
                pltpu.VMEM(got, f32),
                pltpu.VMEM(got2, f32),
                dma((6,)), dma((7,)), dma((3, 2, 3)), dma((3, 2, 3)), dma((4,)), dma((4,)),
                dma((a_count,)), dma((a_count,)), dma((b_count,)), dma((b_count,)),
                pltpu.SemaphoreType.REGULAR((3,)),
            ],
            compiler_params=pltpu.CompilerParams(collective_id=0, has_side_effects=True),
        )(*args)
        final, tiles = pl.pallas_call(
            write_out,
            out_shape=(pltpu.HBM(line, f32), pltpu.HBM((width, 64), f32)),
            in_specs=[vmem, vmem],
            out_specs=(hbm, hbm),
            scratch_shapes=[dma((4,))],
        )(
            pltpu.with_memory_space_constraint(final, pltpu.VMEM),
            pltpu.with_memory_space_constraint(tiles, pltpu.VMEM),
        )
        return final.reshape(fwd.shape), tiles.T

    return jax.shard_map(
        per_device, mesh=mesh, in_specs=in_specs, out_specs=out_specs, check_vma=False
    )
```

```python
import functools
import math

import jax
import jax.numpy as jnp
from jax import lax
from jax.experimental import pallas as pl
from jax.experimental.pallas import tpu as pltpu
from jax.sharding import PartitionSpec as P

STEPS = 2
time_square = 0.4
penalty = 0.5

PAD = 8
ROWS = 128
NODES = 125
SHIFT = (100, -100, 20, -20, 4, -4)
RELAYED = (0, 1)
MESH = pl.DeviceIdType.MESH
f32 = jnp.float32
bf16 = jnp.bfloat16


def on_face(face, node):
    i, j, k = node // 25, (node // 5) % 5, node % 5
    return (i == 0, i == 4, j == 0, j == 4, k == 0, k == 4)[face]


RIM_NODES = [n for n in range(NODES) if any(on_face(f, n) for f in range(6))]
RIM_PLACE = {n: at for at, n in enumerate(RIM_NODES)}
RIM_ROWS = -(-len(RIM_NODES) // 4)
FACE_TILES = [
    (f, t)
    for f in range(6)
    for t in range(ROWS // 8)
    if any(on_face(f, n) for n in range(8 * t, min(8 * t + 8, NODES)))
]


def split(x):
    high = x.astype(bf16)
    return high, (x - high.astype(f32)).astype(bf16)


def mm(a, b, dims=((1,), (0,))):
    return lax.dot_general(a, b, (dims, ((), ())), preferred_element_type=f32)


def pick(x, index):
    dims = lax.GatherDimensionNumbers(
        offset_dims=(), collapsed_slice_dims=(1,), start_index_map=(1,),
        operand_batching_dims=(0,), start_indices_batching_dims=(0,),
    )
    return lax.gather(x, index[:, :, None], dims, (1, 1), mode=lax.GatherScatterMode.PROMISE_IN_BOUNDS)


def gather_rows(load, places):
    pieces = {}
    for r, place in enumerate(places):
        if place is not None:
            pieces.setdefault(place - r, []).append(r)
    sublane = lax.broadcasted_iota(jnp.int32, (8, 128), 0)
    value = None
    for shift, members in pieces.items():
        piece = load(shift)
        if value is None:
            value = piece
        else:
            value = jnp.where((sublane >= members[0]) & (sublane <= members[-1]), piece, value)
    return load(0) if value is None else value


def is_direct(m_size, e_size):
    return m_size * e_size <= 64


def kernel(
    m_size, e_size,
    fwd_in, adj_in, stiff_hbm, proj_hbm, mat_hbm, nb_hbm, dest_hbm, count_hbm, smooth_hbm,
    fwd_out, tiles_out,
    stiff_in, proj_in, mat_in, nb_in, dest_in, count_in, smooth_in,
    F, N, K, A, S, T, HOT, W, M, IDX, RIM, LIVE, send, rim, U, coef, coef_in, msg, mine, part, got, got2,
    in_s, small_s, rim_s, rim_r, coef_s, coef_r, a_s, a_r, b_s, b_r, rounds,
):
    me = lax.axis_index("mesh")
    ev = lax.axis_index("event")
    total = m_size * e_size
    direct = is_direct(m_size, e_size)
    lin = ev * m_size + me
    after = lax.rem(me + 1, m_size)
    before = lax.rem(me + m_size - 1, m_size)

    barrier = pltpu.get_barrier_semaphore()
    core = lax.rem(ev, 2)
    chip = lax.div(ev, 2)
    chips = e_size // 2
    near = [((2 * chip + 1 - core, me), None)]
    for step in (1, -1):
        inside = (chip + step >= 0) & (chip + step < chips)
        near += [((2 * (chip + step) + c, me), inside) for c in range(2)]
    near_count = 1 + 2 * ((chip > 0).astype(jnp.int32) + (chip < chips - 1).astype(jnp.int32))

    def greet(sem, devices):
        for device, inside in devices:
            if inside is None:
                pl.semaphore_signal(sem, inc=1, device_id=device, device_id_type=MESH)
            else:

                @pl.when(inside)
                def _():
                    pl.semaphore_signal(sem, inc=1, device_id=device, device_id_type=MESH)

    for o in range(1, m_size):
        pl.semaphore_signal(
            barrier, inc=1, device_id=(ev, lax.rem(me + o, m_size)), device_id_type=MESH
        )
    greet(barrier, near)

    loads = {}
    for fc in (3, 4, 5, 0, 1, 2):
        source = fwd_in if fc < 3 else adj_in
        load = pltpu.make_async_copy(
            source.at[pl.ds(NODES * (fc % 3), NODES), 0], F.at[fc, pl.ds(PAD, NODES)], in_s.at[fc]
        )
        load.start()
        loads[fc] = load

    small = []
    for n, (src, dst) in enumerate((
        (smooth_hbm, smooth_in), (stiff_hbm, stiff_in), (nb_hbm, nb_in), (count_hbm, count_in),
        (mat_hbm, mat_in), (proj_hbm, proj_in), (dest_hbm, dest_in),
    )):
        load = pltpu.make_async_copy(src, dst, small_s.at[n])
        load.start()
        small.append(load)

    lane = lax.broadcasted_iota(jnp.int32, (1, 128), 1)
    zero8 = jnp.zeros((PAD, 128), f32)
    for fc in range(6):
        F[fc, 0:PAD, :] = zero8
        F[fc, PAD + NODES : 144, :] = jnp.zeros((144 - PAD - NODES, 128), f32)

    def pack(f, c, fc):
        for v in range(-(-RIM_ROWS // 8)):
            parts = []
            for g in range(4):
                inside = range(RIM_ROWS * g + 8 * v, min(RIM_ROWS * (g + 1), RIM_ROWS * g + 8 * v + 8))
                places = [RIM_NODES[n] if n < len(RIM_NODES) else None for n in inside]
                part = gather_rows(lambda low: F[fc, low + PAD : low + 2 * PAD, :], places)
                parts.append(pltpu.roll(part, 32 * g, 1) if g else part)
            send[f, c, 8 * v : 8 * v + 8, :] = jnp.where(
                lane < 64, jnp.where(lane < 32, parts[0], parts[1]),
                jnp.where(lane < 96, parts[2], parts[3]),
            )

    def load_field(f, then=None):
        for c in range(3):
            loads[3 * f + c].wait()
            pack(f, c, 3 * f + c)
            if then is not None:
                then(c)


    def remote(src, dst, s, r, device):
        copy = pltpu.make_async_remote_copy(
            src_ref=src, dst_ref=dst, send_sem=s, recv_sem=r, device_id=device, device_id_type=MESH
        )
        copy.start()
        return copy

    paired = m_size == 4
    first = 1 - lax.rem(me, 2) if paired else 0
    second = 1 - first
    sides = (first, second)
    used = pl.ds(0, RIM_ROWS)

    def rim_copy(f, k, c):
        slot = sides[1 - k] if paired else sides[k]
        return pltpu.make_async_remote_copy(
            src_ref=send.at[f, c, used], dst_ref=rim.at[f, slot, c, used],
            send_sem=rim_s.at[f, k, c], recv_sem=rim_r.at[f, k, c],
            device_id=(ev, jnp.where(slot == 0, after, before)), device_id_type=MESH,
        )

    def relay_copy(f, c):
        return pltpu.make_async_remote_copy(
            src_ref=rim.at[f, first, c, used], dst_ref=rim.at[f, second, c, used],
            send_sem=rim_s.at[f, 1, c], recv_sem=rim_r.at[f, 1, c],
            device_id=(ev, lax.rem(me + 2, m_size)), device_id_type=MESH,
        )

    def send_near(f):
        for c in range(3):
            rim_copy(f, 0, c).start()

    def send_far(f):
        for c in range(3):
            rim_copy(f, 1, c).start()

    def at_core(which, job):
        @pl.when(core == which)
        def _():
            job()

    def far_of(c):
        if c == 0:
            pl.semaphore_wait(barrier, near_count + (m_size - 1))

        def leave():
            rim_copy(1, 1, c).start()

        if paired and 1 in RELAYED:
            at_core(0, leave)
            at_core(1, lambda: rim_copy(1, 0, c).start())
        else:
            leave()

    load_field(1, far_of)
    if paired and 1 in RELAYED:
        at_core(0, lambda: send_near(1))
    else:
        send_near(1)
    def forward_of(c):
        at_core(0, lambda: rim_copy(0, 1, c).start())

    load_field(0, forward_of)
    at_core(0, lambda: send_near(0))
    coef[...] = jnp.zeros((8, 128), f32)

    @pl.when(ev == 0)
    def _():
        coef_in[2] = jnp.zeros((8, 128), f32)

    @pl.when(ev == e_size - 1)
    def _():
        coef_in[3] = jnp.zeros((8, 128), f32)

    small[0].wait()
    coef[0:4, 0:4] = smooth_in[...]
    coef_copies = [
        remote(coef, coef_in.at[0], coef_s.at[0], coef_r.at[0], (ev, after)),
        remote(coef, coef_in.at[1], coef_s.at[1], coef_r.at[1], (ev, before)),
    ]
    beside, above, below = near[:1], near[1:3], near[3:]
    is_first, is_last = chip == 0, chip == chips - 1

    def wait_up():
        pl.semaphore_wait(rounds.at[0], 2)
        greet(rounds.at[0], above)

    def wait_down():
        pl.semaphore_wait(rounds.at[1], 2)
        greet(rounds.at[1], below)

    greet(rounds.at[2], beside)
    pl.when(is_first)(lambda: greet(rounds.at[0], above))
    pl.when(is_last)(lambda: greet(rounds.at[1], below))
    between = jnp.logical_not(is_first | is_last)
    turns = between & (chip == chips - 2)

    for load in small[1:]:
        load.wait()
    live = jnp.where(lane < count_in[0:1, 0:1], 1.0, 0.0).astype(f32)
    LIVE[...] = jnp.broadcast_to(live, (8, 128))
    for fc in range(6):
        F[fc, PAD : PAD + NODES, :] = F[fc, PAD : PAD + NODES, :] * live

    node = lax.broadcasted_iota(jnp.int32, (ROWS, 128), 0).astype(f32)
    i = jnp.floor((node + 0.5) / 25.0)
    rest = node - 25.0 * i
    j = jnp.floor((rest + 0.5) / 5.0)
    k = rest - 5.0 * j
    count = jnp.zeros((ROWS, 128), f32)
    for f, test in enumerate((i == 0.0, i == 4.0, j == 0.0, j == 4.0, k == 0.0, k == 4.0)):
        mask = jnp.where(test & (node < NODES - 0.5), 1.0, 0.0).astype(f32)
        W[f] = mask
        count = count + mask
    W[6] = count
    nb = nb_in[:, 0, :]
    target = lax.shift_right_logical(nb, 7)
    slot = nb & 127
    relative = lax.rem(target - me + m_size, m_size)
    for f in range(6):
        IDX[f] = jnp.broadcast_to(slot[f : f + 1], (8, 128))
        IDX[6 + f] = jnp.broadcast_to(relative[f : f + 1], (8, 128))
        far = jnp.where(relative[f : f + 1] == jnp.where(second == 1, 1, m_size - 1), 32, 0)
        RIM[f] = jnp.broadcast_to((slot[f : f + 1] & 31) + far, (8, 128))
    for c in range(3):
        U[c, 0:PAD, :] = zero8
        U[c, PAD + 4 * RIM_ROWS :, :] = jnp.zeros((U.shape[1] - PAD - 4 * RIM_ROWS, 128), f32)
    S[...] = jnp.zeros((ROWS, ROWS), f32)
    S[0:NODES, 0:NODES] = stiff_in[...]
    s_hi, s_lo = split(S[...])
    material = mat_in[...]

    def strain(base):
        wide = jnp.concatenate([F[base + c, PAD : PAD + ROWS, :] for c in range(3)], axis=1)
        hi, lo = split(wide)
        both = mm(s_hi, hi) + (mm(s_hi, lo) + mm(s_lo, hi))
        return [both[:, 128 * c : 128 * (c + 1)] for c in range(3)]

    def build_masks(which, here):
        for n, (f, t) in enumerate(FACE_TILES):
            M[which, n] = jnp.where(here(IDX[6 + f]), W[f, 8 * t : 8 * t + 8, :], 0.0)

    def face_sums(read, which):
        sums = [None] * (ROWS // 8)
        for n, (f, t) in enumerate(FACE_TILES):
            g = read(f, t) * M[which, n]
            sums[t] = g if sums[t] is None else sums[t] + g
        return sums

    def own_pass(base):
        for c in range(3):
            def read(f, t):
                at = 8 * t + SHIFT[f] + PAD
                return pick(F[base + c, at : at + 8, :], IDX[f])

            sums = face_sums(read, 0)
            for t in range(ROWS // 8):
                at = pl.ds(8 * t, 8)
                v = F[base + c, 8 * t + PAD : 8 * t + 2 * PAD, :]
                acc = sums[t] - W[6, at, :] * v
                N[base + c, at, :] = N[base + c, at, :] + (time_square * penalty) * acc

    def arrive(f, k):
        for c in range(3):
            rim_copy(f, k, c).wait_recv()
            if k == 0 and paired and f in RELAYED:

                @pl.when(core == 1)
                def _():
                    relay_copy(f, c).start()

    def unpack(f, k):
        side = sides[k]
        for c in range(3):
            for g in range(4):
                at = pl.ds(PAD + RIM_ROWS * g, RIM_ROWS)
                turn = (32 * k - 32 * g) % 128
                part = rim[f, side, c, 0:RIM_ROWS, :]
                part = pltpu.roll(part, turn, 1) if turn else part
                U[c, at, :] = part if k == 0 else jnp.where(lane < 32, U[c, at, :], part)

    def rim_pass(base, store):
        for c in range(3):

            def read(f, t):
                places = [
                    RIM_PLACE[8 * t + r + SHIFT[f]] if 8 * t + r < NODES and on_face(f, 8 * t + r) else None
                    for r in range(8)
                ]
                rows = gather_rows(lambda low: U[c, low + PAD : low + 2 * PAD, :], places)
                return pick(rows, RIM[f])

            sums = face_sums(read, 1)
            for t in range(ROWS // 8):
                old = N[base + c, 8 * t : 8 * t + 8, :]
                store(c, t, old + (time_square * penalty) * sums[t])

    if paired:
        at_core(1, lambda: send_near(0))
    build_masks(0, lambda relative: relative == 0)
    st_f = strain(0)
    st_a = strain(3)
    energy = jnp.zeros((ROWS, 128), f32)
    for c in range(3):
        vf = F[c, PAD : PAD + ROWS, :]
        energy = energy + vf * st_a[c]
        N[c] = vf - time_square * material * st_f[c]
        N[3 + c] = F[3 + c, PAD : PAD + ROWS, :] - time_square * material * st_a[c]
    K[...] = energy
    if not paired:
        at_core(1, lambda: (send_near(0), send_far(0)))
    else:
        pass
    own_pass(3)
    own_pass(0)
    pl.when(between)(wait_up)
    pl.when(turns)(wait_down)
    build_masks(1, lambda relative: (relative == 1) | (relative == m_size - 1))

    def keep_adjoint(c, t, value):
        F[3 + c, 8 * t + PAD : 8 * t + 2 * PAD, :] = LIVE[...] * value

    def keep_forward(c, t, value):
        value = LIVE[...] * value
        at = pl.ds(8 * t + PAD, 8)
        line = pl.ds(8 * t, 8)
        N[c, line, :] = 2.0 * value - F[c, at, :]
        F[c, at, :] = value
        K[line, :] = K[line, :] + value * A[c, line, :]

    elements = F.shape[-1]
    width = smooth_in.shape[1]
    scale = math.sqrt(width / elements) / STEPS
    pad = jnp.zeros((proj_in.shape[0], ROWS - NODES), f32)
    half = jnp.concatenate([proj_in[...], pad], axis=1)
    t_hi, t_lo = split(jnp.concatenate([half, half], axis=0))
    T[...] = jnp.concatenate([t_hi, t_hi, t_lo], axis=1)
    row = lax.broadcasted_iota(jnp.int32, (total * width, 128), 0)
    owner = lax.div(row, width)
    tile = width * (lax.rem(owner, e_size) * m_size + lax.div(owner, e_size)) + lax.rem(row, width)
    dest = dest_in[...]
    nt = ((1,), (1,))
    for at, offset in ((0, -2), (128, 2)):
        HOT[:, at : at + 128] = jnp.where(tile + offset == dest, 1.0, 0.0).astype(f32).astype(bf16)

    arrive(1, 0)
    unpack(1, 0)
    if paired and 0 in RELAYED:
        at_core(1, lambda: arrive(0, 0))
    arrive(1, 1)
    unpack(1, 1)
    rim_pass(3, keep_adjoint)
    pl.when(between & jnp.logical_not(turns))(wait_down)
    for c, value in enumerate(strain(3)):
        A[c] = value
    if paired and 0 in RELAYED:
        at_core(0, lambda: arrive(0, 0))
    else:
        arrive(0, 0)
    unpack(0, 0)
    arrive(0, 1)
    unpack(0, 1)
    rim_pass(0, keep_forward)

    def send_second():
        for c in range(3):
            pack(2, c, c)
        if paired and 2 in RELAYED:
            at_core(0, lambda: send_far(2))
        else:
            send_far(2)
        send_near(2)

    ahead = chip == 0
    pl.when(ahead)(send_second)
    k_hi, k_lo = split(K[...])
    blocks = mm(T[:, 0:256], jnp.concatenate([k_hi, k_lo], axis=0)) + mm(T[:, 256:384], k_hi)
    blocks = blocks * scale
    low_half = lax.broadcasted_iota(jnp.int32, (128, 128), 0) < 64
    b_hi, b_lo = split(jnp.concatenate(
        [jnp.where(low_half, blocks, 0.0), jnp.where(low_half, 0.0, blocks)], axis=1
    ))
    packed = mm(HOT[...], b_hi, nt) + mm(HOT[...], b_lo, nt)
    msg[...] = packed.reshape(m_size, e_size, width, 128)

    pl.semaphore_wait(rounds.at[2], 1)
    if chips > 1:
        pl.when(is_last)(wait_up)
        pl.when(is_first)(wait_down)

    def peer(oe, om):
        return lax.rem(ev + oe, e_size), lax.rem(me + om, m_size)

    if direct:
        def to_owner(e, om):
            m = lax.rem(me + om, m_size)
            slot = lax.rem(e - ev + e_size, e_size) * m_size + om - 1
            remote(msg.at[m, e], got.at[slot], a_s.at[0], a_r.at[0], (e, m))

        for e in range(e_size):

            @pl.when(ev != e)
            def _():
                for om in range(m_size):
                    to_owner(jnp.int32(e), om)

        for om in range(1, m_size):
            to_owner(ev, om)
    else:
        a_copies = [
            remote(msg.at[lax.rem(me + o, m_size)], got.at[pl.ds(e_size * (o - 1), e_size)],
                   a_s.at[o - 1], a_r.at[o - 1], (ev, lax.rem(me + o, m_size)))
            for o in range(1, m_size)
        ]

    pl.when(jnp.logical_not(ahead))(send_second)

    st_f = strain(0)
    for c in range(3):
        N[c] = N[c] - time_square * material * st_f[c]
    own_pass(0)

    for copy in coef_copies:
        copy.wait_recv()
    has_next, has_last = ev < e_size - 1, ev > 0

    def chain_copy(n, step):
        return pltpu.make_async_remote_copy(
            src_ref=coef_in.at[n], dst_ref=coef_in.at[2 + n], send_sem=coef_s.at[2 + n],
            recv_sem=coef_r.at[2 + n], device_id=(lax.rem(ev + step + e_size, e_size), me),
            device_id_type=MESH,
        )

    to_next, to_last = chain_copy(0, 1), chain_copy(1, -1)
    pl.when(has_next)(lambda: to_next.start())
    pl.when(has_last)(lambda: to_last.start())
    if not direct:
        for copy in a_copies:
            copy.wait_recv()
        mine_sum = msg[me]
        for o in range(m_size - 1):
            mine_sum = mine_sum + got[e_size * o : e_size * (o + 1)]
        part[...] = mine_sum
        b_copies = [
            remote(part.at[lax.rem(ev + o, e_size)], got2.at[o - 1], b_s.at[o - 1], b_r.at[o - 1],
                   (lax.rem(ev + o, e_size), me))
            for o in range(1, e_size)
        ]

    def final(c, t, value):
        fwd_out[c, 8 * t : 8 * t + 8, :] = LIVE[...] * value

    arrive(2, 0)
    unpack(2, 0)
    arrive(2, 1)
    unpack(2, 1)
    rim_pass(0, final)

    pl.when(has_last)(lambda: to_next.wait_recv())
    pl.when(has_next)(lambda: to_last.wait_recv())
    own_coef = pltpu.roll(coef[...], 2, 1)
    left = jnp.where(lin > 0, jnp.where(me > 0, coef_in[0], coef_in[2]), 0.0)
    right = jnp.where(
        lin < total - 1, jnp.where(me < m_size - 1, coef_in[1], coef_in[3]), 0.0
    )
    left = jnp.where(lane < 2, pltpu.roll(left, 126, 1), 0.0)
    right = pltpu.roll(right, 6, 1)
    mine[...] = jnp.zeros((128, 128), f32)
    mine[0:8, :] = own_coef + left + right
    coefs = mine[...].T[0:8]

    def smooth(x):
        chain = pltpu.roll(x, 1, 0) + pltpu.roll(x, 7, 0) - 2.0 * x
        new = x + coefs[:, 0:1] * chain
        for d, shift in ((1, 4), (2, 2), (3, 0)):
            digit = lax.shift_right_logical(lane, shift) & 3
            up = jnp.where(digit == 0, 0.0, pltpu.roll(x, 1 << shift, 1))
            down = jnp.where(digit == 3, 0.0, pltpu.roll(x, 128 - (1 << shift), 1))
            new = new + coefs[:, d : d + 1] * (up + down - 2.0 * x)
        return jnp.where(lane < 64, new, 0.0)

    if direct:
        gathered = pltpu.make_async_remote_copy(
            src_ref=got, dst_ref=got, send_sem=a_s.at[0], recv_sem=a_r.at[0],
            device_id=peer(1, 0), device_id_type=MESH,
        )
        gathered.wait_recv()
        parts = [msg[me, ev]] + [got[n] for n in range(total - 1)]
    else:
        for copy in b_copies:
            copy.wait_recv()
        parts = [part[ev]] + [got2[o] for o in range(e_size - 1)]
    while len(parts) > 1:
        parts = [sum(parts[n : n + 2][1:], parts[n]) for n in range(0, len(parts), 2)]
    summed = parts[0]
    x = jnp.concatenate([summed, pltpu.roll(summed, 64, 1)], axis=0)
    x = smooth(smooth(jnp.where(lane < 64, x, 0.0)))
    tiles_out[...] = x[2 : 2 + width, 0:64]

    for f in range(3):
        for k in range(2):
            for c in range(3):
                rim_copy(f, k, c).wait_send()
    if direct:
        gathered.wait_send()
    else:
        for copy in a_copies + b_copies:
            copy.wait_send()
    for copy in coef_copies:
        copy.wait_send()
    pl.when(has_next)(lambda: to_next.wait_send())
    pl.when(has_last)(lambda: to_last.wait_send())


def write_out(final_vmem, tiles_vmem, final_hbm, tiles_hbm, sems):
    copies = [
        pltpu.make_async_copy(
            final_vmem.at[c, pl.ds(0, NODES)], final_hbm.at[pl.ds(NODES * c, NODES), 0], sems.at[c]
        )
        for c in range(3)
    ]
    copies.append(pltpu.make_async_copy(tiles_vmem, tiles_hbm, sems.at[3]))
    for copy in copies:
        copy.start()
    for copy in copies:
        copy.wait()


def solution(mesh):
    m_size, e_size = mesh.shape["mesh"], mesh.shape["event"]
    in_specs = (
        P("event", None, None, "mesh"),
        P("event", None, None, "mesh"),
        P(),
        P(),
        P("event", "mesh"),
        P("event", None, "mesh"),
        P("event", "mesh"),
        P("event", "mesh"),
        P(None, ("event", "mesh")),
    )
    out_specs = (P("event", None, None, "mesh"), P(None, ("event", "mesh")))

    def per_device(*args):
        fwd, smoothing = args[0], args[-1]
        width = smoothing.shape[1]
        dma = pltpu.SemaphoreType.DMA
        vmem = pl.BlockSpec(memory_space=pltpu.VMEM)
        hbm = pl.BlockSpec(memory_space=pltpu.HBM)
        line = (3 * NODES, 1, fwd.shape[-1])
        args = (args[0].reshape(line), args[1].reshape(line), args[2], args[3].T, args[4],
                args[5].reshape(6, 1, fwd.shape[-1]), *args[6:])
        if is_direct(m_size, e_size):
            a_count, b_count = 1, 1
            part, got, got2 = (1, width, 128), (m_size * e_size - 1, width, 128), (1, width, 128)
        else:
            a_count, b_count = m_size - 1, e_size - 1
            part, got, got2 = (e_size, width, 128), ((m_size - 1) * e_size, width, 128), (e_size - 1, width, 128)
        final, tiles = pl.pallas_call(
            functools.partial(kernel, m_size, e_size),
            out_shape=(
                pltpu.VMEM((3, ROWS, 128), f32),
                pltpu.VMEM((width, 64), f32),
            ),
            in_specs=[hbm] * len(args),
            out_specs=(vmem, vmem),
            scratch_shapes=[pltpu.VMEM(x.shape, x.dtype) for x in args[2:]]
            + [
                pltpu.VMEM((6, 144, 128), f32),
                pltpu.VMEM((6, ROWS, 128), f32),
                pltpu.VMEM((ROWS, 128), f32),
                pltpu.VMEM((3, ROWS, 128), f32),
                pltpu.VMEM((ROWS, ROWS), f32),
                pltpu.VMEM((128, 3 * ROWS), bf16),
                pltpu.VMEM((m_size * e_size * width, 256), bf16),
                pltpu.VMEM((7, ROWS, 128), f32),
                pltpu.VMEM((2, len(FACE_TILES), 8, 128), f32),
                pltpu.VMEM((12, 8, 128), jnp.int32),
                pltpu.VMEM((6, 8, 128), jnp.int32),
                pltpu.VMEM((8, 128), f32),
                pltpu.VMEM((3, 3, 32, 128), f32),
                pltpu.VMEM((3, 2, 3, 32, 128), f32),
                pltpu.VMEM((3, 120, 128), f32),
                pltpu.VMEM((8, 128), f32),
                pltpu.VMEM((4, 8, 128), f32),
                pltpu.VMEM((m_size, e_size, width, 128), f32),
                pltpu.VMEM((128, 128), f32),
                pltpu.VMEM(part, f32),
                pltpu.VMEM(got, f32),
                pltpu.VMEM(got2, f32),
                dma((6,)), dma((7,)), dma((3, 2, 3)), dma((3, 2, 3)), dma((4,)), dma((4,)),
                dma((a_count,)), dma((a_count,)), dma((b_count,)), dma((b_count,)),
                pltpu.SemaphoreType.REGULAR((3,)),
            ],
            compiler_params=pltpu.CompilerParams(collective_id=0, has_side_effects=True),
        )(*args)
        final, tiles = pl.pallas_call(
            write_out,
            out_shape=(pltpu.HBM(line, f32), pltpu.HBM((width, 64), f32)),
            in_specs=[vmem, vmem],
            out_specs=(hbm, hbm),
            scratch_shapes=[dma((4,))],
        )(
            pltpu.with_memory_space_constraint(final, pltpu.VMEM),
            pltpu.with_memory_space_constraint(tiles, pltpu.VMEM),
        )
        return final.reshape(fwd.shape), tiles.T

    return jax.shard_map(
        per_device, mesh=mesh, in_specs=in_specs, out_specs=out_specs, check_vma=False
    )
```
